128 devices in a mesh: horiz: 32 (over x_lo, y, z), tracer: 2 (over core), level: 2 (over x_hi).
Axes of the slice: x: 4 (x_hi: 2, x_lo: 2; x = x_hi * 2 + x_lo), y: 4, z: 4, core: 2. Of those that a mesh axis runs over, the one named last changes fastest.
Arguments:
- forward_init: float32 [32, 64, 128, 128], P('tracer', 'level', 'horiz'), may hold values from -6 to 6
- adjoint_init: float32 [32, 64, 128, 128], P('tracer', 'level', 'horiz'), may hold values from -6 to 6
- east_flow: float32 [64, 128, 128], P('level', 'horiz'), may hold values from -0.24 to 0.24
- north_flow: float32 [64, 128, 128], P('level', 'horiz'), may hold values from -0.24 to 0.24
- mixing: float32 [63, 128, 128], P(None, 'horiz'), may hold values from 0.05 to 5
- depth: int32 [128, 128], P('horiz'), may hold values from 32 to 64
- color: int32 [128, 128], P('horiz'), may hold values from 0 to 31
- fold: int32 [128], replicated, may hold values from 0 to 127, each once
Outputs:
- forward_final: float32 [32, 64, 128, 128], P('tracer', 'level', 'horiz')
- adjoint_final: float32 [32, 64, 128, 128], P('tracer', 'level', 'horiz')
- sensitivity: float32 [64, 128, 128], P('level', 'horiz')
The draws below stay inside these ranges and needn't reach their ends.
Inputs may be any that keep to these rules, and one draw needn't show every extreme that they name: `fold`: each column number appears exactly once.
All inputs are finite; a program needn't handle non-finite values.
Results may differ from the reference program's by a relative error of at most 0.0003.
Values sent between devices are 32-bit elements; how exact they have to be, the bound alone decides.
No kernel may reach another device: no remote copies, remote signals or barrier semaphores. Data moves between devices by JAX's collectives and lax.ppermute only.
A program may use at most 256 MiB of HBM per device.

```python
import math
import jax
import jax.numpy as jnp
from jax import lax

NTR = 32
NLEV = 64
NX = 128
STEPS = 4
NY = 128


def touch_ends(values, own_key, low, high):
    shape = values.shape
    spot = [jax.random.randint(jax.random.fold_in(own_key, axis), (), 0, shape[axis]) for axis in range(len(shape))]
    values = values.at[tuple(spot)].set(low)
    longest = shape.index(max(shape))
    spot[longest] = (spot[longest] + 1) % shape[longest]
    return values.at[tuple(spot)].set(high)


def level_of(key, dims, pieces, least, high):
    gain = 1.0
    for dim, shards_of in pieces:
        draws = jax.random.uniform(jax.random.fold_in(jax.random.fold_in(key, 6), dim), (shards_of,), jnp.float32, least / len(pieces), high / len(pieces))
        gain = gain * jnp.repeat(jnp.exp(draws), dims[dim] // shards_of).reshape((-1,) + (1,) * (len(dims) - 1 - dim))
    return gain


def noise(own_key, shape, scale, limit, shards=(), held_as=jnp.bfloat16):
    entries = scale * jax.random.normal(own_key, shape, jnp.float32)
    if shards:
        entries = entries * level_of(own_key, shape, shards, -0.22, 0.18)
    return jnp.clip(entries, -limit, limit).astype(held_as)


def setup_inputs(seed: int = 0) -> dict:
    arg_keys = jax.random.split(jax.random.key(seed), 9)
    return {
        "forward_init": noise(arg_keys[0], (NTR, NLEV, NY, NX), 1.0, 6.0, ((0, 2), (1, 2), (2, 32)), jnp.float32),
        "adjoint_init": noise(arg_keys[1], (NTR, NLEV, NY, NX), 1.0, 6.0, ((0, 2), (1, 2), (2, 32)), jnp.float32),
        "east_flow": jnp.clip(jax.random.uniform(arg_keys[2], (NLEV, NY, NX), jnp.float32, -0.24, 0.24) * level_of(arg_keys[2], (NLEV, NY, NX), ((0, 2), (1, 32)), -0.4, 0.0), -0.24, 0.24),
        "north_flow": jnp.clip(jax.random.uniform(arg_keys[3], (NLEV, NY, NX), jnp.float32, -0.24, 0.24) * level_of(arg_keys[3], (NLEV, NY, NX), ((0, 2), (1, 32)), -0.4, 0.0), -0.24, 0.24),
        "mixing": jnp.clip(jnp.exp(math.log(5.0) - 4.6051702 * jax.random.uniform(arg_keys[4], (NLEV - 1, NY, NX), jnp.float32) ** level_of(arg_keys[4], (NLEV - 1, NY, NX), ((1, 32),), -0.2, 0.2)), 0.05, 5.0),
        "depth": touch_ends(jax.random.randint(arg_keys[5], (NY, NX), NLEV // 2, NLEV + 1), jax.random.fold_in(arg_keys[5], 1), NLEV // 2, NLEV).astype(jnp.int32),
        "color": touch_ends(jax.random.randint(arg_keys[6], (NY, NX), 0, NTR), jax.random.fold_in(arg_keys[6], 1), 0, NTR - 1).astype(jnp.int32),
        "fold": jax.random.permutation(arg_keys[7], NX).astype(jnp.int32),
    }


def tri_solve(inside, diagonal, rhs):
    zero_row = jnp.zeros_like(inside[:1])
    down_all = jnp.concatenate([inside, zero_row], 0)
    up_all = jnp.concatenate([zero_row, inside], 0)

    def forward_sweep(carry, items):
        factor, partial_value = carry
        diag_now, up_now, down_now, rhs_now = items
        denominator = diag_now - up_now * factor
        partial_value = (rhs_now + up_now * partial_value) / denominator
        factor = down_now / denominator
        return (factor, partial_value), (factor, partial_value)

    start_pair = (jnp.zeros_like(rhs[0]), jnp.zeros_like(rhs[0]))
    ignored, (factors, partials) = lax.scan(forward_sweep, start_pair, (diagonal, up_all, down_all, rhs))

    def back_sweep(solved, items):
        factor, partial_value = items
        solved = partial_value + factor * solved
        return solved, solved

    ignored, result = lax.scan(back_sweep, jnp.zeros_like(rhs[0]), (factors, partials), reverse=True)
    return result


def reference(forward_init, adjoint_init, east_flow, north_flow, mixing, depth, color, fold):
    level_ids = jnp.arange(NLEV, dtype=jnp.int32)[:, None, None]
    depth_north = jnp.concatenate([depth[1:], jnp.take(depth[-1], fold)[None]], 0)
    wet_mask = (level_ids < depth[None]).astype(jnp.float32)
    wet_north = (level_ids < depth_north[None]).astype(jnp.float32)
    wet_east = jnp.roll(wet_mask, -1, 2)
    east_open = east_flow * wet_mask * wet_east
    north_open = north_flow * wet_mask * wet_north
    coupling = mixing * wet_mask[:-1] * wet_mask[1:]
    zero_row = jnp.zeros_like(coupling[:1])
    diagonal = 1.0 + jnp.concatenate([zero_row, coupling], 0) + jnp.concatenate([coupling, zero_row], 0)
    interface = wet_mask * jnp.concatenate([wet_mask[1:], zero_row], 0)

    def advect(tracer_now, flow_sign, source):
        east_face = flow_sign * east_open
        west_face = jnp.roll(east_face, 1, 2)
        north_face = flow_sign * north_open
        south_face = jnp.concatenate([jnp.zeros_like(north_face[:, :1]), north_face[:, :-1]], 1)
        north_cell = jnp.concatenate([tracer_now[:, 1:], jnp.take(tracer_now[:, -1], fold, axis=1)[:, None]], 1)
        south_cell = jnp.concatenate([jnp.zeros_like(tracer_now[:, :1]), tracer_now[:, :-1]], 1)
        east_cell = jnp.roll(tracer_now, -1, 2)
        west_cell = jnp.roll(tracer_now, 1, 2)
        centre = tracer_now
        explicit = (centre + jnp.maximum(west_face, 0.0) * west_cell + jnp.minimum(west_face, 0.0) * centre
                    - jnp.maximum(east_face, 0.0) * centre - jnp.minimum(east_face, 0.0) * east_cell
                    + jnp.maximum(south_face, 0.0) * south_cell + jnp.minimum(south_face, 0.0) * centre
                    - jnp.maximum(north_face, 0.0) * centre - jnp.minimum(north_face, 0.0) * north_cell
                    + source) * wet_mask
        return explicit

    def level_diff(values):
        below_vals = jnp.concatenate([values[1:], jnp.zeros_like(values[:1])], 0)
        return (below_vals - values) * interface

    forward_now = forward_init * wet_mask[None]
    adjoint_now = adjoint_init * wet_mask[None]
    sens = jnp.zeros((NLEV, NY, NX), jnp.float32)
    for step_no in range(STEPS):
        def one_pair(total, items):
            fwd_one, adj_one, tracer_id = items
            source = (color == tracer_id).astype(jnp.float32)[None]
            fwd_new = tri_solve(coupling, diagonal, advect(fwd_one, 1.0, source))
            adj_new = tri_solve(coupling, diagonal, advect(adj_one, -1.0, source))
            total = total + level_diff(fwd_new) * level_diff(adj_new)
            return total, (fwd_new, adj_new)

        sens, (forward_now, adjoint_now) = lax.scan(
            one_pair, sens, (forward_now, adjoint_now, jnp.arange(NTR, dtype=jnp.int32)))
    return forward_now, adjoint_now, sens / STEPS
```

```python
import functools
import jax
import jax.numpy as jnp
from jax import lax
from jax.experimental import pallas as pl
from jax.experimental.pallas import tpu as pltpu
from jax.sharding import PartitionSpec as P

STEPS = 4
LANES = 128
C0F, C0A, CWF, CWA, CEF, CEA, CSF, CSA, CNF, CNA, UP, WI, BACK = range(13)
E0F, E0A, ESF, ESA, T0F, T0A, TNF, TNA = range(8)
F32 = jnp.float32
UNROLL = 2


def order(flags_ref, n_lev):
    bottom = flags_ref[0]
    return bottom * (n_lev - 1), 1 - 2 * bottom


def west(v):
    return pltpu.roll(v, 1, 1)


def east(v):
    return pltpu.roll(v, LANES - 1, 1)


def spread(v):
    return jnp.broadcast_to(v, (8, LANES))


def pick(c_ref, which, lev, row):
    return spread(c_ref[which, lev, row : row + 1, :])


def sweep(flags_ref, n_lev, n_pair, rows, put, last):
    k0, dk = order(flags_ref, n_lev)
    halves = n_pair // 8
    zero = jnp.zeros((8, LANES), F32)

    def body(s, carry):
        lev = k0 + dk * s
        out = []
        at = 0
        for i, (coef, src, center, south, north) in enumerate(rows):
            up = coef(UP, lev)
            wi = coef(WI, lev)
            srcs = [src(g) * wi for g in range(halves)]
            for kind in range(2):
                c0, cw, ce, cs, cn = (coef(base + kind, lev) for base in (C0F, CWF, CEF, CSF, CNF))
                for g in range(halves):
                    c = center(lev, kind, g)
                    v = c0 * c + cw * west(c)
                    v = v + (ce * east(c) + cs * south(lev, kind, g))
                    v = v + (cn * north(lev, kind, g) + srcs[g])
                    v = v + up * carry[at]
                    put(lev, i, kind, g, v)
                    out.append(v)
                    at += 1
        return tuple(out)

    final = lax.fori_loop(0, n_lev, body, (zero,) * (len(rows) * 2 * halves), unroll=UNROLL)
    at = 0
    for i in range(len(rows)):
        for kind in range(2):
            for g in range(halves):
                last(i, kind, g, final[at])
                at += 1


def back(flags_ref, n_lev, n_pair, rows, wx_ref, far_ref, c_ref, part, put, acc_in, acc_out):
    bottom = flags_ref[0]
    k0, dk = order(flags_ref, n_lev)
    halves = n_pair // 8
    mid = k0 + dk * (n_lev - 1)
    own, far = [], []
    for i, row in enumerate(rows):
        wa, wb, ff = (spread(wx_ref[j, row : row + 1, :]) for j in range(3))
        for kind in range(2):
            for g in range(halves):
                p_far = far_ref[row, pl.ds((kind * halves + g) * 8, 8), :]
                x = wa * part(mid, i, kind, g) + wb * p_far
                own.append(x)
                far.append(p_far + ff * x)

    def tally(s, now, nxt):
        at = jnp.where(bottom == 0, s + 1, n_lev - 1 - s)
        for i in range(len(rows)):
            b = i * 2 * halves
            total = acc_in(at, i)
            for g in range(halves):
                f, a = b + g, b + halves + g
                total = total + (nxt[f] - now[f]) * (nxt[a] - now[a])
            acc_out(at, i, total)

    def store(lev, xs):
        at = 0
        for i in range(len(rows)):
            for kind in range(2):
                for g in range(halves):
                    put(lev, i, kind, g, xs[at])
                    at += 1

    tally(n_lev - 1, own, far)
    store(mid, own)

    def body(q, nxt):
        s = n_lev - 2 - q
        lev = k0 + dk * s
        now = []
        at = 0
        for i, row in enumerate(rows):
            f = pick(c_ref, BACK, lev, row)
            for kind in range(2):
                for g in range(halves):
                    now.append(part(lev, i, kind, g) + f * nxt[at])
                    at += 1
        tally(s, now, nxt)
        store(lev, now)
        return tuple(now)

    lax.fori_loop(0, n_lev - 1, body, tuple(own), unroll=UNROLL)


def fold_rows(flags_ref, fold_ref, nf_ref, get, mf_ref, n_lev, n_pair):
    @pl.when(flags_ref[1] == 1)
    def _():
        where_to = spread(fold_ref[0:1, :])

        def body(lev, _):
            n3 = spread(nf_ref[lev, 3:4, :])
            for g in range(n_pair // 8):
                f = jnp.take_along_axis(get(lev, 0, g), where_to, axis=1)
                a = jnp.take_along_axis(get(lev, 1, g), where_to, axis=1)
                mf_ref[lev, pl.ds(g * 8, 8), :] = jnp.where(n3 < 0.0, f, a)
            return 0

        lax.fori_loop(0, n_lev, body, 0)


def rows_at(ref, row, lev, kind, g, halves):
    return ref[lev, row, pl.ds((kind * halves + g) * 8, 8), :]


def send_first(n_lev, n_pair, n_rows, flags_ref, f_ref, a_ref, nf_ref, depth_ref, north_ref, south_ref):
    stride = n_lev * n_rows
    first = flags_ref[0] * n_lev
    depth = depth_ref[...]

    def body(lev, _):
        wet = jnp.where(first + lev < depth, 1.0, 0.0)
        w0 = spread(wet[0:1])
        w3 = spread(wet[n_rows - 1 : n_rows])
        n3 = spread(nf_ref[lev, n_rows - 1 : n_rows, :])
        for g in range(n_pair // 8):
            at = g * 8 * stride + lev * n_rows
            low, high = pl.ds(at, 8, stride=stride), pl.ds(at + n_rows - 1, 8, stride=stride)
            to = pl.ds(g * 8, 8)
            north_ref[lev, to, :] = jnp.where(n3 > 0.0, f_ref[high, :], a_ref[high, :]) * w3
            south_ref[lev, to, :] = f_ref[low, :] * w0
            south_ref[n_lev + lev, to, :] = a_ref[low, :] * w0
        return 0

    lax.fori_loop(0, n_lev, body, 0, unroll=UNROLL)
    for lev in range(n_lev):
        page, line = n_lev + lev // n_pair, lev % n_pair
        north_ref[page, line : line + 1, :] = nf_ref[lev, n_rows - 1 : n_rows, :]
    high = depth[n_rows - 1 : n_rows].astype(F32)
    low = depth[0:1].astype(F32)
    north_ref[n_lev + n_lev // n_pair] = jnp.broadcast_to(high, (n_pair, LANES))
    south_ref[2 * n_lev] = jnp.broadcast_to(low, (n_pair, LANES))


def prepare(
    n_lev, n_pair, n_rows, flags_ref, f_ref, a_ref, ef_ref, nf_ref, mix_ref, depth_ref, color_ref, fold_ref,
    xe_ref, xi_ref, pi_ref, c_ref, wx_ref, hot_ref, mf_ref, inv_ref,
):
    halves = n_pair // 8
    stride = n_lev * n_rows
    bottom = flags_ref[0]
    first = bottom * n_lev
    k0, dk = order(flags_ref, n_lev)
    depth = depth_ref[...]

    def lay(lev, _):
        wet = jnp.where(first + lev < depth, 1.0, 0.0)
        for row in range(n_rows):
            w = spread(wet[row : row + 1])
            to_ref, line = (xe_ref, row // 3) if row in (0, 3) else (xi_ref, row - 1)
            for kind, from_ref in enumerate((f_ref, a_ref)):
                for g in range(halves):
                    v = from_ref[pl.ds(g * 8 * stride + lev * n_rows + row, 8, stride=stride), :]
                    to_ref[lev, line, pl.ds((kind * halves + g) * 8, 8), :] = v * w
        return 0

    lax.fori_loop(0, n_lev, lay, 0, unroll=UNROLL)

    def coupling(k):
        inner = jnp.where((k >= 0) & (k < 2 * n_lev - 1), 1.0, 0.0)
        m = mix_ref[jnp.clip(k, 0, 2 * n_lev - 2)]
        return m * jnp.where(k + 1 < depth, inner, 0.0)

    def eliminate(s, carry):
        own_f, far_f = carry
        k = bottom * (2 * n_lev - 1) + dk * s
        prev, nxt = coupling(k - 1 + bottom), coupling(k - bottom)
        inverse = 1.0 / (1.0 + nxt + prev * (1.0 - own_f))
        lev = k0 + dk * s
        inv_ref[lev] = inverse
        c_ref[UP, lev] = prev * inverse
        own_f = nxt * inverse
        c_ref[BACK, lev] = own_f
        k = (1 - bottom) * (2 * n_lev - 1) - dk * s
        prev, nxt = coupling(k - bottom), coupling(k - 1 + bottom)
        far_f = nxt / (1.0 + nxt + prev * (1.0 - far_f))
        return own_f, far_f

    one = jnp.zeros((n_rows, LANES), F32)
    own_f, far_f = lax.fori_loop(0, n_lev, eliminate, (one, one), unroll=UNROLL)
    meet = 1.0 / (1.0 - own_f * far_f)
    wx_ref[0] = meet
    wx_ref[1] = own_f * meet
    wx_ref[2] = far_f

    depth_east = east(depth)
    depth_north = jnp.concatenate([depth[1:], jnp.zeros((1, LANES), jnp.int32)], 0)

    def coefs(lev, _):
        k = first + lev
        wet = jnp.where(k < depth, 1.0, 0.0)
        inverse = inv_ref[lev]
        e = ef_ref[lev] * wet * jnp.where(k < depth_east, 1.0, 0.0)
        n = nf_ref[lev] * wet * jnp.where(k < depth_north, 1.0, 0.0)
        w = west(e)
        s = jnp.concatenate([jnp.zeros((1, LANES), F32), n[:-1]], 0)
        plus = [jnp.maximum(v, 0.0) for v in (w, e, s, n)]
        minus = [jnp.maximum(-v, 0.0) for v in (w, e, s, n)]
        c_ref[C0F, lev] = (1.0 - minus[0] - plus[1] - minus[2] - plus[3]) * inverse
        c_ref[C0A, lev] = (1.0 - plus[0] - minus[1] - plus[2] - minus[3]) * inverse
        c_ref[CWF, lev], c_ref[CWA, lev] = plus[0] * inverse, minus[0] * inverse
        c_ref[CEF, lev], c_ref[CEA, lev] = minus[1] * inverse, plus[1] * inverse
        c_ref[CSF, lev], c_ref[CSA, lev] = plus[2] * inverse, minus[2] * inverse
        c_ref[CNF, lev], c_ref[CNA, lev] = minus[3] * inverse, plus[3] * inverse
        c_ref[WI, lev] = wet * inverse
        return 0

    lax.fori_loop(0, n_lev, coefs, 0, unroll=UNROLL)

    ids = lax.broadcasted_iota(jnp.int32, (n_pair, LANES), 0) + flags_ref[3]
    for row in range(n_rows):
        hot_ref[row] = jnp.where(color_ref[row : row + 1, :] == ids, 1.0, 0.0)

    inner_sweep(n_lev, n_pair, flags_ref, xe_ref, xi_ref, c_ref, hot_ref, pi_ref)
    fold_rows(
        flags_ref, fold_ref, nf_ref, lambda lev, kind, g: rows_at(xe_ref, 1, lev, kind, g, halves), mf_ref, n_lev, n_pair
    )


def inner_sweep(n_lev, n_pair, flags_ref, xe_ref, xi_ref, c_ref, hot_ref, pi_ref):
    halves = n_pair // 8

    def row(number):
        line = number - 1

        def at(ref, which):
            return lambda lev, kind, g: rows_at(ref, which, lev, kind, g, halves)

        return (
            lambda which, lev: pick(c_ref, which, lev, number),
            lambda g: hot_ref[number, pl.ds(g * 8, 8), :],
            at(xi_ref, line),
            at(xe_ref, 0) if line == 0 else at(xi_ref, 0),
            at(xi_ref, 1) if line == 0 else at(xe_ref, 1),
        )

    def put(lev, i, kind, g, v):
        pi_ref[lev, i, pl.ds((kind * halves + g) * 8, 8), :] = v

    sweep(flags_ref, n_lev, n_pair, [row(1), row(2)], put, lambda *_: None)


def edge_sweep(
    is_first, n_lev, n_pair, flags_ref, xe_ref, xi_ref, pi_ref, c_ref, hot_ref, mf_ref, ms_ref, mn_ref, ec_in, *rest
):
    halves = n_pair // 8
    is_top = flags_ref[1] == 1
    if is_first:
        nf_ref, depth_ref, fold_ref = ec_in
        pe_ref, edge_ref, ec_ref, fs_ref = rest
        first = flags_ref[0] * n_lev
        depth = depth_ref[...]
        own0, own3 = depth[0:1], depth[3:4]
        page = n_lev + n_lev // n_pair
        south_depth = ms_ref[page, 0:1, :]
        folded = jnp.take_along_axis(spread(own3.astype(F32)), spread(fold_ref[0:1, :]), axis=1)[0:1]
        north_depth = jnp.where(is_top, folded, mn_ref[2 * n_lev, 0:1, :])
        open_south = jnp.where(flags_ref[2] == 1, 0.0, 1.0)
        for lev in range(n_lev):
            k = first + lev
            kf = k.astype(F32)
            raw = ms_ref[n_lev + lev // n_pair, lev % n_pair : lev % n_pair + 1, :]
            fs_ref[lev] = spread(raw)
            wi0, wi3 = c_ref[WI, lev, 0:1, :], c_ref[WI, lev, 3:4, :]
            s = raw * jnp.where(kf < south_depth, 1.0, 0.0) * open_south * wi0
            n = nf_ref[lev, 3:4, :] * jnp.where(kf < north_depth, 1.0, 0.0) * wi3
            sp, sm, np_, nm = (jnp.maximum(v, 0.0) for v in (s, -s, n, -n))
            ec_ref[E0F, lev] = spread(c_ref[C0F, lev, 0:1, :] - sm)
            ec_ref[E0A, lev] = spread(c_ref[C0A, lev, 0:1, :] - sp)
            ec_ref[ESF, lev] = spread(sp)
            ec_ref[ESA, lev] = spread(sm)
            ec_ref[T0F, lev] = spread(c_ref[C0F, lev, 3:4, :] - np_)
            ec_ref[T0A, lev] = spread(c_ref[C0A, lev, 3:4, :] - nm)
            ec_ref[TNF, lev] = spread(nm)
            ec_ref[TNA, lev] = spread(np_)
    else:
        ec_ref = ec_in
        pe_ref, edge_ref = rest

    low = {C0F: E0F, C0A: E0A, CSF: ESF, CSA: ESA}
    high = {C0F: T0F, C0A: T0A, CNF: TNF, CNA: TNA}

    def coef(number, table):
        def get(which, lev):
            return ec_ref[table[which], lev] if which in table else pick(c_ref, which, lev, number)

        return get

    def north_of_edge(lev, kind, g):
        to = pl.ds(g * 8, 8)
        if is_first:
            n3 = spread(nf_ref[lev, 3:4, :])
            come = jnp.where(n3 < 0.0, mn_ref[lev, to, :], mn_ref[n_lev + lev, to, :])
        else:
            come = mn_ref[lev, to, :]
        return jnp.where(is_top, mf_ref[lev, to, :], come)

    def at(ref, which):
        return lambda lev, kind, g: rows_at(ref, which, lev, kind, g, halves)

    rows = [
        (
            coef(0, low),
            lambda g: hot_ref[0, pl.ds(g * 8, 8), :],
            at(xe_ref, 0),
            lambda lev, kind, g: ms_ref[lev, pl.ds(g * 8, 8), :],
            at(xi_ref, 0),
        ),
        (
            coef(3, high),
            lambda g: hot_ref[3, pl.ds(g * 8, 8), :],
            at(xe_ref, 1),
            at(xi_ref, 1),
            north_of_edge,
        ),
    ]

    def put(lev, i, kind, g, v):
        pe_ref[lev, i, pl.ds((kind * halves + g) * 8, 8), :] = v

    def last(i, kind, g, v):
        edge_ref[3 * i, pl.ds((kind * halves + g) * 8, 8), :] = v

    sweep(flags_ref, n_lev, n_pair, rows, put, last)
    k0, dk = order(flags_ref, n_lev)
    mid = k0 + dk * (n_lev - 1)
    edge_ref[1] = pi_ref[mid, 0]
    edge_ref[2] = pi_ref[mid, 1]


def first_edge(n_lev, n_pair, *refs):
    edge_sweep(True, n_lev, n_pair, *refs[:9], refs[9:12], *refs[12:])


def next_edge(n_lev, n_pair, *refs):
    edge_sweep(False, n_lev, n_pair, *refs)


def tallies(is_first, in_ref, out_ref, n_lev):
    if is_first:
        out_ref[0] = jnp.zeros(out_ref.shape[1:], F32)
        out_ref[n_lev] = jnp.zeros(out_ref.shape[1:], F32)
    else:
        out_ref[0] = in_ref[0]
        out_ref[n_lev] = in_ref[n_lev]
    zero = jnp.zeros((8, LANES), F32)

    def put(at, i, v):
        out_ref[at, i] = v

    return (lambda at, i: zero) if is_first else (lambda at, i: in_ref[at, i]), put


def edge_back(is_first, n_lev, n_pair, flags_ref, pe_ref, far_ref, c_ref, wx_ref, nf_ref, fs_ref, *rest):
    halves = n_pair // 8
    acc_ref, (xe_ref, north_ref, south_ref, out_ref) = (None, rest) if is_first else (rest[0], rest[1:])
    acc_in, acc_out = tallies(is_first, acc_ref, out_ref, n_lev)
    held = {}

    def put(lev, i, kind, g, v):
        xe_ref[lev, i, pl.ds((kind * halves + g) * 8, 8), :] = v
        if kind == 0:
            held[i, g] = v
        elif i == 0:
            south_ref[lev, pl.ds(g * 8, 8), :] = jnp.where(fs_ref[lev] < 0.0, held[i, g], v)
        else:
            n3 = spread(nf_ref[lev, 3:4, :])
            north_ref[lev, pl.ds(g * 8, 8), :] = jnp.where(n3 > 0.0, held[i, g], v)

    back(
        flags_ref, n_lev, n_pair, (0, 3), wx_ref, far_ref, c_ref,
        lambda lev, i, kind, g: rows_at(pe_ref, i, lev, kind, g, halves), put, acc_in, acc_out,
    )


def inner(is_first, n_lev, n_pair, flags_ref, pi_ref, far_ref, c_ref, wx_ref, nf_ref, fold_ref, hot_ref, xe_ref, *rest):
    halves = n_pair // 8
    acc_ref, (xi_ref, pn_ref, mf_ref, out_ref) = (None, rest) if is_first else (rest[0], rest[1:])
    acc_in, acc_out = tallies(is_first, acc_ref, out_ref, n_lev)

    def put(lev, i, kind, g, v):
        xi_ref[lev, i, pl.ds((kind * halves + g) * 8, 8), :] = v

    back(
        flags_ref, n_lev, n_pair, (1, 2), wx_ref, far_ref, c_ref,
        lambda lev, i, kind, g: rows_at(pi_ref, i, lev, kind, g, halves), put, acc_in, acc_out,
    )
    inner_sweep(n_lev, n_pair, flags_ref, xe_ref, xi_ref, c_ref, hot_ref, pn_ref)
    fold_rows(
        flags_ref, fold_ref, nf_ref, lambda lev, kind, g: rows_at(xe_ref, 1, lev, kind, g, halves), mf_ref, n_lev, n_pair
    )


def finish(
    n_lev, n_pair, n_rows, flags_ref, pe_ref, pi_ref, far_ref, c_ref, wx_ref, depth_ref, acce_ref, acci_ref,
    f_ref, a_ref, sens_ref, te_ref, ti_ref,
):
    halves = n_pair // 8
    stride = n_lev * n_rows

    for rows, p_ref, acc_ref, t_ref in (((0, 3), pe_ref, acce_ref, te_ref), ((1, 2), pi_ref, acci_ref, ti_ref)):
        acc_in, acc_out = tallies(False, acc_ref, t_ref, n_lev)

        def put(lev, i, kind, g, v, rows=rows):
            to = f_ref if kind == 0 else a_ref
            to[pl.ds(g * 8 * stride + lev * n_rows + rows[i], 8, stride=stride), :] = v

        back(
            flags_ref, n_lev, n_pair, rows, wx_ref, far_ref, c_ref,
            lambda lev, i, kind, g, p_ref=p_ref: rows_at(p_ref, i, lev, kind, g, halves), put, acc_in, acc_out,
        )
    first = flags_ref[0] * n_lev
    depth = depth_ref[...]

    def reduce(lev, _):
        k = first + lev
        live = jnp.where((k + 1 < depth) & (k + 1 < 2 * n_lev), 1.0 / STEPS, 0.0)
        e0, e3 = (jnp.sum(te_ref[lev + 1, i], axis=0, keepdims=True) for i in range(2))
        i1, i2 = (jnp.sum(ti_ref[lev + 1, i], axis=0, keepdims=True) for i in range(2))
        sens_ref[lev] = jnp.concatenate([e0, i1, i2, e3], 0) * live
        return 0

    lax.fori_loop(0, n_lev, reduce, 0, unroll=UNROLL)


def vmem(*shape):
    return pltpu.VMEM(shape, F32)


def call(kernel, outs, args, flops, scratch=()):
    spec = pl.BlockSpec(memory_space=pltpu.VMEM)
    return pl.pallas_call(
        kernel,
        out_shape=tuple(outs),
        in_specs=[pl.BlockSpec(memory_space=pltpu.SMEM)] + [spec] * (len(args) - 1),
        out_specs=tuple([spec] * len(outs)),
        scratch_shapes=list(scratch),
        compiler_params=pltpu.CompilerParams(vmem_limit_bytes=24 * 2**20),
        cost_estimate=pl.CostEstimate(flops=flops, bytes_accessed=flops // 8, transcendentals=0),
    )(args[0], *[pltpu.with_memory_space_constraint(a, pltpu.VMEM) for a in args[1:]])


def per_device(forward_init, adjoint_init, east_flow, north_flow, mixing, depth, color, fold):
    n_pair, n_lev, n_rows, n_x = forward_init.shape
    n_all = 2 * n_pair
    count = lax.axis_size("horiz")
    place = lax.axis_index("horiz")
    flags = jnp.stack(
        [
            lax.axis_index("level"),
            (place == count - 1).astype(jnp.int32),
            (place == 0).astype(jnp.int32),
            lax.axis_index("tracer") * n_pair,
        ]
    ).astype(jnp.int32)
    northward = [(i, (i + 1) % count) for i in range(count)]
    southward = [((i + 1) % count, i) for i in range(count)]
    swap = [(0, 1), (1, 0)]
    f2 = forward_init.reshape(n_pair * n_lev * n_rows, n_x)
    a2 = adjoint_init.reshape(n_pair * n_lev * n_rows, n_x)
    fold2 = fold.reshape(1, n_x)
    work = n_lev * n_rows * n_all * n_x
    pages = n_lev // n_pair

    to_north, to_south = call(
        functools.partial(send_first, n_lev, n_pair, n_rows),
        [vmem(n_lev + pages + 1, n_pair, n_x), vmem(2 * n_lev + 1, n_pair, n_x)],
        [flags, f2, a2, north_flow, depth],
        work,
    )
    from_south = lax.ppermute(to_north, "horiz", northward)
    from_north = lax.ppermute(to_south, "horiz", southward)
    state = vmem(n_lev, 2, n_all, n_x)
    halo = vmem(n_lev, n_pair, n_x)
    acc = vmem(n_lev + 1, 2, 8, n_x)
    xe, xi, pi, c, wx, hot, mf = call(
        functools.partial(prepare, n_lev, n_pair, n_rows),
        [state, state, state, vmem(13, n_lev, n_rows, n_x), vmem(3, n_rows, n_x), vmem(n_rows, n_pair, n_x), halo],
        [flags, f2, a2, east_flow, north_flow, mixing, depth, color, fold2],
        work * 10,
        [vmem(n_lev, n_rows, n_x)],
    )
    edges = vmem(n_rows, n_all, n_x)
    acce = acci = None
    for step in range(STEPS):
        if step == 0:
            pe, edge, ec, fs = call(
                functools.partial(first_edge, n_lev, n_pair),
                [state, edges, vmem(8, n_lev, 8, n_x), vmem(n_lev, 8, n_x)],
                [flags, xe, xi, pi, c, hot, mf, from_south, from_north, north_flow, depth, fold2],
                work * 5,
            )
        else:
            pe, edge = call(
                functools.partial(next_edge, n_lev, n_pair),
                [state, edges],
                [flags, xe, xi, pi, c, hot, mf, from_south, from_north, ec],
                work * 5,
            )
        far = lax.ppermute(edge, "level", swap)
        if step == STEPS - 1:
            break
        more = [] if step == 0 else [acce]
        xe, to_north, to_south, acce = call(
            functools.partial(edge_back, step == 0, n_lev, n_pair),
            [state, halo, halo, acc],
            [flags, pe, far, c, wx, north_flow, fs] + more,
            work * 2,
        )
        from_south = lax.ppermute(to_north, "horiz", northward)
        from_north = lax.ppermute(to_south, "horiz", southward)
        more = [] if step == 0 else [acci]
        xi, pi, mf, acci = call(
            functools.partial(inner, step == 0, n_lev, n_pair),
            [state, state, halo, acc],
            [flags, pi, far, c, wx, north_flow, fold2, hot, xe] + more,
            work * 7,
        )
    flat = vmem(n_pair * n_lev * n_rows, n_x)
    f_out, a_out, sens = call(
        functools.partial(finish, n_lev, n_pair, n_rows),
        [flat, flat, vmem(n_lev, n_rows, n_x)],
        [flags, pe, pi, far, c, wx, depth, acce, acci],
        work * 4,
        [acc, acc],
    )
    sens = sens + lax.ppermute(sens, "tracer", swap)
    return f_out.reshape(forward_init.shape), a_out.reshape(adjoint_init.shape), sens


def solution(mesh):
    tracers, flows = P("tracer", "level", "horiz", None), P("level", "horiz", None)
    return jax.shard_map(
        per_device,
        mesh=mesh,
        in_specs=(tracers, tracers, flows, flows, P(None, "horiz", None), P("horiz", None), P("horiz", None), P()),
        out_specs=(tracers, tracers, flows),
        check_vma=False,
    )
```

```python
import functools
import jax
import jax.numpy as jnp
from jax import lax
from jax.experimental import pallas as pl
from jax.experimental.pallas import tpu as pltpu
from jax.sharding import PartitionSpec as P

STEPS = 4
LANES = 128
C0F, C0A, CWF, CWA, CEF, CEA, CSF, CSA, CNF, CNA, UP, WI, BACK = range(13)
E0F, E0A, ESF, ESA, T0F, T0A, TNF, TNA = range(8)
F32 = jnp.float32
UNROLL = 8
PIECE = 8


def order(flags_ref, n_lev):
    bottom = flags_ref[0]
    return bottom * (n_lev - 1), 1 - 2 * bottom


def west(v):
    return pltpu.roll(v, 1, 1)


def east(v):
    return pltpu.roll(v, LANES - 1, 1)


def spread(v):
    return jnp.broadcast_to(v, (8, LANES))


def pick(c_ref, which, lev, row):
    return spread(c_ref[which, lev, row : row + 1, :])


def sweep(flags_ref, n_lev, n_pair, rows, put, last):
    k0, dk = order(flags_ref, n_lev)
    halves = n_pair // 8
    zero = jnp.zeros((8, LANES), F32)

    def body(s, carry):
        lev = k0 + dk * s
        out = []
        for i, (up, explicit, swept) in enumerate(rows):
            values = explicit(lev)
            factor = up(lev) if swept else None
            for kind in range(2):
                for g in range(halves):
                    v = values[kind][g]
                    if swept:
                        v = v + factor * carry[len(out)]
                        out.append(v)
                    put(lev, i, kind, g, v)
        return tuple(out)

    n_swept = sum(row[2] for row in rows)
    final = lax.fori_loop(0, n_lev, body, (zero,) * (n_swept * 2 * halves), unroll=UNROLL)
    for at, v in enumerate(final):
        last(at // (2 * halves), at // halves % 2, at % halves, v)


def own_part(n_pair, coef, src, center, sides):
    halves = n_pair // 8

    def explicit(lev):
        wi = coef(WI, lev)
        srcs = [src(g) * wi for g in range(halves)]
        out = []
        for kind in range(2):
            c0, cw, ce = (coef(base + kind, lev) for base in (C0F, CWF, CEF))
            cs = [coef(base + kind, lev) for base, _ in sides]
            vs = []
            for g in range(halves):
                c = center(lev, kind, g)
                v = (c0 * c + srcs[g]) + (cw * west(c) + ce * east(c))
                for k, (_, side) in zip(cs, sides):
                    v = v + k * side(lev, kind, g)
                vs.append(v)
            out.append(vs)
        return out

    return explicit


def back(flags_ref, n_lev, n_pair, rows, wx_ref, far_ref, c_ref, part, put, acc_in, acc_out, done=None):
    bottom = flags_ref[0]
    k0, dk = order(flags_ref, n_lev)
    halves = n_pair // 8
    mid = k0 + dk * (n_lev - 1)
    own, far = [], []
    for i, row in enumerate(rows):
        wa, wb, ff = (spread(wx_ref[j, row : row + 1, :]) for j in range(3))
        for kind in range(2):
            for g in range(halves):
                p_far = far_ref[row, pl.ds((kind * halves + g) * 8, 8), :]
                x = wa * part(mid, i, kind, g) + wb * p_far
                own.append(x)
                far.append(p_far + ff * x)

    def tally(s, now, nxt):
        at = jnp.where(bottom == 0, s + 1, n_lev - 1 - s)
        for i in range(len(rows)):
            b = i * 2 * halves
            total = acc_in(at, i)
            for g in range(halves):
                f, a = b + g, b + halves + g
                total = total + (nxt[f] - now[f]) * (nxt[a] - now[a])
            acc_out(at, i, total)

    def store(lev, xs):
        at = 0
        for i in range(len(rows)):
            for kind in range(2):
                for g in range(halves):
                    put(lev, i, kind, g, xs[at])
                    at += 1

    tally(n_lev - 1, own, far)
    store(mid, own)

    def body(q, nxt):
        s = n_lev - 2 - q
        lev = k0 + dk * s
        now = []
        at = 0
        for i, row in enumerate(rows):
            f = pick(c_ref, BACK, lev, row)
            for kind in range(2):
                for g in range(halves):
                    now.append(part(lev, i, kind, g) + f * nxt[at])
                    at += 1
        tally(s, now, nxt)
        store(lev, now)
        return tuple(now)

    if done is None:
        lax.fori_loop(0, n_lev - 1, body, tuple(own), unroll=UNROLL)
        return
    now = lax.fori_loop(0, PIECE - 1, body, tuple(own), unroll=PIECE - 1)
    done(0)
    for piece in range(1, n_lev // PIECE):
        now = lax.fori_loop(piece * PIECE - 1, (piece + 1) * PIECE - 1, body, now, unroll=PIECE)
        done(piece)


def fold_rows(flags_ref, fold_ref, nf_ref, get, mf_ref, n_lev, n_pair):
    @pl.when(flags_ref[1] == 1)
    def _():
        where_to = spread(fold_ref[0:1, :])

        def body(lev, _):
            n3 = spread(nf_ref[lev, 3:4, :])
            for g in range(n_pair // 8):
                f = jnp.take_along_axis(get(lev, 0, g), where_to, axis=1)
                a = jnp.take_along_axis(get(lev, 1, g), where_to, axis=1)
                mf_ref[lev, pl.ds(g * 8, 8), :] = jnp.where(n3 < 0.0, f, a)
            return 0

        lax.fori_loop(0, n_lev, body, 0, unroll=4)


def rows_at(ref, row, lev, kind, g, halves):
    return ref[lev, row, pl.ds((kind * halves + g) * 8, 8), :]


def send_first(
    n_lev, n_pair, n_rows, f_hbm, a_hbm, nf_hbm, depth_hbm, north_ref, south_ref, f_ref, a_ref, nf_ref, depth_ref, sems
):
    stride = n_lev * n_rows
    part = 4 * stride
    first = lax.axis_index("level") * n_lev
    small = [
        pltpu.make_async_copy(nf_hbm, nf_ref, sems.at[0]),
        pltpu.make_async_copy(depth_hbm, depth_ref, sems.at[1]),
    ]
    large = [
        [
            pltpu.make_async_copy(
                hbm.at[pl.ds(j * part, part), :], to.at[pl.ds(j * part, part), :], sems.at[2 + 2 * j + i]
            )
            for i, (hbm, to) in enumerate(((f_hbm, f_ref), (a_hbm, a_ref)))
        ]
        for j in range(n_pair // 4)
    ]
    for copy in small:
        copy.start()
    for pair in large:
        for copy in pair:
            copy.start()
    for copy in small:
        copy.wait()
    depth = depth_ref[...]
    for lev in range(n_lev):
        page, line = n_lev + lev // n_pair, lev % n_pair
        north_ref[page, line : line + 1, :] = nf_ref[lev, n_rows - 1 : n_rows, :]
    high = depth[n_rows - 1 : n_rows].astype(F32)
    low = depth[0:1].astype(F32)
    north_ref[n_lev + n_lev // n_pair] = jnp.broadcast_to(high, (n_pair, LANES))
    south_ref[2 * n_lev] = jnp.broadcast_to(low, (n_pair, LANES))
    for g in range(n_pair // 8):
        for pair in large[2 * g : 2 * g + 2]:
            for copy in pair:
                copy.wait()

        def body(lev, _, g=g):
            wet = jnp.where(first + lev < depth, 1.0, 0.0)
            w0 = spread(wet[0:1])
            w3 = spread(wet[n_rows - 1 : n_rows])
            n3 = spread(nf_ref[lev, n_rows - 1 : n_rows, :])
            at = g * 8 * stride + lev * n_rows
            low, high = pl.ds(at, 8, stride=stride), pl.ds(at + n_rows - 1, 8, stride=stride)
            to = pl.ds(g * 8, 8)
            north_ref[lev, to, :] = jnp.where(n3 > 0.0, f_ref[high, :], a_ref[high, :]) * w3
            south_ref[lev, to, :] = f_ref[low, :] * w0
            south_ref[n_lev + lev, to, :] = a_ref[low, :] * w0
            return 0

        lax.fori_loop(0, n_lev, body, 0, unroll=UNROLL)


def prepare(
    n_lev, n_pair, n_rows, flags_ref, f_ref, a_ref, ef_ref, nf_ref, mix_ref, depth_ref, color_ref, fold_ref,
    xe_ref, pi_ref, be_ref, c_ref, wx_ref, hot_ref, mf_ref, inv_ref, xi_ref,
):
    halves = n_pair // 8
    stride = n_lev * n_rows
    bottom = flags_ref[0]
    first = bottom * n_lev
    k0, dk = order(flags_ref, n_lev)
    depth = depth_ref[...]

    def lay(lev, _):
        wet = jnp.where(first + lev < depth, 1.0, 0.0)
        for row in range(n_rows):
            w = spread(wet[row : row + 1])
            to_ref, line = (xe_ref, row // 3) if row in (0, 3) else (xi_ref, row - 1)
            for kind, from_ref in enumerate((f_ref, a_ref)):
                for g in range(halves):
                    v = from_ref[pl.ds(g * 8 * stride + lev * n_rows + row, 8, stride=stride), :]
                    to_ref[lev, line, pl.ds((kind * halves + g) * 8, 8), :] = v * w
        return 0

    lax.fori_loop(0, n_lev, lay, 0, unroll=UNROLL)

    def coupling(k):
        inner = jnp.where((k >= 0) & (k < 2 * n_lev - 1), 1.0, 0.0)
        m = mix_ref[jnp.clip(k, 0, 2 * n_lev - 2)]
        return m * jnp.where(k + 1 < depth, inner, 0.0)

    def eliminate(s, carry):
        own_f, far_f = carry
        k = bottom * (2 * n_lev - 1) + dk * s
        prev, nxt = coupling(k - 1 + bottom), coupling(k - bottom)
        inverse = 1.0 / (1.0 + nxt + prev * (1.0 - own_f))
        lev = k0 + dk * s
        inv_ref[lev] = inverse
        c_ref[UP, lev] = prev * inverse
        own_f = nxt * inverse
        c_ref[BACK, lev] = own_f
        k = (1 - bottom) * (2 * n_lev - 1) - dk * s
        prev, nxt = coupling(k - bottom), coupling(k - 1 + bottom)
        far_f = nxt / (1.0 + nxt + prev * (1.0 - far_f))
        return own_f, far_f

    one = jnp.zeros((n_rows, LANES), F32)
    own_f, far_f = lax.fori_loop(0, n_lev, eliminate, (one, one), unroll=UNROLL)
    meet = 1.0 / (1.0 - own_f * far_f)
    wx_ref[0] = meet
    wx_ref[1] = own_f * meet
    wx_ref[2] = far_f

    depth_east = east(depth)
    depth_north = jnp.concatenate([depth[1:], jnp.zeros((1, LANES), jnp.int32)], 0)

    def coefs(lev, _):
        k = first + lev
        wet = jnp.where(k < depth, 1.0, 0.0)
        inverse = inv_ref[lev]
        e = ef_ref[lev] * wet * jnp.where(k < depth_east, 1.0, 0.0)
        n = nf_ref[lev] * wet * jnp.where(k < depth_north, 1.0, 0.0)
        w = west(e)
        s = jnp.concatenate([jnp.zeros((1, LANES), F32), n[:-1]], 0)
        plus = [jnp.maximum(v, 0.0) for v in (w, e, s, n)]
        minus = [jnp.maximum(-v, 0.0) for v in (w, e, s, n)]
        c_ref[C0F, lev] = (1.0 - minus[0] - plus[1] - minus[2] - plus[3]) * inverse
        c_ref[C0A, lev] = (1.0 - plus[0] - minus[1] - plus[2] - minus[3]) * inverse
        c_ref[CWF, lev], c_ref[CWA, lev] = plus[0] * inverse, minus[0] * inverse
        c_ref[CEF, lev], c_ref[CEA, lev] = minus[1] * inverse, plus[1] * inverse
        c_ref[CSF, lev], c_ref[CSA, lev] = plus[2] * inverse, minus[2] * inverse
        c_ref[CNF, lev], c_ref[CNA, lev] = minus[3] * inverse, plus[3] * inverse
        c_ref[WI, lev] = wet * inverse
        return 0

    lax.fori_loop(0, n_lev, coefs, 0, unroll=UNROLL)

    ids = lax.broadcasted_iota(jnp.int32, (n_pair, LANES), 0) + flags_ref[3]
    for row in range(n_rows):
        hot_ref[row] = jnp.where(color_ref[row : row + 1, :] == ids, 1.0, 0.0)

    inner_sweep(n_lev, n_pair, flags_ref, xe_ref, xi_ref, c_ref, None, hot_ref, pi_ref, be_ref)
    fold_rows(
        flags_ref, fold_ref, nf_ref, lambda lev, kind, g: rows_at(xe_ref, 1, lev, kind, g, halves), mf_ref, n_lev, n_pair
    )


def inner_sweep(n_lev, n_pair, flags_ref, xe_ref, xi_ref, c_ref, ec_ref, hot_ref, pi_ref, be_ref):
    halves = n_pair // 8

    def at(ref, line):
        return lambda lev, kind, g: rows_at(ref, line, lev, kind, g, halves)

    x = [at(xe_ref, 0), at(xi_ref, 0), at(xi_ref, 1), at(xe_ref, 1)]

    def row(number):
        edge = {0: {C0F: E0F, C0A: E0A}, 3: {C0F: T0F, C0A: T0A}}.get(number, {}) if ec_ref is not None else {}

        def coef(which, lev):
            return ec_ref[edge[which], lev] if which in edge else pick(c_ref, which, lev, number)

        sides = []
        if number > 0:
            sides.append((CSF, x[number - 1]))
        if number < 3:
            sides.append((CNF, x[number + 1]))
        explicit = own_part(n_pair, coef, lambda g: hot_ref[number, pl.ds(g * 8, 8), :], x[number], sides)
        return lambda lev: coef(UP, lev), explicit, number in (1, 2)

    def put(lev, i, kind, g, v):
        to, line = (pi_ref, i) if i < 2 else (be_ref, i - 2)
        to[lev, line, pl.ds((kind * halves + g) * 8, 8), :] = v

    sweep(flags_ref, n_lev, n_pair, [row(1), row(2), row(0), row(3)], put, lambda *_: None)


def edge_sweep(is_first, n_lev, n_pair, flags_ref, be_ref, pi_ref, c_ref, mf_ref, ms_ref, mn_ref, *rest):
    halves = n_pair // 8
    is_top = flags_ref[1] == 1
    if is_first:
        xe_ref, nf_ref, depth_ref, fold_ref, pe_ref, edge_ref, ec_ref, fs_ref = rest
        first = flags_ref[0] * n_lev
        depth = depth_ref[...]
        own3 = depth[3:4]
        page = n_lev + n_lev // n_pair
        south_depth = ms_ref[page, 0:1, :]
        folded = jnp.take_along_axis(spread(own3.astype(F32)), spread(fold_ref[0:1, :]), axis=1)[0:1]
        north_depth = jnp.where(is_top, folded, mn_ref[2 * n_lev, 0:1, :])
        open_south = jnp.where(flags_ref[2] == 1, 0.0, 1.0)
        for lev in range(n_lev):
            k = first + lev
            kf = k.astype(F32)
            raw = ms_ref[n_lev + lev // n_pair, lev % n_pair : lev % n_pair + 1, :]
            fs_ref[lev] = spread(raw)
            wi0, wi3 = c_ref[WI, lev, 0:1, :], c_ref[WI, lev, 3:4, :]
            s = raw * jnp.where(kf < south_depth, 1.0, 0.0) * open_south * wi0
            n = nf_ref[lev, 3:4, :] * jnp.where(kf < north_depth, 1.0, 0.0) * wi3
            sp, sm, np_, nm = (jnp.maximum(v, 0.0) for v in (s, -s, n, -n))
            ec_ref[E0F, lev] = spread(c_ref[C0F, lev, 0:1, :] - sm)
            ec_ref[E0A, lev] = spread(c_ref[C0A, lev, 0:1, :] - sp)
            ec_ref[ESF, lev] = spread(sp)
            ec_ref[ESA, lev] = spread(sm)
            ec_ref[T0F, lev] = spread(c_ref[C0F, lev, 3:4, :] - np_)
            ec_ref[T0A, lev] = spread(c_ref[C0A, lev, 3:4, :] - nm)
            ec_ref[TNF, lev] = spread(nm)
            ec_ref[TNA, lev] = spread(np_)
    else:
        ec_ref, pe_ref, edge_ref = rest

    def come_north(lev, g):
        to = pl.ds(g * 8, 8)
        if is_first:
            n3 = spread(nf_ref[lev, 3:4, :])
            come = jnp.where(n3 < 0.0, mn_ref[lev, to, :], mn_ref[n_lev + lev, to, :])
        else:
            come = mn_ref[lev, to, :]
        return jnp.where(is_top, mf_ref[lev, to, :], come)

    def row(i, number, inflow, come):
        def explicit(lev):
            ks = [ec_ref[inflow + kind, lev] for kind in range(2)]
            ms = [come(lev, g) for g in range(halves)]
            out = []
            for kind in range(2):
                vs = []
                for g in range(halves):
                    v = rows_at(be_ref, i, lev, kind, g, halves) + ks[kind] * ms[g]
                    if is_first:
                        v = v - ks[1 - kind] * rows_at(xe_ref, i, lev, kind, g, halves)
                    vs.append(v)
                out.append(vs)
            return out

        return lambda lev: pick(c_ref, UP, lev, number), explicit, True

    def put(lev, i, kind, g, v):
        pe_ref[lev, i, pl.ds((kind * halves + g) * 8, 8), :] = v

    def last(i, kind, g, v):
        edge_ref[3 * i, pl.ds((kind * halves + g) * 8, 8), :] = v

    rows = [row(0, 0, ESF, lambda lev, g: ms_ref[lev, pl.ds(g * 8, 8), :]), row(1, 3, TNF, come_north)]
    sweep(flags_ref, n_lev, n_pair, rows, put, last)
    k0, dk = order(flags_ref, n_lev)
    mid = k0 + dk * (n_lev - 1)
    edge_ref[1] = pi_ref[mid, 0]
    edge_ref[2] = pi_ref[mid, 1]


def tallies(is_first, in_ref, out_ref, n_lev):
    if is_first:
        out_ref[0] = jnp.zeros(out_ref.shape[1:], F32)
        out_ref[n_lev] = jnp.zeros(out_ref.shape[1:], F32)
    else:
        out_ref[0] = in_ref[0]
        out_ref[n_lev] = in_ref[n_lev]
    zero = jnp.zeros((8, LANES), F32)

    def put(at, i, v):
        out_ref[at, i] = v

    return (lambda at, i: zero) if is_first else (lambda at, i: in_ref[at, i]), put


def edge_back(is_first, n_lev, n_pair, flags_ref, pe_ref, far_ref, c_ref, wx_ref, nf_ref, fs_ref, *rest):
    halves = n_pair // 8
    acc_ref, (xe_ref, north_ref, south_ref, out_ref) = (None, rest) if is_first else (rest[0], rest[1:])
    acc_in, acc_out = tallies(is_first, acc_ref, out_ref, n_lev)
    held = {}

    def put(lev, i, kind, g, v):
        xe_ref[lev, i, pl.ds((kind * halves + g) * 8, 8), :] = v
        if kind == 0:
            held[i, g] = v
        elif i == 0:
            south_ref[lev, pl.ds(g * 8, 8), :] = jnp.where(fs_ref[lev] < 0.0, held[i, g], v)
        else:
            n3 = spread(nf_ref[lev, 3:4, :])
            north_ref[lev, pl.ds(g * 8, 8), :] = jnp.where(n3 > 0.0, held[i, g], v)

    back(
        flags_ref, n_lev, n_pair, (0, 3), wx_ref, far_ref, c_ref,
        lambda lev, i, kind, g: rows_at(pe_ref, i, lev, kind, g, halves), put, acc_in, acc_out,
    )


def inner(
    is_first, n_lev, n_pair, flags_ref, pi_ref, far_ref, c_ref, ec_ref, wx_ref, nf_ref, fold_ref, hot_ref, xe_ref, *rest
):
    halves = n_pair // 8
    acc_ref, (pn_ref, be_ref, mf_ref, out_ref, xi_ref) = (None, rest) if is_first else (rest[0], rest[1:])
    acc_in, acc_out = tallies(is_first, acc_ref, out_ref, n_lev)

    def put(lev, i, kind, g, v):
        xi_ref[lev, i, pl.ds((kind * halves + g) * 8, 8), :] = v

    back(
        flags_ref, n_lev, n_pair, (1, 2), wx_ref, far_ref, c_ref,
        lambda lev, i, kind, g: rows_at(pi_ref, i, lev, kind, g, halves), put, acc_in, acc_out,
    )
    inner_sweep(n_lev, n_pair, flags_ref, xe_ref, xi_ref, c_ref, ec_ref, hot_ref, pn_ref, be_ref)
    fold_rows(
        flags_ref, fold_ref, nf_ref, lambda lev, kind, g: rows_at(xe_ref, 1, lev, kind, g, halves), mf_ref, n_lev, n_pair
    )


def finish(
    n_lev, n_pair, n_rows, flags_ref, pe_ref, pi_ref, far_ref, c_ref, wx_ref, depth_ref, acce_ref, acci_ref,
    f_hbm, a_hbm, sens_ref, te_ref, ti_ref, f_ref, a_ref, sems,
):
    halves = n_pair // 8
    stride = n_lev * n_rows
    bottom = lax.axis_index("level")
    ps = [(pe_ref, 0), (pi_ref, 0), (pi_ref, 1), (pe_ref, 1)]
    e_in, e_out = tallies(False, acce_ref, te_ref, n_lev)
    i_in, i_out = tallies(False, acci_ref, ti_ref, n_lev)
    copies = []

    def put(lev, i, kind, g, v):
        to = f_ref if kind == 0 else a_ref
        to[pl.ds(g * 8 * stride + lev * n_rows + i, 8, stride=stride), :] = v

    def done(piece):
        low = jnp.where(bottom == 0, n_lev - (piece + 1) * PIECE, piece * PIECE)
        at = pl.ds(pl.multiple_of(low * n_rows, PIECE * n_rows), PIECE * n_rows)
        for kind, (ref, hbm) in enumerate(((f_ref, f_hbm), (a_ref, a_hbm))):
            copy = pltpu.make_async_copy(
                ref.reshape(n_pair, stride, LANES).at[:, at, :], hbm.at[:, at, :], sems.at[2 * piece + kind]
            )
            copy.start()
            copies.append(copy)

    back(
        flags_ref, n_lev, n_pair, range(4), wx_ref, far_ref, c_ref,
        lambda lev, i, kind, g: rows_at(ps[i][0], ps[i][1], lev, kind, g, halves), put,
        lambda at, i: e_in(at, i // 3) if i in (0, 3) else i_in(at, i - 1),
        lambda at, i, v: e_out(at, i // 3, v) if i in (0, 3) else i_out(at, i - 1, v),
        done,
    )
    first = flags_ref[0] * n_lev
    depth = depth_ref[...]

    def reduce(lev, _):
        k = first + lev
        live = jnp.where((k + 1 < depth) & (k + 1 < 2 * n_lev), 1.0 / STEPS, 0.0)
        e0, e3 = (jnp.sum(te_ref[lev + 1, i], axis=0, keepdims=True) for i in range(2))
        i1, i2 = (jnp.sum(ti_ref[lev + 1, i], axis=0, keepdims=True) for i in range(2))
        sens_ref[lev] = jnp.concatenate([e0, i1, i2, e3], 0) * live
        return 0

    lax.fori_loop(0, n_lev, reduce, 0, unroll=UNROLL)
    for copy in copies:
        copy.wait()


def vmem(*shape):
    return pltpu.VMEM(shape, F32)


def call(kernel, outs, args, flops, scratch=(), first=pltpu.SMEM, hbm=0):
    spec = pl.BlockSpec(memory_space=pltpu.VMEM)
    far = pl.BlockSpec(memory_space=pltpu.HBM)
    return pl.pallas_call(
        kernel,
        out_shape=tuple(outs),
        in_specs=[pl.BlockSpec(memory_space=pltpu.SMEM)] + [spec] * (len(args) - 1)
        if first is pltpu.SMEM
        else [far] * len(args),
        out_specs=tuple([far] * hbm + [spec] * (len(outs) - hbm)),
        scratch_shapes=list(scratch),
        compiler_params=pltpu.CompilerParams(vmem_limit_bytes=24 * 2**20),
        cost_estimate=pl.CostEstimate(flops=flops, bytes_accessed=flops // 8, transcendentals=0),
    )(
        *(
            args[:1] + [pltpu.with_memory_space_constraint(a, pltpu.VMEM) for a in args[1:]]
            if first is pltpu.SMEM
            else [pltpu.with_memory_space_constraint(a, pltpu.HBM) for a in args]
        )
    )


def per_device(forward_init, adjoint_init, east_flow, north_flow, mixing, depth, color, fold):
    n_pair, n_lev, n_rows, n_x = forward_init.shape
    n_all = 2 * n_pair
    count = lax.axis_size("horiz")
    place = lax.axis_index("horiz")
    flags = jnp.stack(
        [
            lax.axis_index("level"),
            (place == count - 1).astype(jnp.int32),
            (place == 0).astype(jnp.int32),
            lax.axis_index("tracer") * n_pair,
        ]
    ).astype(jnp.int32)
    northward = [(i, (i + 1) % count) for i in range(count)]
    southward = [((i + 1) % count, i) for i in range(count)]
    swap = [(0, 1), (1, 0)]
    f2 = forward_init.reshape(n_pair * n_lev * n_rows, n_x)
    a2 = adjoint_init.reshape(n_pair * n_lev * n_rows, n_x)
    fold2 = fold.reshape(1, n_x)
    work = n_lev * n_rows * n_all * n_x
    pages = n_lev // n_pair

    flat = vmem(n_pair * n_lev * n_rows, n_x)
    to_north, to_south, f2, a2, north_flow, depth = call(
        functools.partial(send_first, n_lev, n_pair, n_rows),
        [
            vmem(n_lev + pages + 1, n_pair, n_x),
            vmem(2 * n_lev + 1, n_pair, n_x),
            flat,
            flat,
            vmem(n_lev, n_rows, n_x),
            pltpu.VMEM((n_rows, n_x), jnp.int32),
        ],
        [f2, a2, north_flow, depth],
        work,
        [pltpu.SemaphoreType.DMA((2 + n_pair // 2,))],
        first=pltpu.HBM,
    )
    from_north = lax.ppermute(to_south, "horiz", southward)
    from_south = lax.ppermute(to_north, "horiz", northward)
    state = vmem(n_lev, 2, n_all, n_x)
    halo = vmem(n_lev, n_pair, n_x)
    acc = vmem(n_lev + 1, 2, 8, n_x)
    xe, pi, be, c, wx, hot, mf = call(
        functools.partial(prepare, n_lev, n_pair, n_rows),
        [state] * 3 + [vmem(13, n_lev, n_rows, n_x), vmem(3, n_rows, n_x), vmem(n_rows, n_pair, n_x), halo],
        [flags, f2, a2, east_flow, north_flow, mixing, depth, color, fold2],
        work * 10,
        [vmem(n_lev, n_rows, n_x), state],
    )
    edges = vmem(n_rows, n_all, n_x)
    acce = acci = None
    for step in range(STEPS):
        if step == 0:
            pe, edge, ec, fs = call(
                functools.partial(edge_sweep, True, n_lev, n_pair),
                [state, edges, vmem(8, n_lev, 8, n_x), vmem(n_lev, 8, n_x)],
                [flags, be, pi, c, mf, from_south, from_north, xe, north_flow, depth, fold2],
                work * 3,
            )
        else:
            pe, edge = call(
                functools.partial(edge_sweep, False, n_lev, n_pair),
                [state, edges],
                [flags, be, pi, c, mf, from_south, from_north, ec],
                work * 2,
            )
        far = lax.ppermute(edge, "level", swap)
        if step == STEPS - 1:
            break
        more = [] if step == 0 else [acce]
        xe, to_north, to_south, acce = call(
            functools.partial(edge_back, step == 0, n_lev, n_pair),
            [state, halo, halo, acc],
            [flags, pe, far, c, wx, north_flow, fs] + more,
            work * 2,
        )
        from_south = lax.ppermute(to_north, "horiz", northward)
        from_north = lax.ppermute(to_south, "horiz", southward)
        more = [] if step == 0 else [acci]
        pi, be, mf, acci = call(
            functools.partial(inner, step == 0, n_lev, n_pair),
            [state, state, halo, acc],
            [flags, pi, far, c, ec, wx, north_flow, fold2, hot, xe] + more,
            work * 9,
            [state],
        )
    out = jax.ShapeDtypeStruct((n_pair, n_lev * n_rows, n_x), F32)
    f_out, a_out, sens = call(
        functools.partial(finish, n_lev, n_pair, n_rows),
        [out, out, vmem(n_lev, n_rows, n_x)],
        [flags, pe, pi, far, c, wx, depth, acce, acci],
        work * 4,
        [acc, acc, flat, flat, pltpu.SemaphoreType.DMA((2 * n_lev // PIECE,))],
        hbm=2,
    )
    sens = sens + lax.ppermute(sens, "tracer", swap)
    return f_out.reshape(forward_init.shape), a_out.reshape(adjoint_init.shape), sens


def solution(mesh):
    tracers, flows = P("tracer", "level", "horiz", None), P("level", "horiz", None)
    return jax.shard_map(
        per_device,
        mesh=mesh,
        in_specs=(tracers, tracers, flows, flows, P(None, "horiz", None), P("horiz", None), P("horiz", None), P()),
        out_specs=(tracers, tracers, flows),
        check_vma=False,
    )
```

```python
import functools
import jax
import jax.numpy as jnp
from jax import lax
from jax.experimental import pallas as pl
from jax.experimental.pallas import tpu as pltpu
from jax.sharding import PartitionSpec as P

STEPS = 4
LANES = 128
C0F, C0A, CWF, CWA, CEF, CEA, CSF, CSA, CNF, CNA, UP, WI, BACK = range(13)
E0F, E0A, ESF, ESA, T0F, T0A, TNF, TNA = range(8)
F32 = jnp.float32
UNROLL = 8
PIECES = 4


def order(flags, n_lev):
    bottom = flags[0]
    return bottom * (n_lev - 1), 1 - 2 * bottom


def west(v):
    return pltpu.roll(v, 1, 1)


def east(v):
    return pltpu.roll(v, LANES - 1, 1)


def spread(v):
    return jnp.broadcast_to(v, (8, LANES))


def pick(c_ref, which, lev, row):
    return spread(c_ref[which, lev, row : row + 1, :])


def sweep(flags, n_lev, n_pair, rows, put, last):
    k0, dk = order(flags, n_lev)
    halves = n_pair // 8
    zero = jnp.zeros((8, LANES), F32)

    def body(s, carry):
        lev = k0 + dk * s
        out = []
        for i, (up, explicit, swept) in enumerate(rows):
            values = explicit(lev)
            factor = up(lev) if swept else None
            for kind in range(2):
                for g in range(halves):
                    v = values[kind][g]
                    if swept:
                        v = v + factor * carry[len(out)]
                        out.append(v)
                    put(lev, i, kind, g, v)
        return tuple(out)

    n_swept = sum(row[2] for row in rows)
    final = lax.fori_loop(0, n_lev, body, (zero,) * (n_swept * 2 * halves), unroll=UNROLL)
    for at, v in enumerate(final):
        last(at // (2 * halves), at // halves % 2, at % halves, v)


def own_part(n_pair, coef, src, center, sides):
    halves = n_pair // 8

    def explicit(lev):
        wi = coef(WI, lev)
        srcs = [src(g) * wi for g in range(halves)]
        out = []
        for kind in range(2):
            c0, cw, ce = (coef(base + kind, lev) for base in (C0F, CWF, CEF))
            cs = [coef(base + kind, lev) for base, _ in sides]
            vs = []
            for g in range(halves):
                c = center(lev, kind, g)
                v = (c0 * c + srcs[g]) + (cw * west(c) + ce * east(c))
                for k, (_, side) in zip(cs, sides):
                    v = v + k * side(lev, kind, g)
                vs.append(v)
            out.append(vs)
        return out

    return explicit


def back(flags, n_lev, n_pair, rows, wx_ref, far_ref, c_ref, part, put, acc_in, acc_out):
    bottom = flags[0]
    k0, dk = order(flags, n_lev)
    halves = n_pair // 8
    mid = k0 + dk * (n_lev - 1)
    own, far = [], []
    for i, row in enumerate(rows):
        wa, wb, ff = (spread(wx_ref[j, row : row + 1, :]) for j in range(3))
        for kind in range(2):
            for g in range(halves):
                p_far = far_ref[row, pl.ds((kind * halves + g) * 8, 8), :]
                x = wa * part(mid, i, kind, g) + wb * p_far
                own.append(x)
                far.append(p_far + ff * x)

    def tally(s, now, nxt):
        at = jnp.where(bottom == 0, s + 1, n_lev - 1 - s)
        for i in range(len(rows)):
            b = i * 2 * halves
            total = acc_in(at, i)
            for g in range(halves):
                f, a = b + g, b + halves + g
                total = total + (nxt[f] - now[f]) * (nxt[a] - now[a])
            acc_out(at, i, total)

    def store(lev, xs):
        at = 0
        for i in range(len(rows)):
            for kind in range(2):
                for g in range(halves):
                    put(lev, i, kind, g, xs[at])
                    at += 1

    tally(n_lev - 1, own, far)
    store(mid, own)

    def body(q, nxt):
        s = n_lev - 2 - q
        lev = k0 + dk * s
        now = []
        at = 0
        for i, row in enumerate(rows):
            f = pick(c_ref, BACK, lev, row)
            for kind in range(2):
                for g in range(halves):
                    now.append(part(lev, i, kind, g) + f * nxt[at])
                    at += 1
        tally(s, now, nxt)
        store(lev, now)
        return tuple(now)

    lax.fori_loop(0, n_lev - 1, body, tuple(own), unroll=UNROLL)


def fold_rows(flags, fold_ref, nf_ref, get, mf_ref, n_lev, n_pair):
    @pl.when(flags[1] == 1)
    def _():
        where_to = spread(fold_ref[0:1, :])

        def body(lev, _):
            n3 = spread(nf_ref[lev, 3:4, :])
            for g in range(n_pair // 8):
                f = jnp.take_along_axis(get(lev, 0, g), where_to, axis=1)
                a = jnp.take_along_axis(get(lev, 1, g), where_to, axis=1)
                mf_ref[lev, pl.ds(g * 8, 8), :] = jnp.where(n3 < 0.0, f, a)
            return 0

        lax.fori_loop(0, n_lev, body, 0, unroll=4)


def rows_at(ref, row, lev, kind, g, halves):
    return ref[lev, row, pl.ds((kind * halves + g) * 8, 8), :]


def send_first(
    n_lev, n_pair, n_rows, f_hbm, a_hbm, nf_hbm, depth_hbm, even_ref, odd_ref, f_ref, a_ref, nf_ref, depth_ref, sems
):
    stride = n_lev * n_rows
    part = 4 * stride
    first = lax.axis_index("level") * n_lev
    small = [
        pltpu.make_async_copy(nf_hbm, nf_ref, sems.at[0]),
        pltpu.make_async_copy(depth_hbm, depth_ref, sems.at[1]),
    ]
    large = [
        [
            pltpu.make_async_copy(
                hbm.at[pl.ds(j * part, part), :], to.at[pl.ds(j * part, part), :], sems.at[2 + 2 * j + i]
            )
            for i, (hbm, to) in enumerate(((f_hbm, f_ref), (a_hbm, a_ref)))
        ]
        for j in range(n_pair // 4)
    ]
    for copy in small:
        copy.start()
    for pair in large:
        for copy in pair:
            copy.start()
    for copy in small:
        copy.wait()
    depth = depth_ref[...]
    up_even = lax.rem(lax.axis_index("horiz"), 2) == 0
    high = depth[n_rows - 1 : n_rows].astype(F32)
    low = depth[0:1].astype(F32)
    even_ref[2 * n_lev] = jnp.broadcast_to(jnp.where(up_even, high, low), (n_pair, LANES))
    odd_ref[2 * n_lev] = jnp.broadcast_to(jnp.where(up_even, low, high), (n_pair, LANES))
    for g in range(n_pair // 8):
        for pair in large[2 * g : 2 * g + 2]:
            for copy in pair:
                copy.wait()

        def body(lev, _, g=g):
            wet = jnp.where(first + lev < depth, 1.0, 0.0)
            w0 = spread(wet[0:1])
            w3 = spread(wet[n_rows - 1 : n_rows])
            n3 = spread(nf_ref[lev, n_rows - 1 : n_rows, :])
            at = g * 8 * stride + lev * n_rows
            low, high = pl.ds(at, 8, stride=stride), pl.ds(at + n_rows - 1, 8, stride=stride)
            to = pl.ds(g * 8, 8)
            north = jnp.where(n3 > 0.0, f_ref[high, :], a_ref[high, :]) * w3
            south = f_ref[low, :] * w0
            even_ref[lev, to, :] = jnp.where(up_even, north, south)
            odd_ref[lev, to, :] = jnp.where(up_even, south, north)
            south = a_ref[low, :] * w0
            even_ref[n_lev + lev, to, :] = south
            odd_ref[n_lev + lev, to, :] = south
            return 0

        lax.fori_loop(0, n_lev, body, 0, unroll=UNROLL)

    def flow(ref):
        for lev in range(n_lev):
            page, line = n_lev + lev // n_pair, lev % n_pair
            ref[page, line : line + 1, :] = nf_ref[lev, n_rows - 1 : n_rows, :]

    pl.when(up_even)(lambda: flow(even_ref))
    pl.when(jnp.logical_not(up_even))(lambda: flow(odd_ref))


def prepare(
    n_lev, n_pair, n_rows, f_ref, a_ref, ef_ref, nf_ref, mix_ref, depth_ref, color_ref, fold_ref,
    xe_ref, pi_ref, be_ref, c_ref, wx_ref, hot_ref, mf_ref, inv_ref, xi_ref,
):
    flags = where_am_i(n_pair)
    halves = n_pair // 8
    stride = n_lev * n_rows
    bottom = flags[0]
    first = bottom * n_lev
    k0, dk = order(flags, n_lev)
    depth = depth_ref[...]

    def lay(lev, _):
        wet = jnp.where(first + lev < depth, 1.0, 0.0)
        for row in range(n_rows):
            w = spread(wet[row : row + 1])
            to_ref, line = (xe_ref, row // 3) if row in (0, 3) else (xi_ref, row - 1)
            for kind, from_ref in enumerate((f_ref, a_ref)):
                for g in range(halves):
                    v = from_ref[pl.ds(g * 8 * stride + lev * n_rows + row, 8, stride=stride), :]
                    to_ref[lev, line, pl.ds((kind * halves + g) * 8, 8), :] = v * w
        return 0

    lax.fori_loop(0, n_lev, lay, 0, unroll=UNROLL)

    def coupling(k):
        inner = jnp.where((k >= 0) & (k < 2 * n_lev - 1), 1.0, 0.0)
        m = mix_ref[jnp.clip(k, 0, 2 * n_lev - 2)]
        return m * jnp.where(k + 1 < depth, inner, 0.0)

    def eliminate(s, carry):
        own_f, far_f = carry
        k = bottom * (2 * n_lev - 1) + dk * s
        prev, nxt = coupling(k - 1 + bottom), coupling(k - bottom)
        inverse = 1.0 / (1.0 + nxt + prev * (1.0 - own_f))
        lev = k0 + dk * s
        inv_ref[lev] = inverse
        c_ref[UP, lev] = prev * inverse
        own_f = nxt * inverse
        c_ref[BACK, lev] = own_f
        k = (1 - bottom) * (2 * n_lev - 1) - dk * s
        prev, nxt = coupling(k - bottom), coupling(k - 1 + bottom)
        far_f = nxt / (1.0 + nxt + prev * (1.0 - far_f))
        return own_f, far_f

    one = jnp.zeros((n_rows, LANES), F32)
    own_f, far_f = lax.fori_loop(0, n_lev, eliminate, (one, one), unroll=UNROLL)
    meet = 1.0 / (1.0 - own_f * far_f)
    wx_ref[0] = meet
    wx_ref[1] = own_f * meet
    wx_ref[2] = far_f

    depth_east = east(depth)
    depth_north = jnp.concatenate([depth[1:], jnp.zeros((1, LANES), jnp.int32)], 0)

    def coefs(lev, _):
        k = first + lev
        wet = jnp.where(k < depth, 1.0, 0.0)
        inverse = inv_ref[lev]
        e = ef_ref[lev] * wet * jnp.where(k < depth_east, 1.0, 0.0)
        n = nf_ref[lev] * wet * jnp.where(k < depth_north, 1.0, 0.0)
        w = west(e)
        s = jnp.concatenate([jnp.zeros((1, LANES), F32), n[:-1]], 0)
        plus = [jnp.maximum(v, 0.0) for v in (w, e, s, n)]
        minus = [jnp.maximum(-v, 0.0) for v in (w, e, s, n)]
        c_ref[C0F, lev] = (1.0 - minus[0] - plus[1] - minus[2] - plus[3]) * inverse
        c_ref[C0A, lev] = (1.0 - plus[0] - minus[1] - plus[2] - minus[3]) * inverse
        c_ref[CWF, lev], c_ref[CWA, lev] = plus[0] * inverse, minus[0] * inverse
        c_ref[CEF, lev], c_ref[CEA, lev] = minus[1] * inverse, plus[1] * inverse
        c_ref[CSF, lev], c_ref[CSA, lev] = plus[2] * inverse, minus[2] * inverse
        c_ref[CNF, lev], c_ref[CNA, lev] = minus[3] * inverse, plus[3] * inverse
        c_ref[WI, lev] = wet * inverse
        return 0

    lax.fori_loop(0, n_lev, coefs, 0, unroll=UNROLL)

    ids = lax.broadcasted_iota(jnp.int32, (n_pair, LANES), 0) + flags[3]
    for row in range(n_rows):
        hot_ref[row] = jnp.where(color_ref[row : row + 1, :] == ids, 1.0, 0.0)

    inner_sweep(n_lev, n_pair, flags, xe_ref, xi_ref, c_ref, None, hot_ref, pi_ref, be_ref)
    fold_rows(
        flags, fold_ref, nf_ref, lambda lev, kind, g: rows_at(xe_ref, 1, lev, kind, g, halves), mf_ref, n_lev, n_pair
    )


def inner_sweep(n_lev, n_pair, flags, xe_ref, xi_ref, c_ref, ec_ref, hot_ref, pi_ref, be_ref):
    halves = n_pair // 8

    def at(ref, line):
        return lambda lev, kind, g: rows_at(ref, line, lev, kind, g, halves)

    x = [at(xe_ref, 0), at(xi_ref, 0), at(xi_ref, 1), at(xe_ref, 1)]

    def row(number):
        edge = {0: {C0F: E0F, C0A: E0A}, 3: {C0F: T0F, C0A: T0A}}.get(number, {}) if ec_ref is not None else {}

        def coef(which, lev):
            return ec_ref[edge[which], lev] if which in edge else pick(c_ref, which, lev, number)

        sides = []
        if number > 0:
            sides.append((CSF, x[number - 1]))
        if number < 3:
            sides.append((CNF, x[number + 1]))
        explicit = own_part(n_pair, coef, lambda g: hot_ref[number, pl.ds(g * 8, 8), :], x[number], sides)
        return lambda lev: coef(UP, lev), explicit, number in (1, 2)

    def put(lev, i, kind, g, v):
        to, line = (pi_ref, i) if i < 2 else (be_ref, i - 2)
        to[lev, line, pl.ds((kind * halves + g) * 8, 8), :] = v

    sweep(flags, n_lev, n_pair, [row(1), row(2), row(0), row(3)], put, lambda *_: None)


def edge_sweep(is_first, n_lev, n_pair, be_ref, pi_ref, c_ref, mf_ref, even_ref, odd_ref, *rest):
    flags = where_am_i(n_pair)
    halves = n_pair // 8
    is_top = flags[1] == 1
    up_even = flags[4] == 0

    def from_south(*at):
        return jnp.where(up_even, odd_ref[at], even_ref[at])

    def from_north(*at):
        return jnp.where(up_even, even_ref[at], odd_ref[at])

    if is_first:
        xe_ref, nf_ref, depth_ref, fold_ref, pe_ref, edge_ref, ec_ref, fs_ref = rest
        first = flags[0] * n_lev
        depth = depth_ref[...]
        own3 = depth[3:4]
        south_depth = from_south(2 * n_lev, slice(0, 1), slice(None))
        folded = jnp.take_along_axis(spread(own3.astype(F32)), spread(fold_ref[0:1, :]), axis=1)[0:1]
        north_depth = jnp.where(is_top, folded, from_north(2 * n_lev, slice(0, 1), slice(None)))
        open_south = jnp.where(flags[2] == 1, 0.0, 1.0)
        for lev in range(n_lev):
            k = first + lev
            kf = k.astype(F32)
            line = lev % n_pair
            raw = from_south(n_lev + lev // n_pair, slice(line, line + 1), slice(None))
            fs_ref[lev] = spread(raw)
            wi0, wi3 = c_ref[WI, lev, 0:1, :], c_ref[WI, lev, 3:4, :]
            s = raw * jnp.where(kf < south_depth, 1.0, 0.0) * open_south * wi0
            n = nf_ref[lev, 3:4, :] * jnp.where(kf < north_depth, 1.0, 0.0) * wi3
            sp, sm, np_, nm = (jnp.maximum(v, 0.0) for v in (s, -s, n, -n))
            ec_ref[E0F, lev] = spread(c_ref[C0F, lev, 0:1, :] - sm)
            ec_ref[E0A, lev] = spread(c_ref[C0A, lev, 0:1, :] - sp)
            ec_ref[ESF, lev] = spread(sp)
            ec_ref[ESA, lev] = spread(sm)
            ec_ref[T0F, lev] = spread(c_ref[C0F, lev, 3:4, :] - np_)
            ec_ref[T0A, lev] = spread(c_ref[C0A, lev, 3:4, :] - nm)
            ec_ref[TNF, lev] = spread(nm)
            ec_ref[TNA, lev] = spread(np_)
    else:
        ec_ref, pe_ref, edge_ref = rest

    def come_north(lev, g):
        to = pl.ds(g * 8, 8)
        if is_first:
            n3 = spread(nf_ref[lev, 3:4, :])
            come = jnp.where(n3 < 0.0, from_north(lev, to, slice(None)), from_north(n_lev + lev, to, slice(None)))
        else:
            come = from_north(lev, to, slice(None))
        return jnp.where(is_top, mf_ref[lev, to, :], come)

    def row(i, number, inflow, come):
        def explicit(lev):
            ks = [ec_ref[inflow + kind, lev] for kind in range(2)]
            ms = [come(lev, g) for g in range(halves)]
            out = []
            for kind in range(2):
                vs = []
                for g in range(halves):
                    v = rows_at(be_ref, i, lev, kind, g, halves) + ks[kind] * ms[g]
                    if is_first:
                        v = v - ks[1 - kind] * rows_at(xe_ref, i, lev, kind, g, halves)
                    vs.append(v)
                out.append(vs)
            return out

        return lambda lev: pick(c_ref, UP, lev, number), explicit, True

    def put(lev, i, kind, g, v):
        pe_ref[lev, i, pl.ds((kind * halves + g) * 8, 8), :] = v

    def last(i, kind, g, v):
        edge_ref[3 * i, pl.ds((kind * halves + g) * 8, 8), :] = v

    rows = [row(0, 0, ESF, lambda lev, g: from_south(lev, pl.ds(g * 8, 8), slice(None))), row(1, 3, TNF, come_north)]
    sweep(flags, n_lev, n_pair, rows, put, last)
    k0, dk = order(flags, n_lev)
    mid = k0 + dk * (n_lev - 1)
    edge_ref[1] = pi_ref[mid, 0]
    edge_ref[2] = pi_ref[mid, 1]


def tallies(is_first, in_ref, out_ref, n_lev):
    if is_first:
        out_ref[0] = jnp.zeros(out_ref.shape[1:], F32)
        out_ref[n_lev] = jnp.zeros(out_ref.shape[1:], F32)
    else:
        out_ref[0] = in_ref[0]
        out_ref[n_lev] = in_ref[n_lev]
    zero = jnp.zeros((8, LANES), F32)

    def put(at, i, v):
        out_ref[at, i] = v

    return (lambda at, i: zero) if is_first else (lambda at, i: in_ref[at, i]), put


def edge_back(is_first, n_lev, n_pair, pe_ref, far_ref, c_ref, wx_ref, nf_ref, fs_ref, *rest):
    flags = where_am_i(n_pair)
    halves = n_pair // 8
    acc_ref, (xe_ref, even_ref, odd_ref, out_ref) = (None, rest) if is_first else (rest[0], rest[1:])
    acc_in, acc_out = tallies(is_first, acc_ref, out_ref, n_lev)
    held, south = {}, {}
    up_even = flags[4] == 0

    def put(lev, i, kind, g, v):
        xe_ref[lev, i, pl.ds((kind * halves + g) * 8, 8), :] = v
        if kind == 0:
            held[i, g] = v
        elif i == 0:
            south[g] = jnp.where(fs_ref[lev] < 0.0, held[i, g], v)
        else:
            n3 = spread(nf_ref[lev, 3:4, :])
            north = jnp.where(n3 > 0.0, held[i, g], v)
            even_ref[lev, pl.ds(g * 8, 8), :] = jnp.where(up_even, north, south[g])
            odd_ref[lev, pl.ds(g * 8, 8), :] = jnp.where(up_even, south[g], north)

    back(
        flags, n_lev, n_pair, (0, 3), wx_ref, far_ref, c_ref,
        lambda lev, i, kind, g: rows_at(pe_ref, i, lev, kind, g, halves), put, acc_in, acc_out,
    )


def inner(
    is_first, n_lev, n_pair, pi_ref, far_ref, c_ref, ec_ref, wx_ref, nf_ref, fold_ref, hot_ref, xe_ref, *rest
):
    flags = where_am_i(n_pair)
    halves = n_pair // 8
    acc_ref, (pn_ref, be_ref, mf_ref, out_ref, xi_ref) = (None, rest) if is_first else (rest[0], rest[1:])
    acc_in, acc_out = tallies(is_first, acc_ref, out_ref, n_lev)

    def put(lev, i, kind, g, v):
        xi_ref[lev, i, pl.ds((kind * halves + g) * 8, 8), :] = v

    back(
        flags, n_lev, n_pair, (1, 2), wx_ref, far_ref, c_ref,
        lambda lev, i, kind, g: rows_at(pi_ref, i, lev, kind, g, halves), put, acc_in, acc_out,
    )
    inner_sweep(n_lev, n_pair, flags, xe_ref, xi_ref, c_ref, ec_ref, hot_ref, pn_ref, be_ref)
    fold_rows(
        flags, fold_ref, nf_ref, lambda lev, kind, g: rows_at(xe_ref, 1, lev, kind, g, halves), mf_ref, n_lev, n_pair
    )


def finish(
    n_lev, n_pair, n_rows, pe_ref, pi_ref, far_ref, c_ref, wx_ref, depth_ref, acce_ref, acci_ref,
    f_ref, a_ref, sens_ref, te_ref, ti_ref,
):
    flags = where_am_i(n_pair)
    halves = n_pair // 8
    stride = n_lev * n_rows
    ps = [(pe_ref, 0), (pi_ref, 0), (pi_ref, 1), (pe_ref, 1)]
    e_in, e_out = tallies(False, acce_ref, te_ref, n_lev)
    i_in, i_out = tallies(False, acci_ref, ti_ref, n_lev)

    def put(lev, i, kind, g, v):
        to = f_ref if kind == 0 else a_ref
        to[pl.ds(g * 8 * stride + lev * n_rows + i, 8, stride=stride), :] = v

    back(
        flags, n_lev, n_pair, range(4), wx_ref, far_ref, c_ref,
        lambda lev, i, kind, g: rows_at(ps[i][0], ps[i][1], lev, kind, g, halves), put,
        lambda at, i: e_in(at, i // 3) if i in (0, 3) else i_in(at, i - 1),
        lambda at, i, v: e_out(at, i // 3, v) if i in (0, 3) else i_out(at, i - 1, v),
    )
    first = flags[0] * n_lev
    depth = depth_ref[...]

    def reduce(lev, _):
        k = first + lev
        live = jnp.where((k + 1 < depth) & (k + 1 < 2 * n_lev), 1.0 / STEPS, 0.0)
        e0, e3 = (jnp.sum(te_ref[lev + 1, i], axis=0, keepdims=True) for i in range(2))
        i1, i2 = (jnp.sum(ti_ref[lev + 1, i], axis=0, keepdims=True) for i in range(2))
        sens_ref[lev] = jnp.concatenate([e0, i1, i2, e3], 0) * live
        return 0

    lax.fori_loop(0, n_lev, reduce, 0, unroll=UNROLL)


def hand_out(pieces, f_ref, a_ref, f_hbm, a_hbm, sems):
    size = f_ref.shape[0] // pieces
    copies = [
        pltpu.make_async_copy(ref.at[pl.ds(j * size, size), :], hbm.at[pl.ds(j * size, size), :], sems.at[2 * j + k])
        for j in range(pieces)
        for k, (ref, hbm) in enumerate(((f_ref, f_hbm), (a_ref, a_hbm)))
    ]
    for copy in copies:
        copy.start()
    for copy in copies:
        copy.wait()


def vmem(*shape):
    return pltpu.VMEM(shape, F32)


def where_am_i(n_pair):
    place, count = lax.axis_index("horiz"), lax.axis_size("horiz")
    return (
        lax.axis_index("level"),
        jnp.where(place == count - 1, 1, 0),
        jnp.where(place == 0, 1, 0),
        lax.axis_index("tracer") * n_pair,
        lax.rem(place, 2),
    )


def call(kernel, outs, args, flops, scratch=(), hbm_in=False, hbm_out=0):
    near, far = pl.BlockSpec(memory_space=pltpu.VMEM), pl.BlockSpec(memory_space=pltpu.HBM)
    return pl.pallas_call(
        kernel,
        out_shape=tuple(outs),
        in_specs=[far if hbm_in else near] * len(args),
        out_specs=tuple([far] * hbm_out + [near] * (len(outs) - hbm_out)),
        scratch_shapes=list(scratch),
        compiler_params=pltpu.CompilerParams(vmem_limit_bytes=24 * 2**20),
        cost_estimate=pl.CostEstimate(flops=flops, bytes_accessed=flops // 8, transcendentals=0),
    )(*[pltpu.with_memory_space_constraint(a, pltpu.HBM if hbm_in else pltpu.VMEM) for a in args])


def per_device(forward_init, adjoint_init, east_flow, north_flow, mixing, depth, color, fold):
    n_pair, n_lev, n_rows, n_x = forward_init.shape
    n_all = 2 * n_pair
    count = lax.axis_size("horiz")
    even = [(2 * i + t, 2 * (i ^ 1) + t) for i in range(count) for t in range(2)]
    odd = []
    for i in range(count):
        partner = ((i - 1) ^ 1) + 1 if i > 0 else count
        odd += [(2 * i + t, 2 * partner + t if partner < count else 2 * i + 1 - t) for t in range(2)]
    pairs = ("horiz", "tracer")
    swap = [(0, 1), (1, 0)]
    f2 = forward_init.reshape(n_pair * n_lev * n_rows, n_x)
    a2 = adjoint_init.reshape(n_pair * n_lev * n_rows, n_x)
    fold2 = fold.reshape(1, n_x)
    work = n_lev * n_rows * n_all * n_x

    flat = vmem(n_pair * n_lev * n_rows, n_x)
    to_even, to_odd, f2, a2, north_flow, depth = call(
        functools.partial(send_first, n_lev, n_pair, n_rows),
        [
            vmem(2 * n_lev + 1, n_pair, n_x),
            vmem(2 * n_lev + 1, n_pair, n_x),
            flat,
            flat,
            vmem(n_lev, n_rows, n_x),
            pltpu.VMEM((n_rows, n_x), jnp.int32),
        ],
        [f2, a2, north_flow, depth],
        work,
        [pltpu.SemaphoreType.DMA((2 + n_pair // 2,))],
        hbm_in=True,
    )
    from_odd = lax.ppermute(to_odd, pairs, odd)
    from_even = lax.ppermute(to_even, pairs, even)
    state = vmem(n_lev, 2, n_all, n_x)
    halo = vmem(n_lev, n_pair, n_x)
    acc = vmem(n_lev + 1, 2, 8, n_x)
    xe, pi, be, c, wx, hot, mf = call(
        functools.partial(prepare, n_lev, n_pair, n_rows),
        [state] * 3 + [vmem(13, n_lev, n_rows, n_x), vmem(3, n_rows, n_x), vmem(n_rows, n_pair, n_x), halo],
        [f2, a2, east_flow, north_flow, mixing, depth, color, fold2],
        work * 10,
        [vmem(n_lev, n_rows, n_x), state],
    )
    edges = vmem(n_rows, n_all, n_x)
    acce = acci = None
    for step in range(STEPS):
        if step == 0:
            pe, edge, ec, fs = call(
                functools.partial(edge_sweep, True, n_lev, n_pair),
                [state, edges, vmem(8, n_lev, 8, n_x), vmem(n_lev, 8, n_x)],
                [be, pi, c, mf, from_even, from_odd, xe, north_flow, depth, fold2],
                work * 3,
            )
        else:
            pe, edge = call(
                functools.partial(edge_sweep, False, n_lev, n_pair),
                [state, edges],
                [be, pi, c, mf, from_even, from_odd, ec],
                work * 2,
            )
        far = lax.ppermute(edge, "level", swap)
        if step == STEPS - 1:
            break
        more = [] if step == 0 else [acce]
        xe, to_even, to_odd, acce = call(
            functools.partial(edge_back, step == 0, n_lev, n_pair),
            [state, halo, halo, acc],
            [pe, far, c, wx, north_flow, fs] + more,
            work * 2,
        )
        from_odd = lax.ppermute(to_odd, pairs, odd)
        from_even = lax.ppermute(to_even, pairs, even)
        more = [] if step == 0 else [acci]
        pi, be, mf, acci = call(
            functools.partial(inner, step == 0, n_lev, n_pair),
            [state, state, halo, acc],
            [pi, far, c, ec, wx, north_flow, fold2, hot, xe] + more,
            work * 9,
            [state],
        )
    f_flat, a_flat, sens = call(
        functools.partial(finish, n_lev, n_pair, n_rows),
        [flat, flat, vmem(n_lev, n_rows, n_x)],
        [pe, pi, far, c, wx, depth, acce, acci],
        work * 4,
        [acc, acc],
    )
    out = jax.ShapeDtypeStruct(f_flat.shape, F32)
    f_out, a_out = call(
        functools.partial(hand_out, PIECES),
        [out, out],
        [f_flat, a_flat],
        work * 4,
        [pltpu.SemaphoreType.DMA((2 * PIECES,))],
        hbm_out=2,
    )
    sens = sens + lax.ppermute(sens, "tracer", swap)
    return f_out.reshape(forward_init.shape), a_out.reshape(adjoint_init.shape), sens


def solution(mesh):
    tracers, flows = P("tracer", "level", "horiz", None), P("level", "horiz", None)
    return jax.shard_map(
        per_device,
        mesh=mesh,
        in_specs=(tracers, tracers, flows, flows, P(None, "horiz", None), P("horiz", None), P("horiz", None), P()),
        out_specs=(tracers, tracers, flows),
        check_vma=False,
    )
```

```python
import functools
import jax
import jax.numpy as jnp
from jax import lax
from jax.experimental import pallas as pl
from jax.experimental.pallas import tpu as pltpu
from jax.sharding import PartitionSpec as P

STEPS = 4
LANES = 128
C0F, C0A, CWF, CWA, CEF, CEA, CSF, CSA, CNF, CNA, UP, WI, BACK = range(13)
E0F, E0A, ESF, ESA, T0F, T0A, TNF, TNA = range(8)
F32 = jnp.float32
UNROLL = 8


def order(flags, n_lev):
    bottom = flags[0]
    return bottom * (n_lev - 1), 1 - 2 * bottom


def west(v):
    return pltpu.roll(v, 1, 1)


def east(v):
    return pltpu.roll(v, LANES - 1, 1)


def spread(v):
    return jnp.broadcast_to(v, (8, LANES))


def pick(c_ref, which, lev, row):
    return spread(c_ref[which, lev, row : row + 1, :])


def sweep(flags, n_lev, n_pair, rows, put, last):
    k0, dk = order(flags, n_lev)
    halves = n_pair // 8
    zero = jnp.zeros((8, LANES), F32)

    def body(s, carry):
        lev = k0 + dk * s
        out = []
        for i, (up, explicit, swept) in enumerate(rows):
            values = explicit(lev)
            factor = up(lev) if swept else None
            for kind in range(2):
                for g in range(halves):
                    v = values[kind][g]
                    if swept:
                        v = v + factor * carry[len(out)]
                        out.append(v)
                    put(lev, i, kind, g, v)
        return tuple(out)

    n_swept = sum(row[2] for row in rows)
    final = lax.fori_loop(0, n_lev, body, (zero,) * (n_swept * 2 * halves), unroll=UNROLL)
    for at, v in enumerate(final):
        last(at // (2 * halves), at // halves % 2, at % halves, v)


def own_part(n_pair, coef, src, center, sides):
    halves = n_pair // 8

    def explicit(lev):
        wi = coef(WI, lev)
        srcs = [src(g) * wi for g in range(halves)]
        out = []
        for kind in range(2):
            c0, cw, ce = (coef(base + kind, lev) for base in (C0F, CWF, CEF))
            cs = [coef(base + kind, lev) for base, _ in sides]
            vs = []
            for g in range(halves):
                c = center(lev, kind, g)
                v = (c0 * c + srcs[g]) + (cw * west(c) + ce * east(c))
                for k, (_, side) in zip(cs, sides):
                    v = v + k * side(lev, kind, g)
                vs.append(v)
            out.append(vs)
        return out

    return explicit


def back(flags, n_lev, n_pair, rows, wx_ref, far_ref, c_ref, part, put, acc_in, acc_out):
    bottom = flags[0]
    k0, dk = order(flags, n_lev)
    halves = n_pair // 8
    mid = k0 + dk * (n_lev - 1)
    own, far = [], []
    for i, row in enumerate(rows):
        wa, wb, ff = (spread(wx_ref[j, row : row + 1, :]) for j in range(3))
        for kind in range(2):
            for g in range(halves):
                p_far = far_ref[row, pl.ds((kind * halves + g) * 8, 8), :]
                x = wa * part(mid, i, kind, g) + wb * p_far
                own.append(x)
                far.append(p_far + ff * x)

    def tally(s, now, nxt):
        at = jnp.where(bottom == 0, s + 1, n_lev - 1 - s)
        for i in range(len(rows)):
            b = i * 2 * halves
            total = acc_in(at, i)
            for g in range(halves):
                f, a = b + g, b + halves + g
                total = total + (nxt[f] - now[f]) * (nxt[a] - now[a])
            acc_out(at, i, total)

    def store(lev, xs):
        at = 0
        for i in range(len(rows)):
            for kind in range(2):
                for g in range(halves):
                    put(lev, i, kind, g, xs[at])
                    at += 1

    tally(n_lev - 1, own, far)
    store(mid, own)

    def body(q, nxt):
        s = n_lev - 2 - q
        lev = k0 + dk * s
        now = []
        at = 0
        for i, row in enumerate(rows):
            f = pick(c_ref, BACK, lev, row)
            for kind in range(2):
                for g in range(halves):
                    now.append(part(lev, i, kind, g) + f * nxt[at])
                    at += 1
        tally(s, now, nxt)
        store(lev, now)
        return tuple(now)

    lax.fori_loop(0, n_lev - 1, body, tuple(own), unroll=UNROLL)


def fold_rows(flags, fold_ref, nf_ref, get, mf_ref, n_lev, n_pair):
    @pl.when(flags[1] == 1)
    def _():
        where_to = spread(fold_ref[0:1, :])

        def body(lev, _):
            n3 = spread(nf_ref[lev, 3:4, :])
            for g in range(n_pair // 8):
                f = jnp.take_along_axis(get(lev, 0, g), where_to, axis=1)
                a = jnp.take_along_axis(get(lev, 1, g), where_to, axis=1)
                mf_ref[lev, pl.ds(g * 8, 8), :] = jnp.where(n3 < 0.0, f, a)
            return 0

        lax.fori_loop(0, n_lev, body, 0, unroll=4)


def rows_at(ref, row, lev, kind, g, halves):
    return ref[lev, row, pl.ds((kind * halves + g) * 8, 8), :]


def send_first(
    n_lev, n_pair, n_rows, f_hbm, a_hbm, nf_hbm, depth_hbm, even_ref, odd_ref, f_ref, a_ref, nf_ref, depth_ref, sems
):
    stride = n_lev * n_rows
    part = 4 * stride
    first = lax.axis_index("level") * n_lev
    small = [
        pltpu.make_async_copy(nf_hbm, nf_ref, sems.at[0]),
        pltpu.make_async_copy(depth_hbm, depth_ref, sems.at[1]),
    ]
    large = [
        [
            pltpu.make_async_copy(
                hbm.at[pl.ds(j * part, part), :], to.at[pl.ds(j * part, part), :], sems.at[2 + 2 * j + i]
            )
            for i, (hbm, to) in enumerate(((f_hbm, f_ref), (a_hbm, a_ref)))
        ]
        for j in range(n_pair // 4)
    ]
    for copy in small:
        copy.start()
    for pair in large:
        for copy in pair:
            copy.start()
    for copy in small:
        copy.wait()
    depth = depth_ref[...]
    up_even = lax.rem(lax.axis_index("horiz"), 2) == 0
    high = depth[n_rows - 1 : n_rows].astype(F32)
    low = depth[0:1].astype(F32)
    even_ref[2 * n_lev] = jnp.broadcast_to(jnp.where(up_even, high, low), (n_pair, LANES))
    odd_ref[2 * n_lev] = jnp.broadcast_to(jnp.where(up_even, low, high), (n_pair, LANES))
    for g in range(n_pair // 8):
        for pair in large[2 * g : 2 * g + 2]:
            for copy in pair:
                copy.wait()

        def body(lev, _, g=g):
            wet = jnp.where(first + lev < depth, 1.0, 0.0)
            w0 = spread(wet[0:1])
            w3 = spread(wet[n_rows - 1 : n_rows])
            n3 = spread(nf_ref[lev, n_rows - 1 : n_rows, :])
            at = g * 8 * stride + lev * n_rows
            low, high = pl.ds(at, 8, stride=stride), pl.ds(at + n_rows - 1, 8, stride=stride)
            to = pl.ds(g * 8, 8)
            north = jnp.where(n3 > 0.0, f_ref[high, :], a_ref[high, :]) * w3
            south = f_ref[low, :] * w0
            even_ref[lev, to, :] = jnp.where(up_even, north, south)
            odd_ref[lev, to, :] = jnp.where(up_even, south, north)
            south = a_ref[low, :] * w0
            even_ref[n_lev + lev, to, :] = south
            odd_ref[n_lev + lev, to, :] = south
            return 0

        lax.fori_loop(0, n_lev, body, 0, unroll=UNROLL)

    def flow(ref):
        for lev in range(n_lev):
            page, line = n_lev + lev // n_pair, lev % n_pair
            ref[page, line : line + 1, :] = nf_ref[lev, n_rows - 1 : n_rows, :]

    pl.when(up_even)(lambda: flow(even_ref))
    pl.when(jnp.logical_not(up_even))(lambda: flow(odd_ref))


def prepare(
    n_lev, n_pair, n_rows, f_ref, a_ref, ef_ref, nf_ref, mix_ref, depth_ref, color_ref, fold_ref,
    xe_ref, pi_ref, be_ref, c_ref, wx_ref, hot_ref, mf_ref, inv_ref, xi_ref,
):
    flags = where_am_i(n_pair)
    halves = n_pair // 8
    stride = n_lev * n_rows
    bottom = flags[0]
    first = bottom * n_lev
    k0, dk = order(flags, n_lev)
    depth = depth_ref[...]

    def lay(lev, _):
        wet = jnp.where(first + lev < depth, 1.0, 0.0)
        for row in range(n_rows):
            w = spread(wet[row : row + 1])
            to_ref, line = (xe_ref, row // 3) if row in (0, 3) else (xi_ref, row - 1)
            for kind, from_ref in enumerate((f_ref, a_ref)):
                for g in range(halves):
                    v = from_ref[pl.ds(g * 8 * stride + lev * n_rows + row, 8, stride=stride), :]
                    to_ref[lev, line, pl.ds((kind * halves + g) * 8, 8), :] = v * w
        return 0

    lax.fori_loop(0, n_lev, lay, 0, unroll=UNROLL)

    def coupling(k):
        inner = jnp.where((k >= 0) & (k < 2 * n_lev - 1), 1.0, 0.0)
        m = mix_ref[jnp.clip(k, 0, 2 * n_lev - 2)]
        return m * jnp.where(k + 1 < depth, inner, 0.0)

    def eliminate(s, carry):
        own_f, far_f = carry
        k = bottom * (2 * n_lev - 1) + dk * s
        prev, nxt = coupling(k - 1 + bottom), coupling(k - bottom)
        inverse = 1.0 / (1.0 + nxt + prev * (1.0 - own_f))
        lev = k0 + dk * s
        inv_ref[lev] = inverse
        c_ref[UP, lev] = prev * inverse
        own_f = nxt * inverse
        c_ref[BACK, lev] = own_f
        k = (1 - bottom) * (2 * n_lev - 1) - dk * s
        prev, nxt = coupling(k - bottom), coupling(k - 1 + bottom)
        far_f = nxt / (1.0 + nxt + prev * (1.0 - far_f))
        return own_f, far_f

    one = jnp.zeros((n_rows, LANES), F32)
    own_f, far_f = lax.fori_loop(0, n_lev, eliminate, (one, one), unroll=UNROLL)
    meet = 1.0 / (1.0 - own_f * far_f)
    wx_ref[0] = meet
    wx_ref[1] = own_f * meet
    wx_ref[2] = far_f

    depth_east = east(depth)
    depth_north = jnp.concatenate([depth[1:], jnp.zeros((1, LANES), jnp.int32)], 0)

    def coefs(lev, _):
        k = first + lev
        wet = jnp.where(k < depth, 1.0, 0.0)
        inverse = inv_ref[lev]
        e = ef_ref[lev] * wet * jnp.where(k < depth_east, 1.0, 0.0)
        n = nf_ref[lev] * wet * jnp.where(k < depth_north, 1.0, 0.0)
        w = west(e)
        s = jnp.concatenate([jnp.zeros((1, LANES), F32), n[:-1]], 0)
        plus = [jnp.maximum(v, 0.0) for v in (w, e, s, n)]
        minus = [jnp.maximum(-v, 0.0) for v in (w, e, s, n)]
        c_ref[C0F, lev] = (1.0 - minus[0] - plus[1] - minus[2] - plus[3]) * inverse
        c_ref[C0A, lev] = (1.0 - plus[0] - minus[1] - plus[2] - minus[3]) * inverse
        c_ref[CWF, lev], c_ref[CWA, lev] = plus[0] * inverse, minus[0] * inverse
        c_ref[CEF, lev], c_ref[CEA, lev] = minus[1] * inverse, plus[1] * inverse
        c_ref[CSF, lev], c_ref[CSA, lev] = plus[2] * inverse, minus[2] * inverse
        c_ref[CNF, lev], c_ref[CNA, lev] = minus[3] * inverse, plus[3] * inverse
        c_ref[WI, lev] = wet * inverse
        return 0

    lax.fori_loop(0, n_lev, coefs, 0, unroll=UNROLL)

    ids = lax.broadcasted_iota(jnp.int32, (n_pair, LANES), 0) + flags[3]
    for row in range(n_rows):
        hot_ref[row] = jnp.where(color_ref[row : row + 1, :] == ids, 1.0, 0.0)

    inner_sweep(n_lev, n_pair, flags, xe_ref, xi_ref, c_ref, None, hot_ref, pi_ref, be_ref)
    fold_rows(
        flags, fold_ref, nf_ref, lambda lev, kind, g: rows_at(xe_ref, 1, lev, kind, g, halves), mf_ref, n_lev, n_pair
    )


def inner_sweep(n_lev, n_pair, flags, xe_ref, xi_ref, c_ref, ec_ref, hot_ref, pi_ref, be_ref):
    halves = n_pair // 8

    def at(ref, line):
        return lambda lev, kind, g: rows_at(ref, line, lev, kind, g, halves)

    x = [at(xe_ref, 0), at(xi_ref, 0), at(xi_ref, 1), at(xe_ref, 1)]

    def row(number):
        edge = {0: {C0F: E0F, C0A: E0A}, 3: {C0F: T0F, C0A: T0A}}.get(number, {}) if ec_ref is not None else {}

        def coef(which, lev):
            return ec_ref[edge[which], lev] if which in edge else pick(c_ref, which, lev, number)

        sides = []
        if number > 0:
            sides.append((CSF, x[number - 1]))
        if number < 3:
            sides.append((CNF, x[number + 1]))
        explicit = own_part(n_pair, coef, lambda g: hot_ref[number, pl.ds(g * 8, 8), :], x[number], sides)
        return lambda lev: coef(UP, lev), explicit, number in (1, 2)

    def put(lev, i, kind, g, v):
        to, line = (pi_ref, i) if i < 2 else (be_ref, i - 2)
        to[lev, line, pl.ds((kind * halves + g) * 8, 8), :] = v

    sweep(flags, n_lev, n_pair, [row(1), row(2), row(0), row(3)], put, lambda *_: None)


def edge_sweep(is_first, n_lev, n_pair, be_ref, pi_ref, c_ref, mf_ref, even_ref, odd_ref, *rest):
    flags = where_am_i(n_pair)
    halves = n_pair // 8
    is_top = flags[1] == 1
    up_even = flags[4] == 0

    def from_south(*at):
        return jnp.where(up_even, odd_ref[at], even_ref[at])

    def from_north(*at):
        return jnp.where(up_even, even_ref[at], odd_ref[at])

    if is_first:
        xe_ref, nf_ref, depth_ref, fold_ref, pe_ref, edge_ref, ec_ref, fs_ref = rest
        first = flags[0] * n_lev
        depth = depth_ref[...]
        own3 = depth[3:4]
        south_depth = from_south(2 * n_lev, slice(0, 1), slice(None))
        folded = jnp.take_along_axis(spread(own3.astype(F32)), spread(fold_ref[0:1, :]), axis=1)[0:1]
        north_depth = jnp.where(is_top, folded, from_north(2 * n_lev, slice(0, 1), slice(None)))
        open_south = jnp.where(flags[2] == 1, 0.0, 1.0)
        for lev in range(n_lev):
            k = first + lev
            kf = k.astype(F32)
            line = lev % n_pair
            raw = from_south(n_lev + lev // n_pair, slice(line, line + 1), slice(None))
            fs_ref[lev] = spread(raw)
            wi0, wi3 = c_ref[WI, lev, 0:1, :], c_ref[WI, lev, 3:4, :]
            s = raw * jnp.where(kf < south_depth, 1.0, 0.0) * open_south * wi0
            n = nf_ref[lev, 3:4, :] * jnp.where(kf < north_depth, 1.0, 0.0) * wi3
            sp, sm, np_, nm = (jnp.maximum(v, 0.0) for v in (s, -s, n, -n))
            ec_ref[E0F, lev] = spread(c_ref[C0F, lev, 0:1, :] - sm)
            ec_ref[E0A, lev] = spread(c_ref[C0A, lev, 0:1, :] - sp)
            ec_ref[ESF, lev] = spread(sp)
            ec_ref[ESA, lev] = spread(sm)
            ec_ref[T0F, lev] = spread(c_ref[C0F, lev, 3:4, :] - np_)
            ec_ref[T0A, lev] = spread(c_ref[C0A, lev, 3:4, :] - nm)
            ec_ref[TNF, lev] = spread(nm)
            ec_ref[TNA, lev] = spread(np_)
    else:
        ec_ref, pe_ref, edge_ref = rest

    def come_north(lev, g):
        to = pl.ds(g * 8, 8)
        if is_first:
            n3 = spread(nf_ref[lev, 3:4, :])
            come = jnp.where(n3 < 0.0, from_north(lev, to, slice(None)), from_north(n_lev + lev, to, slice(None)))
        else:
            come = from_north(lev, to, slice(None))
        return jnp.where(is_top, mf_ref[lev, to, :], come)

    def row(i, number, inflow, come):
        def explicit(lev):
            ks = [ec_ref[inflow + kind, lev] for kind in range(2)]
            ms = [come(lev, g) for g in range(halves)]
            out = []
            for kind in range(2):
                vs = []
                for g in range(halves):
                    v = rows_at(be_ref, i, lev, kind, g, halves) + ks[kind] * ms[g]
                    if is_first:
                        v = v - ks[1 - kind] * rows_at(xe_ref, i, lev, kind, g, halves)
                    vs.append(v)
                out.append(vs)
            return out

        return lambda lev: pick(c_ref, UP, lev, number), explicit, True

    def put(lev, i, kind, g, v):
        pe_ref[lev, i, pl.ds((kind * halves + g) * 8, 8), :] = v

    def last(i, kind, g, v):
        edge_ref[3 * i, pl.ds((kind * halves + g) * 8, 8), :] = v

    rows = [row(0, 0, ESF, lambda lev, g: from_south(lev, pl.ds(g * 8, 8), slice(None))), row(1, 3, TNF, come_north)]
    sweep(flags, n_lev, n_pair, rows, put, last)
    k0, dk = order(flags, n_lev)
    mid = k0 + dk * (n_lev - 1)
    edge_ref[1] = pi_ref[mid, 0]
    edge_ref[2] = pi_ref[mid, 1]


def tallies(is_first, in_ref, out_ref, n_lev):
    if is_first:
        out_ref[0] = jnp.zeros(out_ref.shape[1:], F32)
        out_ref[n_lev] = jnp.zeros(out_ref.shape[1:], F32)
    else:
        out_ref[0] = in_ref[0]
        out_ref[n_lev] = in_ref[n_lev]
    zero = jnp.zeros((8, LANES), F32)

    def put(at, i, v):
        out_ref[at, i] = v

    return (lambda at, i: zero) if is_first else (lambda at, i: in_ref[at, i]), put


def edge_back(is_first, n_lev, n_pair, pe_ref, far_ref, c_ref, wx_ref, nf_ref, fs_ref, *rest):
    flags = where_am_i(n_pair)
    halves = n_pair // 8
    acc_ref, (xe_ref, even_ref, odd_ref, out_ref) = (None, rest) if is_first else (rest[0], rest[1:])
    acc_in, acc_out = tallies(is_first, acc_ref, out_ref, n_lev)
    held, south = {}, {}
    up_even = flags[4] == 0

    def put(lev, i, kind, g, v):
        xe_ref[lev, i, pl.ds((kind * halves + g) * 8, 8), :] = v
        if kind == 0:
            held[i, g] = v
        elif i == 0:
            south[g] = jnp.where(fs_ref[lev] < 0.0, held[i, g], v)
        else:
            n3 = spread(nf_ref[lev, 3:4, :])
            north = jnp.where(n3 > 0.0, held[i, g], v)
            even_ref[lev, pl.ds(g * 8, 8), :] = jnp.where(up_even, north, south[g])
            odd_ref[lev, pl.ds(g * 8, 8), :] = jnp.where(up_even, south[g], north)

    back(
        flags, n_lev, n_pair, (0, 3), wx_ref, far_ref, c_ref,
        lambda lev, i, kind, g: rows_at(pe_ref, i, lev, kind, g, halves), put, acc_in, acc_out,
    )


def inner(
    is_first, n_lev, n_pair, pi_ref, far_ref, c_ref, ec_ref, wx_ref, nf_ref, fold_ref, hot_ref, xe_ref, *rest
):
    flags = where_am_i(n_pair)
    halves = n_pair // 8
    acc_ref, (pn_ref, be_ref, mf_ref, out_ref, xi_ref) = (None, rest) if is_first else (rest[0], rest[1:])
    acc_in, acc_out = tallies(is_first, acc_ref, out_ref, n_lev)

    def put(lev, i, kind, g, v):
        xi_ref[lev, i, pl.ds((kind * halves + g) * 8, 8), :] = v

    back(
        flags, n_lev, n_pair, (1, 2), wx_ref, far_ref, c_ref,
        lambda lev, i, kind, g: rows_at(pi_ref, i, lev, kind, g, halves), put, acc_in, acc_out,
    )
    inner_sweep(n_lev, n_pair, flags, xe_ref, xi_ref, c_ref, ec_ref, hot_ref, pn_ref, be_ref)
    fold_rows(
        flags, fold_ref, nf_ref, lambda lev, kind, g: rows_at(xe_ref, 1, lev, kind, g, halves), mf_ref, n_lev, n_pair
    )


def finish(
    n_lev, n_pair, n_rows, pe_ref, pi_ref, far_ref, c_ref, wx_ref, depth_ref, acce_ref, acci_ref,
    x_ref, sens_ref, te_ref, ti_ref,
):
    flags = where_am_i(n_pair)
    halves = n_pair // 8
    ps = [(pe_ref, 0), (pi_ref, 0), (pi_ref, 1), (pe_ref, 1)]
    e_in, e_out = tallies(False, acce_ref, te_ref, n_lev)
    i_in, i_out = tallies(False, acci_ref, ti_ref, n_lev)

    def put(lev, i, kind, g, v):
        x_ref[lev * n_rows + i, pl.ds((kind * halves + g) * 8, 8), :] = v

    back(
        flags, n_lev, n_pair, range(4), wx_ref, far_ref, c_ref,
        lambda lev, i, kind, g: rows_at(ps[i][0], ps[i][1], lev, kind, g, halves), put,
        lambda at, i: e_in(at, i // 3) if i in (0, 3) else i_in(at, i - 1),
        lambda at, i, v: e_out(at, i // 3, v) if i in (0, 3) else i_out(at, i - 1, v),
    )
    first = flags[0] * n_lev
    depth = depth_ref[...]

    def reduce(lev, _):
        k = first + lev
        live = jnp.where((k + 1 < depth) & (k + 1 < 2 * n_lev), 1.0 / STEPS, 0.0)
        e0, e3 = (jnp.sum(te_ref[lev + 1, i], axis=0, keepdims=True) for i in range(2))
        i1, i2 = (jnp.sum(ti_ref[lev + 1, i], axis=0, keepdims=True) for i in range(2))
        sens_ref[lev] = jnp.concatenate([e0, i1, i2, e3], 0) * live
        return 0

    lax.fori_loop(0, n_lev, reduce, 0, unroll=UNROLL)


def hand_out(n_pair, x_ref, f_hbm, a_hbm, sems):
    copies = [
        pltpu.make_async_copy(x_ref.at[:, kind * n_pair + j, :], hbm.at[j], sems.at[kind * n_pair + j])
        for j in range(n_pair)
        for kind, hbm in enumerate((f_hbm, a_hbm))
    ]
    for copy in copies:
        copy.start()
    for copy in copies:
        copy.wait()


def vmem(*shape):
    return pltpu.VMEM(shape, F32)


def where_am_i(n_pair):
    place, count = lax.axis_index("horiz"), lax.axis_size("horiz")
    return (
        lax.axis_index("level"),
        jnp.where(place == count - 1, 1, 0),
        jnp.where(place == 0, 1, 0),
        lax.axis_index("tracer") * n_pair,
        lax.rem(place, 2),
    )


def call(kernel, outs, args, flops, scratch=(), hbm_in=False, hbm_out=0):
    near, far = pl.BlockSpec(memory_space=pltpu.VMEM), pl.BlockSpec(memory_space=pltpu.HBM)
    return pl.pallas_call(
        kernel,
        out_shape=tuple(outs),
        in_specs=[far if hbm_in else near] * len(args),
        out_specs=tuple([far] * hbm_out + [near] * (len(outs) - hbm_out)),
        scratch_shapes=list(scratch),
        compiler_params=pltpu.CompilerParams(vmem_limit_bytes=24 * 2**20),
        cost_estimate=pl.CostEstimate(flops=flops, bytes_accessed=flops // 8, transcendentals=0),
    )(*[pltpu.with_memory_space_constraint(a, pltpu.HBM if hbm_in else pltpu.VMEM) for a in args])


def per_device(forward_init, adjoint_init, east_flow, north_flow, mixing, depth, color, fold):
    n_pair, n_lev, n_rows, n_x = forward_init.shape
    n_all = 2 * n_pair
    count = lax.axis_size("horiz")
    even = [(2 * i + t, 2 * (i ^ 1) + t) for i in range(count) for t in range(2)]
    odd = []
    for i in range(count):
        partner = ((i - 1) ^ 1) + 1 if i > 0 else count
        odd += [(2 * i + t, 2 * partner + t if partner < count else 2 * i + 1 - t) for t in range(2)]
    pairs = ("horiz", "tracer")
    swap = [(0, 1), (1, 0)]
    f2 = forward_init.reshape(n_pair * n_lev * n_rows, n_x)
    a2 = adjoint_init.reshape(n_pair * n_lev * n_rows, n_x)
    fold2 = fold.reshape(1, n_x)
    work = n_lev * n_rows * n_all * n_x

    flat = vmem(n_pair * n_lev * n_rows, n_x)
    to_even, to_odd, f2, a2, north_flow, depth = call(
        functools.partial(send_first, n_lev, n_pair, n_rows),
        [
            vmem(2 * n_lev + 1, n_pair, n_x),
            vmem(2 * n_lev + 1, n_pair, n_x),
            flat,
            flat,
            vmem(n_lev, n_rows, n_x),
            pltpu.VMEM((n_rows, n_x), jnp.int32),
        ],
        [f2, a2, north_flow, depth],
        work,
        [pltpu.SemaphoreType.DMA((2 + n_pair // 2,))],
        hbm_in=True,
    )
    from_odd = lax.ppermute(to_odd, pairs, odd)
    from_even = lax.ppermute(to_even, pairs, even)
    state = vmem(n_lev, 2, n_all, n_x)
    halo = vmem(n_lev, n_pair, n_x)
    acc = vmem(n_lev + 1, 2, 8, n_x)
    xe, pi, be, c, wx, hot, mf = call(
        functools.partial(prepare, n_lev, n_pair, n_rows),
        [state] * 3 + [vmem(13, n_lev, n_rows, n_x), vmem(3, n_rows, n_x), vmem(n_rows, n_pair, n_x), halo],
        [f2, a2, east_flow, north_flow, mixing, depth, color, fold2],
        work * 10,
        [vmem(n_lev, n_rows, n_x), state],
    )
    edges = vmem(n_rows, n_all, n_x)
    acce = acci = None
    for step in range(STEPS):
        if step == 0:
            pe, edge, ec, fs = call(
                functools.partial(edge_sweep, True, n_lev, n_pair),
                [state, edges, vmem(8, n_lev, 8, n_x), vmem(n_lev, 8, n_x)],
                [be, pi, c, mf, from_even, from_odd, xe, north_flow, depth, fold2],
                work * 3,
            )
        else:
            pe, edge = call(
                functools.partial(edge_sweep, False, n_lev, n_pair),
                [state, edges],
                [be, pi, c, mf, from_even, from_odd, ec],
                work * 2,
            )
        far = lax.ppermute(edge, "level", swap)
        if step == STEPS - 1:
            break
        more = [] if step == 0 else [acce]
        xe, to_even, to_odd, acce = call(
            functools.partial(edge_back, step == 0, n_lev, n_pair),
            [state, halo, halo, acc],
            [pe, far, c, wx, north_flow, fs] + more,
            work * 2,
        )
        from_odd = lax.ppermute(to_odd, pairs, odd)
        from_even = lax.ppermute(to_even, pairs, even)
        more = [] if step == 0 else [acci]
        pi, be, mf, acci = call(
            functools.partial(inner, step == 0, n_lev, n_pair),
            [state, state, halo, acc],
            [pi, far, c, ec, wx, north_flow, fold2, hot, xe] + more,
            work * 9,
            [state],
        )
    x, sens = call(
        functools.partial(finish, n_lev, n_pair, n_rows),
        [vmem(n_lev * n_rows, n_all, n_x), vmem(n_lev, n_rows, n_x)],
        [pe, pi, far, c, wx, depth, acce, acci],
        work * 4,
        [acc, acc],
    )
    out = jax.ShapeDtypeStruct((n_pair, n_lev * n_rows, n_x), F32)
    f_out, a_out = call(
        functools.partial(hand_out, n_pair),
        [out, out],
        [x],
        work * 4,
        [pltpu.SemaphoreType.DMA((n_all,))],
        hbm_out=2,
    )
    sens = sens + lax.ppermute(sens, "tracer", swap)
    return f_out.reshape(forward_init.shape), a_out.reshape(adjoint_init.shape), sens


def solution(mesh):
    tracers, flows = P("tracer", "level", "horiz", None), P("level", "horiz", None)
    return jax.shard_map(
        per_device,
        mesh=mesh,
        in_specs=(tracers, tracers, flows, flows, P(None, "horiz", None), P("horiz", None), P("horiz", None), P()),
        out_specs=(tracers, tracers, flows),
        check_vma=False,
    )
```

```python
import functools
import jax
import jax.numpy as jnp
from jax import lax
from jax.experimental import pallas as pl
from jax.experimental.pallas import tpu as pltpu
from jax.sharding import PartitionSpec as P

STEPS = 4
LANES = 128
C0F, C0A, CWF, CWA, CEF, CEA, CSF, CSA, CNF, CNA, UP, WI, BACK = range(13)
E0F, E0A, ESF, ESA, T0F, T0A, TNF, TNA = range(8)
F32 = jnp.float32
UNROLL = 8


def order(flags, n_lev):
    bottom = flags[0]
    return bottom * (n_lev - 1), 1 - 2 * bottom


def west(v):
    return pltpu.roll(v, 1, 1)


def east(v):
    return pltpu.roll(v, LANES - 1, 1)


def spread(v):
    return jnp.broadcast_to(v, (8, LANES))


def pick(c_ref, which, lev, row):
    return spread(c_ref[which, lev, row : row + 1, :])


def sweep(flags, n_lev, n_pair, rows, put, last):
    k0, dk = order(flags, n_lev)
    halves = n_pair // 8
    zero = jnp.zeros((8, LANES), F32)

    def body(s, carry):
        lev = k0 + dk * s
        out = []
        for i, (up, explicit, swept) in enumerate(rows):
            values = explicit(lev)
            factor = up(lev) if swept else None
            for kind in range(2):
                for g in range(halves):
                    v = values[kind][g]
                    if swept:
                        v = v + factor * carry[len(out)]
                        out.append(v)
                    put(lev, i, kind, g, v)
        return tuple(out)

    n_swept = sum(row[2] for row in rows)
    final = lax.fori_loop(0, n_lev, body, (zero,) * (n_swept * 2 * halves), unroll=UNROLL)
    for at, v in enumerate(final):
        last(at // (2 * halves), at // halves % 2, at % halves, v)


def own_part(n_pair, coef, src, center, sides):
    halves = n_pair // 8

    def explicit(lev):
        wi = coef(WI, lev)
        srcs = [src(g) * wi for g in range(halves)]
        out = []
        for kind in range(2):
            c0, cw, ce = (coef(base + kind, lev) for base in (C0F, CWF, CEF))
            cs = [coef(base + kind, lev) for base, _ in sides]
            vs = []
            for g in range(halves):
                c = center(lev, kind, g)
                v = (c0 * c + srcs[g]) + (cw * west(c) + ce * east(c))
                for k, (_, side) in zip(cs, sides):
                    v = v + k * side(lev, kind, g)
                vs.append(v)
            out.append(vs)
        return out

    return explicit


def back(flags, n_lev, n_pair, rows, wx_ref, far, c_ref, part, put, acc_in, acc_out):
    bottom = flags[0]
    k0, dk = order(flags, n_lev)
    halves = n_pair // 8
    mid = k0 + dk * (n_lev - 1)
    own, beyond = [], []
    for i, row in enumerate(rows):
        wa, wb, ff = (spread(wx_ref[j, row : row + 1, :]) for j in range(3))
        for kind in range(2):
            for g in range(halves):
                p_far = far(i, row, pl.ds((kind * halves + g) * 8, 8))
                x = wa * part(mid, i, kind, g) + wb * p_far
                own.append(x)
                beyond.append(p_far + ff * x)

    def tally(s, now, nxt):
        at = jnp.where(bottom == 0, s + 1, n_lev - 1 - s)
        for i in range(len(rows)):
            b = i * 2 * halves
            total = acc_in(at, i)
            for g in range(halves):
                f, a = b + g, b + halves + g
                total = total + (nxt[f] - now[f]) * (nxt[a] - now[a])
            acc_out(at, i, total)

    def store(lev, xs):
        at = 0
        for i in range(len(rows)):
            for kind in range(2):
                for g in range(halves):
                    put(lev, i, kind, g, xs[at])
                    at += 1

    tally(n_lev - 1, own, beyond)
    store(mid, own)

    def body(q, nxt):
        s = n_lev - 2 - q
        lev = k0 + dk * s
        now = []
        at = 0
        for i, row in enumerate(rows):
            f = pick(c_ref, BACK, lev, row)
            for kind in range(2):
                for g in range(halves):
                    now.append(part(lev, i, kind, g) + f * nxt[at])
                    at += 1
        tally(s, now, nxt)
        store(lev, now)
        return tuple(now)

    lax.fori_loop(0, n_lev - 1, body, tuple(own), unroll=UNROLL)


def fold_rows(flags, fold_ref, nf_ref, get, mf_ref, n_lev, n_pair):
    @pl.when(flags[1] == 1)
    def _():
        where_to = spread(fold_ref[0:1, :])

        def body(lev, _):
            n3 = spread(nf_ref[lev, 3:4, :])
            for g in range(n_pair // 8):
                f = jnp.take_along_axis(get(lev, 0, g), where_to, axis=1)
                a = jnp.take_along_axis(get(lev, 1, g), where_to, axis=1)
                mf_ref[lev, pl.ds(g * 8, 8), :] = jnp.where(n3 < 0.0, f, a)
            return 0

        lax.fori_loop(0, n_lev, body, 0, unroll=4)


def rows_at(ref, row, lev, kind, g, halves):
    return ref[lev, row, pl.ds((kind * halves + g) * 8, 8), :]


def load(n_pair, f_hbm, a_hbm, nf_hbm, depth_hbm, f_ref, a_ref, nf_ref, depth_ref, sems):
    part = f_ref.shape[0] // 4
    copies = [
        pltpu.make_async_copy(nf_hbm, nf_ref, sems.at[0]),
        pltpu.make_async_copy(depth_hbm, depth_ref, sems.at[1]),
    ]
    for j in range(4):
        for i, (hbm, to) in enumerate(((f_hbm, f_ref), (a_hbm, a_ref))):
            at = pl.ds(j * part, part)
            copies.append(pltpu.make_async_copy(hbm.at[at, :], to.at[at, :], sems.at[2 + 2 * j + i]))
    for copy in copies:
        copy.start()
    for copy in copies:
        copy.wait()


def send_first(n_lev, n_pair, n_rows, f_ref, a_ref, nf_ref, depth_ref, flow_ref, even_ref, odd_ref):
    stride = n_lev * n_rows
    first = lax.axis_index("level") * n_lev
    up_even = lax.rem(lax.axis_index("horiz"), 2) == 0
    depth = depth_ref[...]
    low, high = spread(depth[0:1]), spread(depth[n_rows - 1 : n_rows])
    for g in range(n_pair // 8):
        to = pl.ds(g * 8, 8)
        even_ref[n_lev, to, :] = jnp.where(up_even, high, low).astype(F32)
        odd_ref[n_lev, to, :] = jnp.where(up_even, low, high).astype(F32)

    def body(lev, _):
        w0 = jnp.where(first + lev < low, 1.0, 0.0)
        w3 = jnp.where(first + lev < high, 1.0, 0.0)
        n3 = spread(nf_ref[lev, n_rows - 1 : n_rows, :])
        s0 = spread(flow_ref[lev, n_rows - 1 : n_rows, :])
        for g in range(n_pair // 8):
            at = g * 8 * stride + lev * n_rows
            at0, at3 = pl.ds(at, 8, stride=stride), pl.ds(at + n_rows - 1, 8, stride=stride)
            to = pl.ds(g * 8, 8)
            north = jnp.where(n3 > 0.0, f_ref[at3, :], a_ref[at3, :]) * w3
            south = jnp.where(s0 < 0.0, f_ref[at0, :], a_ref[at0, :]) * w0
            even_ref[lev, to, :] = jnp.where(up_even, north, south)
            odd_ref[lev, to, :] = jnp.where(up_even, south, north)
        return 0

    lax.fori_loop(0, n_lev, body, 0, unroll=UNROLL)


def prepare(
    n_lev, n_pair, n_rows, f_ref, a_ref, ef_ref, nf_ref, mix_ref, depth_ref, color_ref, fold_ref,
    mid_ref, xe_ref, pi_ref, be_ref, c_ref, wx_ref, hot_ref, mf_ref, inv_ref, xi_ref,
):
    flags = where_am_i(n_pair)
    halves = n_pair // 8
    stride = n_lev * n_rows
    bottom = flags[0]
    first = bottom * n_lev
    k0, dk = order(flags, n_lev)
    depth = depth_ref[...]

    def lay(lev, _):
        wet = jnp.where(first + lev < depth, 1.0, 0.0)
        for row in range(n_rows):
            w = spread(wet[row : row + 1])
            to_ref, line = (xe_ref, row // 3) if row in (0, 3) else (xi_ref, row - 1)
            for kind, from_ref in enumerate((f_ref, a_ref)):
                for g in range(halves):
                    v = from_ref[pl.ds(g * 8 * stride + lev * n_rows + row, 8, stride=stride), :]
                    to_ref[lev, line, pl.ds((kind * halves + g) * 8, 8), :] = v * w
        return 0

    lax.fori_loop(0, n_lev, lay, 0, unroll=UNROLL)

    def coupling(k):
        inner = jnp.where((k >= 0) & (k < 2 * n_lev - 1), 1.0, 0.0)
        m = mix_ref[jnp.clip(k, 0, 2 * n_lev - 2)]
        return m * jnp.where(k + 1 < depth, inner, 0.0)

    def eliminate(s, carry):
        own_f, far_f = carry
        k = bottom * (2 * n_lev - 1) + dk * s
        prev, nxt = coupling(k - 1 + bottom), coupling(k - bottom)
        inverse = 1.0 / (1.0 + nxt + prev * (1.0 - own_f))
        lev = k0 + dk * s
        inv_ref[lev] = inverse
        c_ref[UP, lev] = prev * inverse
        own_f = nxt * inverse
        c_ref[BACK, lev] = own_f
        k = (1 - bottom) * (2 * n_lev - 1) - dk * s
        prev, nxt = coupling(k - bottom), coupling(k - 1 + bottom)
        far_f = nxt / (1.0 + nxt + prev * (1.0 - far_f))
        return own_f, far_f

    one = jnp.zeros((n_rows, LANES), F32)
    own_f, far_f = lax.fori_loop(0, n_lev, eliminate, (one, one), unroll=UNROLL)
    meet = 1.0 / (1.0 - own_f * far_f)
    wx_ref[0] = meet
    wx_ref[1] = own_f * meet
    wx_ref[2] = far_f

    depth_east = east(depth)
    depth_north = jnp.concatenate([depth[1:], jnp.zeros((1, LANES), jnp.int32)], 0)

    def coefs(lev, _):
        k = first + lev
        wet = jnp.where(k < depth, 1.0, 0.0)
        inverse = inv_ref[lev]
        e = ef_ref[lev] * wet * jnp.where(k < depth_east, 1.0, 0.0)
        n = nf_ref[lev] * wet * jnp.where(k < depth_north, 1.0, 0.0)
        w = west(e)
        s = jnp.concatenate([jnp.zeros((1, LANES), F32), n[:-1]], 0)
        plus = [jnp.maximum(v, 0.0) for v in (w, e, s, n)]
        minus = [jnp.maximum(-v, 0.0) for v in (w, e, s, n)]
        c_ref[C0F, lev] = (1.0 - minus[0] - plus[1] - minus[2] - plus[3]) * inverse
        c_ref[C0A, lev] = (1.0 - plus[0] - minus[1] - plus[2] - minus[3]) * inverse
        c_ref[CWF, lev], c_ref[CWA, lev] = plus[0] * inverse, minus[0] * inverse
        c_ref[CEF, lev], c_ref[CEA, lev] = minus[1] * inverse, plus[1] * inverse
        c_ref[CSF, lev], c_ref[CSA, lev] = plus[2] * inverse, minus[2] * inverse
        c_ref[CNF, lev], c_ref[CNA, lev] = minus[3] * inverse, plus[3] * inverse
        c_ref[WI, lev] = wet * inverse
        return 0

    lax.fori_loop(0, n_lev, coefs, 0, unroll=UNROLL)

    ids = lax.broadcasted_iota(jnp.int32, (n_pair, LANES), 0) + flags[3]
    for row in range(n_rows):
        hot_ref[row] = jnp.where(color_ref[row : row + 1, :] == ids, 1.0, 0.0)

    inner_sweep(n_lev, n_pair, flags, xe_ref, xi_ref, c_ref, None, hot_ref, pi_ref, be_ref, mid_ref)
    fold_rows(
        flags, fold_ref, nf_ref, lambda lev, kind, g: rows_at(xe_ref, 1, lev, kind, g, halves), mf_ref, n_lev, n_pair
    )


def inner_sweep(n_lev, n_pair, flags, xe_ref, xi_ref, c_ref, ec_ref, hot_ref, pi_ref, be_ref, mid_ref):
    halves = n_pair // 8

    def at(ref, line):
        return lambda lev, kind, g: rows_at(ref, line, lev, kind, g, halves)

    x = [at(xe_ref, 0), at(xi_ref, 0), at(xi_ref, 1), at(xe_ref, 1)]

    def row(number):
        edge = {0: {C0F: E0F, C0A: E0A}, 3: {C0F: T0F, C0A: T0A}}.get(number, {}) if ec_ref is not None else {}

        def coef(which, lev):
            return ec_ref[edge[which], lev] if which in edge else pick(c_ref, which, lev, number)

        sides = []
        if number > 0:
            sides.append((CSF, x[number - 1]))
        if number < 3:
            sides.append((CNF, x[number + 1]))
        explicit = own_part(n_pair, coef, lambda g: hot_ref[number, pl.ds(g * 8, 8), :], x[number], sides)
        return lambda lev: coef(UP, lev), explicit, number in (1, 2)

    def put(lev, i, kind, g, v):
        to, line = (pi_ref, i) if i < 2 else (be_ref, i - 2)
        to[lev, line, pl.ds((kind * halves + g) * 8, 8), :] = v

    def last(i, kind, g, v):
        mid_ref[i, pl.ds((kind * halves + g) * 8, 8), :] = v

    sweep(flags, n_lev, n_pair, [row(1), row(2), row(0), row(3)], put, last)


def edge_sweep(is_first, n_lev, n_pair, inner_ref, be_ref, c_ref, mf_ref, even_ref, odd_ref, *rest):
    flags = where_am_i(n_pair)
    halves = n_pair // 8
    is_top = flags[1] == 1
    up_even = flags[4] == 0

    def from_south(*at):
        return jnp.where(up_even, odd_ref[at], even_ref[at])

    def from_north(*at):
        return jnp.where(up_even, even_ref[at], odd_ref[at])

    if is_first:
        xe_ref, nf_ref, depth_ref, fold_ref, flow_ref, pe_ref, edge_ref, ec_ref, fs_ref = rest
        first = flags[0] * n_lev
        depth = depth_ref[...]
        own3 = depth[3:4]
        south_depth = from_south(n_lev, slice(0, 1), slice(None))
        folded = jnp.take_along_axis(spread(own3.astype(F32)), spread(fold_ref[0:1, :]), axis=1)[0:1]
        north_depth = jnp.where(is_top, folded, from_north(n_lev, slice(0, 1), slice(None)))
        open_south = jnp.where(flags[2] == 1, 0.0, 1.0)
        for lev in range(n_lev):
            k = first + lev
            kf = k.astype(F32)
            raw = flow_ref[lev, 3:4, :]
            fs_ref[lev] = spread(raw)
            wi0, wi3 = c_ref[WI, lev, 0:1, :], c_ref[WI, lev, 3:4, :]
            s = raw * jnp.where(kf < south_depth, 1.0, 0.0) * open_south * wi0
            n = nf_ref[lev, 3:4, :] * jnp.where(kf < north_depth, 1.0, 0.0) * wi3
            sp, sm, np_, nm = (jnp.maximum(v, 0.0) for v in (s, -s, n, -n))
            ec_ref[E0F, lev] = spread(c_ref[C0F, lev, 0:1, :] - sm)
            ec_ref[E0A, lev] = spread(c_ref[C0A, lev, 0:1, :] - sp)
            ec_ref[ESF, lev] = spread(sp)
            ec_ref[ESA, lev] = spread(sm)
            ec_ref[T0F, lev] = spread(c_ref[C0F, lev, 3:4, :] - np_)
            ec_ref[T0A, lev] = spread(c_ref[C0A, lev, 3:4, :] - nm)
            ec_ref[TNF, lev] = spread(nm)
            ec_ref[TNA, lev] = spread(np_)
    else:
        ec_ref, pe_ref, edge_ref = rest

    def come_north(lev, g):
        to = pl.ds(g * 8, 8)
        come = from_north(lev, to, slice(None))
        return jnp.where(is_top, mf_ref[lev, to, :], come)

    def row(i, number, inflow, come):
        def explicit(lev):
            ks = [ec_ref[inflow + kind, lev] for kind in range(2)]
            ms = [come(lev, g) for g in range(halves)]
            out = []
            for kind in range(2):
                vs = []
                for g in range(halves):
                    v = rows_at(be_ref, i, lev, kind, g, halves) + ks[kind] * ms[g]
                    if is_first:
                        v = v - ks[1 - kind] * rows_at(xe_ref, i, lev, kind, g, halves)
                    vs.append(v)
                out.append(vs)
            return out

        return lambda lev: pick(c_ref, UP, lev, number), explicit, True

    def put(lev, i, kind, g, v):
        pe_ref[lev, i, pl.ds((kind * halves + g) * 8, 8), :] = v

    def last(i, kind, g, v):
        edge_ref[i, pl.ds((kind * halves + g) * 8, 8), :] = v

    rows = [row(0, 0, ESF, lambda lev, g: from_south(lev, pl.ds(g * 8, 8), slice(None))), row(1, 3, TNF, come_north)]
    sweep(flags, n_lev, n_pair, rows, put, last)
    if is_first:
        edge_ref[2:4] = inner_ref[...]


def tallies(is_first, in_ref, out_ref, n_lev):
    if is_first:
        out_ref[0] = jnp.zeros(out_ref.shape[1:], F32)
        out_ref[n_lev] = jnp.zeros(out_ref.shape[1:], F32)
    else:
        out_ref[0] = in_ref[0]
        out_ref[n_lev] = in_ref[n_lev]
    zero = jnp.zeros((8, LANES), F32)

    def put(at, i, v):
        out_ref[at, i] = v

    return (lambda at, i: zero) if is_first else (lambda at, i: in_ref[at, i]), put


def edge_back(is_first, n_lev, n_pair, pe_ref, far_ref, c_ref, wx_ref, nf_ref, fs_ref, *rest):
    flags = where_am_i(n_pair)
    halves = n_pair // 8
    acc_ref, (xe_ref, even_ref, odd_ref, out_ref) = (None, rest) if is_first else (rest[0], rest[1:])
    acc_in, acc_out = tallies(is_first, acc_ref, out_ref, n_lev)
    held, south = {}, {}
    up_even = flags[4] == 0

    def put(lev, i, kind, g, v):
        xe_ref[lev, i, pl.ds((kind * halves + g) * 8, 8), :] = v
        if kind == 0:
            held[i, g] = v
        elif i == 0:
            south[g] = jnp.where(fs_ref[lev] < 0.0, held[i, g], v)
        else:
            n3 = spread(nf_ref[lev, 3:4, :])
            north = jnp.where(n3 > 0.0, held[i, g], v)
            even_ref[lev, pl.ds(g * 8, 8), :] = jnp.where(up_even, north, south[g])
            odd_ref[lev, pl.ds(g * 8, 8), :] = jnp.where(up_even, south[g], north)

    back(
        flags, n_lev, n_pair, (0, 3), wx_ref, lambda i, row, at: far_ref[i, at, :], c_ref,
        lambda lev, i, kind, g: rows_at(pe_ref, i, lev, kind, g, halves), put, acc_in, acc_out,
    )


def inner(
    is_first, n_lev, n_pair, pi_ref, far_ref, c_ref, ec_ref, wx_ref, nf_ref, fold_ref, hot_ref, xe_ref, *rest
):
    flags = where_am_i(n_pair)
    halves = n_pair // 8
    acc_ref, (mid_ref, pn_ref, be_ref, mf_ref, out_ref, xi_ref) = (None, rest) if is_first else (rest[0], rest[1:])
    acc_in, acc_out = tallies(is_first, acc_ref, out_ref, n_lev)

    def put(lev, i, kind, g, v):
        xi_ref[lev, i, pl.ds((kind * halves + g) * 8, 8), :] = v

    back(
        flags, n_lev, n_pair, (1, 2), wx_ref, lambda i, row, at: far_ref[2 * is_first + i, at, :], c_ref,
        lambda lev, i, kind, g: rows_at(pi_ref, i, lev, kind, g, halves), put, acc_in, acc_out,
    )
    inner_sweep(n_lev, n_pair, flags, xe_ref, xi_ref, c_ref, ec_ref, hot_ref, pn_ref, be_ref, mid_ref)
    fold_rows(
        flags, fold_ref, nf_ref, lambda lev, kind, g: rows_at(xe_ref, 1, lev, kind, g, halves), mf_ref, n_lev, n_pair
    )


def finish(
    n_lev, n_pair, n_rows, pe_ref, pi_ref, fare_ref, fari_ref, c_ref, wx_ref, depth_ref, acce_ref, acci_ref,
    x_ref, sens_ref, te_ref, ti_ref,
):
    flags = where_am_i(n_pair)
    halves = n_pair // 8
    def far_of(i, row, at):
        return (fare_ref[i // 3] if i in (0, 3) else fari_ref[i - 1])[at.start : at.start + at.size]

    ps = [(pe_ref, 0), (pi_ref, 0), (pi_ref, 1), (pe_ref, 1)]
    e_in, e_out = tallies(False, acce_ref, te_ref, n_lev)
    i_in, i_out = tallies(False, acci_ref, ti_ref, n_lev)

    def put(lev, i, kind, g, v):
        x_ref[lev * n_rows + i, pl.ds((kind * halves + g) * 8, 8), :] = v

    back(
        flags, n_lev, n_pair, range(4), wx_ref, far_of, c_ref,
        lambda lev, i, kind, g: rows_at(ps[i][0], ps[i][1], lev, kind, g, halves), put,
        lambda at, i: e_in(at, i // 3) if i in (0, 3) else i_in(at, i - 1),
        lambda at, i, v: e_out(at, i // 3, v) if i in (0, 3) else i_out(at, i - 1, v),
    )
    first = flags[0] * n_lev
    depth = depth_ref[...]

    def reduce(lev, _):
        k = first + lev
        live = jnp.where((k + 1 < depth) & (k + 1 < 2 * n_lev), 1.0 / STEPS, 0.0)
        e0, e3 = (jnp.sum(te_ref[lev + 1, i], axis=0, keepdims=True) for i in range(2))
        i1, i2 = (jnp.sum(ti_ref[lev + 1, i], axis=0, keepdims=True) for i in range(2))
        sens_ref[lev] = jnp.concatenate([e0, i1, i2, e3], 0) * live
        return 0

    lax.fori_loop(0, n_lev, reduce, 0, unroll=UNROLL)


def hand_out(n_pair, x_ref, f_hbm, a_hbm, sems):
    copies = [
        pltpu.make_async_copy(x_ref.at[:, kind * n_pair + j, :], hbm.at[j], sems.at[kind * n_pair + j])
        for j in range(n_pair)
        for kind, hbm in enumerate((f_hbm, a_hbm))
    ]
    for copy in copies:
        copy.start()
    for copy in copies:
        copy.wait()


def vmem(*shape):
    return pltpu.VMEM(shape, F32)


def where_am_i(n_pair):
    place, count = lax.axis_index("horiz"), lax.axis_size("horiz")
    return (
        lax.axis_index("level"),
        jnp.where(place == count - 1, 1, 0),
        jnp.where(place == 0, 1, 0),
        lax.axis_index("tracer") * n_pair,
        lax.rem(place, 2),
    )


def call(kernel, outs, args, flops, scratch=(), hbm_in=False, hbm_out=0):
    near, far = pl.BlockSpec(memory_space=pltpu.VMEM), pl.BlockSpec(memory_space=pltpu.HBM)
    return pl.pallas_call(
        kernel,
        out_shape=tuple(outs),
        in_specs=[far if hbm_in else near] * len(args),
        out_specs=tuple([far] * hbm_out + [near] * (len(outs) - hbm_out)),
        scratch_shapes=list(scratch),
        compiler_params=pltpu.CompilerParams(vmem_limit_bytes=24 * 2**20),
        cost_estimate=pl.CostEstimate(flops=flops, bytes_accessed=flops // 8, transcendentals=0),
    )(*[pltpu.with_memory_space_constraint(a, pltpu.HBM if hbm_in else pltpu.VMEM) for a in args])


def per_device(forward_init, adjoint_init, east_flow, north_flow, mixing, depth, color, fold):
    n_pair, n_lev, n_rows, n_x = forward_init.shape
    n_all = 2 * n_pair
    count = lax.axis_size("horiz")
    even = [(2 * i + t, 2 * (i ^ 1) + t) for i in range(count) for t in range(2)]
    odd = []
    for i in range(count):
        partner = ((i - 1) ^ 1) + 1 if i > 0 else count
        odd += [(2 * i + t, 2 * partner + t if partner < count else 2 * i + 1 - t) for t in range(2)]
    pairs = ("horiz", "tracer")
    swap = [(0, 1), (1, 0)]
    f2 = forward_init.reshape(n_pair * n_lev * n_rows, n_x)
    a2 = adjoint_init.reshape(n_pair * n_lev * n_rows, n_x)
    fold2 = fold.reshape(1, n_x)
    work = n_lev * n_rows * n_all * n_x

    flat = vmem(n_pair * n_lev * n_rows, n_x)
    flow = lax.ppermute(north_flow, "horiz", [(i, (i + 1) % count) for i in range(count)])
    f2, a2, north_flow, depth = call(
        functools.partial(load, n_pair),
        [flat, flat, vmem(n_lev, n_rows, n_x), pltpu.VMEM((n_rows, n_x), jnp.int32)],
        [f2, a2, north_flow, depth],
        work,
        [pltpu.SemaphoreType.DMA((10,))],
        hbm_in=True,
    )
    message = vmem(n_lev + 1, n_pair, n_x)
    to_even, to_odd = call(
        functools.partial(send_first, n_lev, n_pair, n_rows), [message, message], [f2, a2, north_flow, depth, flow], work
    )
    from_odd = lax.ppermute(to_odd, pairs, odd)
    from_even = lax.ppermute(to_even, pairs, even)
    state = vmem(n_lev, 2, n_all, n_x)
    halo = vmem(n_lev, n_pair, n_x)
    acc = vmem(n_lev + 1, 2, 8, n_x)
    edges = vmem(2, n_all, n_x)
    mid, xe, pi, be, c, wx, hot, mf = call(
        functools.partial(prepare, n_lev, n_pair, n_rows),
        [edges] + [state] * 3 + [vmem(13, n_lev, n_rows, n_x), vmem(3, n_rows, n_x), vmem(n_rows, n_pair, n_x), halo],
        [f2, a2, east_flow, north_flow, mixing, depth, color, fold2],
        work * 10,
        [vmem(n_lev, n_rows, n_x), state],
    )
    acce = acci = None
    for step in range(STEPS):
        if step == 0:
            pe, edge, ec, fs = call(
                functools.partial(edge_sweep, True, n_lev, n_pair),
                [state, vmem(n_rows, n_all, n_x), vmem(8, n_lev, 8, n_x), vmem(n_lev, 8, n_x)],
                [mid, be, c, mf, from_even, from_odd, xe, north_flow, depth, fold2, flow],
                work * 3,
            )
        else:
            pe, edge = call(
                functools.partial(edge_sweep, False, n_lev, n_pair),
                [state, edges],
                [fari, be, c, mf, from_even, from_odd, ec],
                work * 2,
            )
        fare = lax.ppermute(edge, "level", swap)
        if step == 0:
            fari = fare
        if step == STEPS - 1:
            break
        more = [] if step == 0 else [acce]
        xe, to_even, to_odd, acce = call(
            functools.partial(edge_back, step == 0, n_lev, n_pair),
            [state, halo, halo, acc],
            [pe, fare, c, wx, north_flow, fs] + more,
            work * 2,
        )
        from_odd = lax.ppermute(to_odd, pairs, odd)
        from_even = lax.ppermute(to_even, pairs, even)
        more = [] if step == 0 else [acci]
        mid, pi, be, mf, acci = call(
            functools.partial(inner, step == 0, n_lev, n_pair),
            [edges, state, state, halo, acc],
            [pi, fari, c, ec, wx, north_flow, fold2, hot, xe] + more,
            work * 9,
            [state],
        )
        fari = lax.ppermute(mid, "level", swap)
    x, sens = call(
        functools.partial(finish, n_lev, n_pair, n_rows),
        [vmem(n_lev * n_rows, n_all, n_x), vmem(n_lev, n_rows, n_x)],
        [pe, pi, fare, fari, c, wx, depth, acce, acci],
        work * 4,
        [acc, acc],
    )
    out = jax.ShapeDtypeStruct((n_pair, n_lev * n_rows, n_x), F32)
    f_out, a_out = call(
        functools.partial(hand_out, n_pair),
        [out, out],
        [x],
        work * 4,
        [pltpu.SemaphoreType.DMA((n_all,))],
        hbm_out=2,
    )
    sens = sens + lax.ppermute(sens, "tracer", swap)
    return f_out.reshape(forward_init.shape), a_out.reshape(adjoint_init.shape), sens


def solution(mesh):
    tracers, flows = P("tracer", "level", "horiz", None), P("level", "horiz", None)
    return jax.shard_map(
        per_device,
        mesh=mesh,
        in_specs=(tracers, tracers, flows, flows, P(None, "horiz", None), P("horiz", None), P("horiz", None), P()),
        out_specs=(tracers, tracers, flows),
        check_vma=False,
    )
```

```python
import functools
import jax
import jax.numpy as jnp
from jax import lax
from jax.experimental import pallas as pl
from jax.experimental.pallas import tpu as pltpu
from jax.sharding import PartitionSpec as P

STEPS = 4
LANES = 128
C0F, C0A, CWF, CWA, CEF, CEA, CSF, CSA, CNF, CNA, UP, WI, BACK = range(13)
E0F, E0A, ESF, ESA, T0F, T0A, TNF, TNA = range(8)
F32 = jnp.float32
UNROLL = 8


def order(flags, n_lev):
    bottom = flags[0]
    return bottom * (n_lev - 1), 1 - 2 * bottom


def west(v):
    return pltpu.roll(v, 1, 1)


def east(v):
    return pltpu.roll(v, LANES - 1, 1)


def spread(v):
    return jnp.broadcast_to(v, (8, LANES))


def pick(c_ref, which, lev, row):
    return spread(c_ref[which, lev, row : row + 1, :])


def sweep(flags, n_lev, n_pair, rows, put, last):
    k0, dk = order(flags, n_lev)
    halves = n_pair // 8
    zero = jnp.zeros((8, LANES), F32)

    def body(s, carry):
        lev = k0 + dk * s
        out = []
        for i, (up, explicit, swept) in enumerate(rows):
            values = explicit(lev)
            factor = up(lev) if swept else None
            for kind in range(2):
                for g in range(halves):
                    v = values[kind][g]
                    if swept:
                        v = v + factor * carry[len(out)]
                        out.append(v)
                    put(lev, i, kind, g, v)
        return tuple(out)

    n_swept = sum(row[2] for row in rows)
    final = lax.fori_loop(0, n_lev, body, (zero,) * (n_swept * 2 * halves), unroll=UNROLL)
    for at, v in enumerate(final):
        last(at // (2 * halves), at // halves % 2, at % halves, v)


def own_part(n_pair, coef, src, center, sides):
    halves = n_pair // 8

    def explicit(lev):
        wi = coef(WI, lev)
        srcs = [src(g) * wi for g in range(halves)]
        out = []
        for kind in range(2):
            c0, cw, ce = (coef(base + kind, lev) for base in (C0F, CWF, CEF))
            cs = [coef(base + kind, lev) for base, _ in sides]
            vs = []
            for g in range(halves):
                c = center(lev, kind, g)
                v = (c0 * c + srcs[g]) + (cw * west(c) + ce * east(c))
                for k, (_, side) in zip(cs, sides):
                    v = v + k * side(lev, kind, g)
                vs.append(v)
            out.append(vs)
        return out

    return explicit


def back(flags, n_lev, n_pair, rows, wx_ref, far, c_ref, part, put, acc_in, acc_out):
    bottom = flags[0]
    k0, dk = order(flags, n_lev)
    halves = n_pair // 8
    mid = k0 + dk * (n_lev - 1)
    own, beyond = [], []
    for i, row in enumerate(rows):
        wa, wb, ff = (spread(wx_ref[j, row : row + 1, :]) for j in range(3))
        for kind in range(2):
            for g in range(halves):
                p_far = far(i, row, pl.ds((kind * halves + g) * 8, 8))
                x = wa * part(mid, i, kind, g) + wb * p_far
                own.append(x)
                beyond.append(p_far + ff * x)

    def tally(s, now, nxt):
        at = jnp.where(bottom == 0, s + 1, n_lev - 1 - s)
        for i in range(len(rows)):
            b = i * 2 * halves
            total = acc_in(at, i)
            for g in range(halves):
                f, a = b + g, b + halves + g
                total = total + (nxt[f] - now[f]) * (nxt[a] - now[a])
            acc_out(at, i, total)

    def store(lev, xs):
        at = 0
        for i in range(len(rows)):
            for kind in range(2):
                for g in range(halves):
                    put(lev, i, kind, g, xs[at])
                    at += 1

    tally(n_lev - 1, own, beyond)
    store(mid, own)

    def body(q, nxt):
        s = n_lev - 2 - q
        lev = k0 + dk * s
        now = []
        at = 0
        for i, row in enumerate(rows):
            f = pick(c_ref, BACK, lev, row)
            for kind in range(2):
                for g in range(halves):
                    now.append(part(lev, i, kind, g) + f * nxt[at])
                    at += 1
        tally(s, now, nxt)
        store(lev, now)
        return tuple(now)

    lax.fori_loop(0, n_lev - 1, body, tuple(own), unroll=UNROLL)


def fold_rows(flags, fold_ref, nf_ref, get, mf_ref, n_lev, n_pair):
    @pl.when(flags[1] == 1)
    def _():
        where_to = spread(fold_ref[0:1, :])

        def body(lev, _):
            n3 = spread(nf_ref[lev, 3:4, :])
            for g in range(n_pair // 8):
                f = jnp.take_along_axis(get(lev, 0, g), where_to, axis=1)
                a = jnp.take_along_axis(get(lev, 1, g), where_to, axis=1)
                mf_ref[lev, pl.ds(g * 8, 8), :] = jnp.where(n3 < 0.0, f, a)
            return 0

        lax.fori_loop(0, n_lev, body, 0, unroll=4)


def rows_at(ref, row, lev, kind, g, halves):
    return ref[lev, row, pl.ds((kind * halves + g) * 8, 8), :]


def load(n_pair, f_hbm, a_hbm, nf_hbm, depth_hbm, f_ref, a_ref, nf_ref, depth_ref, sems):
    part = f_ref.shape[0] // 4
    copies = [
        pltpu.make_async_copy(nf_hbm, nf_ref, sems.at[0]),
        pltpu.make_async_copy(depth_hbm, depth_ref, sems.at[1]),
    ]
    for j in range(4):
        for i, (hbm, to) in enumerate(((f_hbm, f_ref), (a_hbm, a_ref))):
            at = pl.ds(j * part, part)
            copies.append(pltpu.make_async_copy(hbm.at[at, :], to.at[at, :], sems.at[2 + 2 * j + i]))
    for copy in copies:
        copy.start()
    for copy in copies:
        copy.wait()


def send_first(n_lev, n_pair, n_rows, f_ref, a_ref, nf_ref, depth_ref, flow_ref, even_ref, odd_ref):
    stride = n_lev * n_rows
    first = lax.axis_index("level") * n_lev
    up_even = lax.rem(lax.axis_index("horiz"), 2) == 0
    depth = depth_ref[...]
    low, high = spread(depth[0:1]), spread(depth[n_rows - 1 : n_rows])
    for g in range(n_pair // 8):
        to = pl.ds(g * 8, 8)
        even_ref[n_lev, to, :] = jnp.where(up_even, high, low).astype(F32)
        odd_ref[n_lev, to, :] = jnp.where(up_even, low, high).astype(F32)

    def body(lev, _):
        w0 = jnp.where(first + lev < low, 1.0, 0.0)
        w3 = jnp.where(first + lev < high, 1.0, 0.0)
        n3 = spread(nf_ref[lev, n_rows - 1 : n_rows, :])
        s0 = spread(flow_ref[pl.ds(lev, 1), :])
        for g in range(n_pair // 8):
            at = g * 8 * stride + lev * n_rows
            at0, at3 = pl.ds(at, 8, stride=stride), pl.ds(at + n_rows - 1, 8, stride=stride)
            to = pl.ds(g * 8, 8)
            north = jnp.where(n3 > 0.0, f_ref[at3, :], a_ref[at3, :]) * w3
            south = jnp.where(s0 < 0.0, f_ref[at0, :], a_ref[at0, :]) * w0
            even_ref[lev, to, :] = jnp.where(up_even, north, south)
            odd_ref[lev, to, :] = jnp.where(up_even, south, north)
        return 0

    lax.fori_loop(0, n_lev, body, 0, unroll=UNROLL)


def prepare(
    n_lev, n_pair, n_rows, f_ref, a_ref, ef_ref, nf_ref, mix_ref, depth_ref, color_ref, fold_ref,
    mid_ref, xe_ref, pi_ref, be_ref, c_ref, wx_ref, hot_ref, mf_ref, inv_ref, xi_ref,
):
    flags = where_am_i(n_pair)
    halves = n_pair // 8
    stride = n_lev * n_rows
    bottom = flags[0]
    first = bottom * n_lev
    k0, dk = order(flags, n_lev)
    depth = depth_ref[...]

    def lay(lev, _):
        wet = jnp.where(first + lev < depth, 1.0, 0.0)
        for row in range(n_rows):
            w = spread(wet[row : row + 1])
            to_ref, line = (xe_ref, row // 3) if row in (0, 3) else (xi_ref, row - 1)
            for kind, from_ref in enumerate((f_ref, a_ref)):
                for g in range(halves):
                    v = from_ref[pl.ds(g * 8 * stride + lev * n_rows + row, 8, stride=stride), :]
                    to_ref[lev, line, pl.ds((kind * halves + g) * 8, 8), :] = v * w
        return 0

    lax.fori_loop(0, n_lev, lay, 0, unroll=UNROLL)

    def coupling(k):
        inner = jnp.where((k >= 0) & (k < 2 * n_lev - 1), 1.0, 0.0)
        m = mix_ref[jnp.clip(k, 0, 2 * n_lev - 2)]
        return m * jnp.where(k + 1 < depth, inner, 0.0)

    def eliminate(s, carry):
        own_f, far_f = carry
        k = bottom * (2 * n_lev - 1) + dk * s
        prev, nxt = coupling(k - 1 + bottom), coupling(k - bottom)
        inverse = 1.0 / (1.0 + nxt + prev * (1.0 - own_f))
        lev = k0 + dk * s
        inv_ref[lev] = inverse
        c_ref[UP, lev] = prev * inverse
        own_f = nxt * inverse
        c_ref[BACK, lev] = own_f
        k = (1 - bottom) * (2 * n_lev - 1) - dk * s
        prev, nxt = coupling(k - bottom), coupling(k - 1 + bottom)
        far_f = nxt / (1.0 + nxt + prev * (1.0 - far_f))
        return own_f, far_f

    one = jnp.zeros((n_rows, LANES), F32)
    own_f, far_f = lax.fori_loop(0, n_lev, eliminate, (one, one), unroll=UNROLL)
    meet = 1.0 / (1.0 - own_f * far_f)
    wx_ref[0] = meet
    wx_ref[1] = own_f * meet
    wx_ref[2] = far_f

    depth_east = east(depth)
    depth_north = jnp.concatenate([depth[1:], jnp.zeros((1, LANES), jnp.int32)], 0)

    def coefs(lev, _):
        k = first + lev
        wet = jnp.where(k < depth, 1.0, 0.0)
        inverse = inv_ref[lev]
        e = ef_ref[lev] * wet * jnp.where(k < depth_east, 1.0, 0.0)
        n = nf_ref[lev] * wet * jnp.where(k < depth_north, 1.0, 0.0)
        w = west(e)
        s = jnp.concatenate([jnp.zeros((1, LANES), F32), n[:-1]], 0)
        plus = [jnp.maximum(v, 0.0) for v in (w, e, s, n)]
        minus = [jnp.maximum(-v, 0.0) for v in (w, e, s, n)]
        c_ref[C0F, lev] = (1.0 - minus[0] - plus[1] - minus[2] - plus[3]) * inverse
        c_ref[C0A, lev] = (1.0 - plus[0] - minus[1] - plus[2] - minus[3]) * inverse
        c_ref[CWF, lev], c_ref[CWA, lev] = plus[0] * inverse, minus[0] * inverse
        c_ref[CEF, lev], c_ref[CEA, lev] = minus[1] * inverse, plus[1] * inverse
        c_ref[CSF, lev], c_ref[CSA, lev] = plus[2] * inverse, minus[2] * inverse
        c_ref[CNF, lev], c_ref[CNA, lev] = minus[3] * inverse, plus[3] * inverse
        c_ref[WI, lev] = wet * inverse
        return 0

    lax.fori_loop(0, n_lev, coefs, 0, unroll=UNROLL)

    ids = lax.broadcasted_iota(jnp.int32, (n_pair, LANES), 0) + flags[3]
    for row in range(n_rows):
        hot_ref[row] = jnp.where(color_ref[row : row + 1, :] == ids, 1.0, 0.0)

    inner_sweep(n_lev, n_pair, flags, xe_ref, xi_ref, c_ref, None, hot_ref, pi_ref, be_ref, mid_ref)
    fold_rows(
        flags, fold_ref, nf_ref, lambda lev, kind, g: rows_at(xe_ref, 1, lev, kind, g, halves), mf_ref, n_lev, n_pair
    )


def inner_sweep(n_lev, n_pair, flags, xe_ref, xi_ref, c_ref, ec_ref, hot_ref, pi_ref, be_ref, mid_ref):
    halves = n_pair // 8

    def at(ref, line):
        return lambda lev, kind, g: rows_at(ref, line, lev, kind, g, halves)

    x = [at(xe_ref, 0), at(xi_ref, 0), at(xi_ref, 1), at(xe_ref, 1)]

    def row(number):
        edge = {0: {C0F: E0F, C0A: E0A}, 3: {C0F: T0F, C0A: T0A}}.get(number, {}) if ec_ref is not None else {}

        def coef(which, lev):
            return ec_ref[edge[which], lev] if which in edge else pick(c_ref, which, lev, number)

        sides = []
        if number > 0:
            sides.append((CSF, x[number - 1]))
        if number < 3:
            sides.append((CNF, x[number + 1]))
        explicit = own_part(n_pair, coef, lambda g: hot_ref[number, pl.ds(g * 8, 8), :], x[number], sides)
        return lambda lev: coef(UP, lev), explicit, number in (1, 2)

    def put(lev, i, kind, g, v):
        to, line = (pi_ref, i) if i < 2 else (be_ref, i - 2)
        to[lev, line, pl.ds((kind * halves + g) * 8, 8), :] = v

    def last(i, kind, g, v):
        mid_ref[i, pl.ds((kind * halves + g) * 8, 8), :] = v

    sweep(flags, n_lev, n_pair, [row(1), row(2), row(0), row(3)], put, last)


def edge_sweep(is_first, n_lev, n_pair, inner_ref, be_ref, c_ref, mf_ref, even_ref, odd_ref, *rest):
    flags = where_am_i(n_pair)
    halves = n_pair // 8
    is_top = flags[1] == 1
    up_even = flags[4] == 0

    def from_south(*at):
        return jnp.where(up_even, odd_ref[at], even_ref[at])

    def from_north(*at):
        return jnp.where(up_even, even_ref[at], odd_ref[at])

    if is_first:
        xe_ref, nf_ref, depth_ref, fold_ref, flow_ref, pe_ref, edge_ref, ec_ref, fs_ref = rest
        first = flags[0] * n_lev
        depth = depth_ref[...]
        own3 = depth[3:4]
        south_depth = from_south(n_lev, slice(0, 1), slice(None))
        folded = jnp.take_along_axis(spread(own3.astype(F32)), spread(fold_ref[0:1, :]), axis=1)[0:1]
        north_depth = jnp.where(is_top, folded, from_north(n_lev, slice(0, 1), slice(None)))
        open_south = jnp.where(flags[2] == 1, 0.0, 1.0)
        for lev in range(n_lev):
            k = first + lev
            kf = k.astype(F32)
            raw = flow_ref[lev : lev + 1, :]
            fs_ref[lev] = spread(raw)
            wi0, wi3 = c_ref[WI, lev, 0:1, :], c_ref[WI, lev, 3:4, :]
            s = raw * jnp.where(kf < south_depth, 1.0, 0.0) * open_south * wi0
            n = nf_ref[lev, 3:4, :] * jnp.where(kf < north_depth, 1.0, 0.0) * wi3
            sp, sm, np_, nm = (jnp.maximum(v, 0.0) for v in (s, -s, n, -n))
            ec_ref[E0F, lev] = spread(c_ref[C0F, lev, 0:1, :] - sm)
            ec_ref[E0A, lev] = spread(c_ref[C0A, lev, 0:1, :] - sp)
            ec_ref[ESF, lev] = spread(sp)
            ec_ref[ESA, lev] = spread(sm)
            ec_ref[T0F, lev] = spread(c_ref[C0F, lev, 3:4, :] - np_)
            ec_ref[T0A, lev] = spread(c_ref[C0A, lev, 3:4, :] - nm)
            ec_ref[TNF, lev] = spread(nm)
            ec_ref[TNA, lev] = spread(np_)
    else:
        ec_ref, pe_ref, edge_ref = rest

    def come_north(lev, g):
        to = pl.ds(g * 8, 8)
        come = from_north(lev, to, slice(None))
        return jnp.where(is_top, mf_ref[lev, to, :], come)

    def row(i, number, inflow, come):
        def explicit(lev):
            ks = [ec_ref[inflow + kind, lev] for kind in range(2)]
            ms = [come(lev, g) for g in range(halves)]
            out = []
            for kind in range(2):
                vs = []
                for g in range(halves):
                    v = rows_at(be_ref, i, lev, kind, g, halves) + ks[kind] * ms[g]
                    if is_first:
                        v = v - ks[1 - kind] * rows_at(xe_ref, i, lev, kind, g, halves)
                    vs.append(v)
                out.append(vs)
            return out

        return lambda lev: pick(c_ref, UP, lev, number), explicit, True

    def put(lev, i, kind, g, v):
        pe_ref[lev, i, pl.ds((kind * halves + g) * 8, 8), :] = v

    def last(i, kind, g, v):
        edge_ref[i, pl.ds((kind * halves + g) * 8, 8), :] = v

    rows = [row(0, 0, ESF, lambda lev, g: from_south(lev, pl.ds(g * 8, 8), slice(None))), row(1, 3, TNF, come_north)]
    sweep(flags, n_lev, n_pair, rows, put, last)
    if is_first:
        edge_ref[2:4] = inner_ref[...]


def tallies(is_first, in_ref, out_ref, n_lev):
    if is_first:
        out_ref[0] = jnp.zeros(out_ref.shape[1:], F32)
        out_ref[n_lev] = jnp.zeros(out_ref.shape[1:], F32)
    else:
        out_ref[0] = in_ref[0]
        out_ref[n_lev] = in_ref[n_lev]
    zero = jnp.zeros((8, LANES), F32)

    def put(at, i, v):
        out_ref[at, i] = v

    return (lambda at, i: zero) if is_first else (lambda at, i: in_ref[at, i]), put


def edge_back(is_first, n_lev, n_pair, pe_ref, far_ref, c_ref, wx_ref, nf_ref, fs_ref, *rest):
    flags = where_am_i(n_pair)
    halves = n_pair // 8
    acc_ref, (xe_ref, even_ref, odd_ref, out_ref) = (None, rest) if is_first else (rest[0], rest[1:])
    acc_in, acc_out = tallies(is_first, acc_ref, out_ref, n_lev)
    held, south = {}, {}
    up_even = flags[4] == 0

    def put(lev, i, kind, g, v):
        xe_ref[lev, i, pl.ds((kind * halves + g) * 8, 8), :] = v
        if kind == 0:
            held[i, g] = v
        elif i == 0:
            south[g] = jnp.where(fs_ref[lev] < 0.0, held[i, g], v)
        else:
            n3 = spread(nf_ref[lev, 3:4, :])
            north = jnp.where(n3 > 0.0, held[i, g], v)
            even_ref[lev, pl.ds(g * 8, 8), :] = jnp.where(up_even, north, south[g])
            odd_ref[lev, pl.ds(g * 8, 8), :] = jnp.where(up_even, south[g], north)

    back(
        flags, n_lev, n_pair, (0, 3), wx_ref, lambda i, row, at: far_ref[i, at, :], c_ref,
        lambda lev, i, kind, g: rows_at(pe_ref, i, lev, kind, g, halves), put, acc_in, acc_out,
    )


def inner(
    is_first, n_lev, n_pair, pi_ref, far_ref, c_ref, ec_ref, wx_ref, nf_ref, fold_ref, hot_ref, xe_ref, *rest
):
    flags = where_am_i(n_pair)
    halves = n_pair // 8
    acc_ref, (mid_ref, pn_ref, be_ref, mf_ref, out_ref, xi_ref) = (None, rest) if is_first else (rest[0], rest[1:])
    acc_in, acc_out = tallies(is_first, acc_ref, out_ref, n_lev)

    def put(lev, i, kind, g, v):
        xi_ref[lev, i, pl.ds((kind * halves + g) * 8, 8), :] = v

    back(
        flags, n_lev, n_pair, (1, 2), wx_ref, lambda i, row, at: far_ref[2 * is_first + i, at, :], c_ref,
        lambda lev, i, kind, g: rows_at(pi_ref, i, lev, kind, g, halves), put, acc_in, acc_out,
    )
    inner_sweep(n_lev, n_pair, flags, xe_ref, xi_ref, c_ref, ec_ref, hot_ref, pn_ref, be_ref, mid_ref)
    fold_rows(
        flags, fold_ref, nf_ref, lambda lev, kind, g: rows_at(xe_ref, 1, lev, kind, g, halves), mf_ref, n_lev, n_pair
    )


def finish(
    n_lev, n_pair, n_rows, pe_ref, pi_ref, fare_ref, fari_ref, c_ref, wx_ref, depth_ref, acce_ref, acci_ref,
    x_ref, sens_ref, te_ref, ti_ref,
):
    flags = where_am_i(n_pair)
    halves = n_pair // 8
    def far_of(i, row, at):
        return (fare_ref[i // 3] if i in (0, 3) else fari_ref[i - 1])[at.start : at.start + at.size]

    ps = [(pe_ref, 0), (pi_ref, 0), (pi_ref, 1), (pe_ref, 1)]
    e_in, e_out = tallies(False, acce_ref, te_ref, n_lev)
    i_in, i_out = tallies(False, acci_ref, ti_ref, n_lev)

    def put(lev, i, kind, g, v):
        x_ref[lev * n_rows + i, pl.ds((kind * halves + g) * 8, 8), :] = v

    back(
        flags, n_lev, n_pair, range(4), wx_ref, far_of, c_ref,
        lambda lev, i, kind, g: rows_at(ps[i][0], ps[i][1], lev, kind, g, halves), put,
        lambda at, i: e_in(at, i // 3) if i in (0, 3) else i_in(at, i - 1),
        lambda at, i, v: e_out(at, i // 3, v) if i in (0, 3) else i_out(at, i - 1, v),
    )
    first = flags[0] * n_lev
    depth = depth_ref[...]

    def reduce(lev, _):
        k = first + lev
        live = jnp.where((k + 1 < depth) & (k + 1 < 2 * n_lev), 1.0 / STEPS, 0.0)
        e0, e3 = (jnp.sum(te_ref[lev + 1, i], axis=0, keepdims=True) for i in range(2))
        i1, i2 = (jnp.sum(ti_ref[lev + 1, i], axis=0, keepdims=True) for i in range(2))
        sens_ref[lev] = jnp.concatenate([e0, i1, i2, e3], 0) * live
        return 0

    lax.fori_loop(0, n_lev, reduce, 0, unroll=UNROLL)


def hand_out(n_pair, x_ref, f_hbm, a_hbm, sems):
    copies = [
        pltpu.make_async_copy(x_ref.at[:, kind * n_pair + j, :], hbm.at[j], sems.at[kind * n_pair + j])
        for j in range(n_pair)
        for kind, hbm in enumerate((f_hbm, a_hbm))
    ]
    for copy in copies:
        copy.start()
    for copy in copies:
        copy.wait()


def vmem(*shape):
    return pltpu.VMEM(shape, F32)


def where_am_i(n_pair):
    place, count = lax.axis_index("horiz"), lax.axis_size("horiz")
    return (
        lax.axis_index("level"),
        jnp.where(place == count - 1, 1, 0),
        jnp.where(place == 0, 1, 0),
        lax.axis_index("tracer") * n_pair,
        lax.rem(place, 2),
    )


def call(kernel, outs, args, flops, scratch=(), hbm_in=False, hbm_out=0):
    near, far = pl.BlockSpec(memory_space=pltpu.VMEM), pl.BlockSpec(memory_space=pltpu.HBM)
    return pl.pallas_call(
        kernel,
        out_shape=tuple(outs),
        in_specs=[far if hbm_in else near] * len(args),
        out_specs=tuple([far] * hbm_out + [near] * (len(outs) - hbm_out)),
        scratch_shapes=list(scratch),
        compiler_params=pltpu.CompilerParams(vmem_limit_bytes=24 * 2**20),
        cost_estimate=pl.CostEstimate(flops=flops, bytes_accessed=flops // 8, transcendentals=0),
    )(*[pltpu.with_memory_space_constraint(a, pltpu.HBM if hbm_in else pltpu.VMEM) for a in args])


def per_device(forward_init, adjoint_init, east_flow, north_flow, mixing, depth, color, fold):
    n_pair, n_lev, n_rows, n_x = forward_init.shape
    n_all = 2 * n_pair
    count = lax.axis_size("horiz")
    even = [(2 * i + t, 2 * (i ^ 1) + t) for i in range(count) for t in range(2)]
    odd = []
    for i in range(count):
        partner = ((i - 1) ^ 1) + 1 if i > 0 else count
        odd += [(2 * i + t, 2 * partner + t if partner < count else 2 * i + 1 - t) for t in range(2)]
    pairs = ("horiz", "tracer")
    swap = [(0, 1), (1, 0)]
    f2 = forward_init.reshape(n_pair * n_lev * n_rows, n_x)
    a2 = adjoint_init.reshape(n_pair * n_lev * n_rows, n_x)
    fold2 = fold.reshape(1, n_x)
    work = n_lev * n_rows * n_all * n_x

    flat = vmem(n_pair * n_lev * n_rows, n_x)
    flow = lax.ppermute(north_flow[:, n_rows - 1], "horiz", [(i, (i + 1) % count) for i in range(count)])
    f2, a2, north_flow, depth = call(
        functools.partial(load, n_pair),
        [flat, flat, vmem(n_lev, n_rows, n_x), pltpu.VMEM((n_rows, n_x), jnp.int32)],
        [f2, a2, north_flow, depth],
        work,
        [pltpu.SemaphoreType.DMA((10,))],
        hbm_in=True,
    )
    message = vmem(n_lev + 1, n_pair, n_x)
    to_even, to_odd = call(
        functools.partial(send_first, n_lev, n_pair, n_rows), [message, message], [f2, a2, north_flow, depth, flow], work
    )
    from_odd = lax.ppermute(to_odd, pairs, odd)
    from_even = lax.ppermute(to_even, pairs, even)
    state = vmem(n_lev, 2, n_all, n_x)
    halo = vmem(n_lev, n_pair, n_x)
    acc = vmem(n_lev + 1, 2, 8, n_x)
    edges = vmem(2, n_all, n_x)
    mid, xe, pi, be, c, wx, hot, mf = call(
        functools.partial(prepare, n_lev, n_pair, n_rows),
        [edges] + [state] * 3 + [vmem(13, n_lev, n_rows, n_x), vmem(3, n_rows, n_x), vmem(n_rows, n_pair, n_x), halo],
        [f2, a2, east_flow, north_flow, mixing, depth, color, fold2],
        work * 10,
        [vmem(n_lev, n_rows, n_x), state],
    )
    acce = acci = None
    for step in range(STEPS):
        if step == 0:
            pe, edge, ec, fs = call(
                functools.partial(edge_sweep, True, n_lev, n_pair),
                [state, vmem(n_rows, n_all, n_x), vmem(8, n_lev, 8, n_x), vmem(n_lev, 8, n_x)],
                [mid, be, c, mf, from_even, from_odd, xe, north_flow, depth, fold2, flow],
                work * 3,
            )
        else:
            pe, edge = call(
                functools.partial(edge_sweep, False, n_lev, n_pair),
                [state, edges],
                [fari, be, c, mf, from_even, from_odd, ec],
                work * 2,
            )
        fare = lax.ppermute(edge, "level", swap)
        if step == 0:
            fari = fare
        if step == STEPS - 1:
            break
        more = [] if step == 0 else [acce]
        xe, to_even, to_odd, acce = call(
            functools.partial(edge_back, step == 0, n_lev, n_pair),
            [state, halo, halo, acc],
            [pe, fare, c, wx, north_flow, fs] + more,
            work * 2,
        )
        from_odd = lax.ppermute(to_odd, pairs, odd)
        from_even = lax.ppermute(to_even, pairs, even)
        more = [] if step == 0 else [acci]
        mid, pi, be, mf, acci = call(
            functools.partial(inner, step == 0, n_lev, n_pair),
            [edges, state, state, halo, acc],
            [pi, fari, c, ec, wx, north_flow, fold2, hot, xe] + more,
            work * 9,
            [state],
        )
        fari = lax.ppermute(mid, "level", swap)
    x, sens = call(
        functools.partial(finish, n_lev, n_pair, n_rows),
        [vmem(n_lev * n_rows, n_all, n_x), vmem(n_lev, n_rows, n_x)],
        [pe, pi, fare, fari, c, wx, depth, acce, acci],
        work * 4,
        [acc, acc],
    )
    out = jax.ShapeDtypeStruct((n_pair, n_lev * n_rows, n_x), F32)
    f_out, a_out = call(
        functools.partial(hand_out, n_pair),
        [out, out],
        [x],
        work * 4,
        [pltpu.SemaphoreType.DMA((n_all,))],
        hbm_out=2,
    )
    sens = sens + lax.ppermute(sens, "tracer", swap)
    return f_out.reshape(forward_init.shape), a_out.reshape(adjoint_init.shape), sens


def solution(mesh):
    tracers, flows = P("tracer", "level", "horiz", None), P("level", "horiz", None)
    return jax.shard_map(
        per_device,
        mesh=mesh,
        in_specs=(tracers, tracers, flows, flows, P(None, "horiz", None), P("horiz", None), P("horiz", None), P()),
        out_specs=(tracers, tracers, flows),
        check_vma=False,
    )
```

```python
import functools
import jax
import jax.numpy as jnp
from jax import lax
from jax.experimental import pallas as pl
from jax.experimental.pallas import tpu as pltpu
from jax.sharding import PartitionSpec as P

STEPS = 4
LANES = 128
C0F, C0A, CWF, CWA, CEF, CEA, CSF, CSA, CNF, CNA, UP, WI, BACK = range(13)
E0F, E0A, ESF, ESA, T0F, T0A, TNF, TNA = range(8)
F32 = jnp.float32
UNROLL = 8


def order(flags, n_lev):
    bottom = flags[0]
    return bottom * (n_lev - 1), 1 - 2 * bottom


def west(v):
    return pltpu.roll(v, 1, 1)


def east(v):
    return pltpu.roll(v, LANES - 1, 1)


def spread(v):
    return jnp.broadcast_to(v, (8, LANES))


def pick(c_ref, which, lev, row):
    return spread(c_ref[which, lev, row : row + 1, :])


def sweep(flags, n_lev, n_pair, rows, put, last):
    k0, dk = order(flags, n_lev)
    halves = n_pair // 8
    zero = jnp.zeros((8, LANES), F32)

    def body(s, carry):
        lev = k0 + dk * s
        out = []
        for i, (up, explicit, swept) in enumerate(rows):
            values = explicit(lev)
            factor = up(lev) if swept else None
            for kind in range(2):
                for g in range(halves):
                    v = values[kind][g]
                    if swept:
                        v = v + factor * carry[len(out)]
                        out.append(v)
                    put(lev, i, kind, g, v)
        return tuple(out)

    n_swept = sum(row[2] for row in rows)
    final = lax.fori_loop(0, n_lev, body, (zero,) * (n_swept * 2 * halves), unroll=UNROLL)
    for at, v in enumerate(final):
        last(at // (2 * halves), at // halves % 2, at % halves, v)


def own_part(n_pair, coef, src, center, sides):
    halves = n_pair // 8

    def explicit(lev):
        wi = coef(WI, lev)
        srcs = [src(g) * wi for g in range(halves)]
        out = []
        for kind in range(2):
            c0, cw, ce = (coef(base + kind, lev) for base in (C0F, CWF, CEF))
            cs = [coef(base + kind, lev) for base, _ in sides]
            vs = []
            for g in range(halves):
                c = center(lev, kind, g)
                v = (c0 * c + srcs[g]) + (cw * west(c) + ce * east(c))
                for k, (_, side) in zip(cs, sides):
                    v = v + k * side(lev, kind, g)
                vs.append(v)
            out.append(vs)
        return out

    return explicit


def back(flags, n_lev, n_pair, rows, wx_ref, far, c_ref, part, put, acc_in, acc_out):
    bottom = flags[0]
    k0, dk = order(flags, n_lev)
    halves = n_pair // 8
    mid = k0 + dk * (n_lev - 1)
    own, beyond = [], []
    for i, row in enumerate(rows):
        wa, wb, ff = (spread(wx_ref[j, row : row + 1, :]) for j in range(3))
        for kind in range(2):
            for g in range(halves):
                p_far = far(i, row, pl.ds((kind * halves + g) * 8, 8))
                x = wa * part(mid, i, kind, g) + wb * p_far
                own.append(x)
                beyond.append(p_far + ff * x)

    def tally(s, now, nxt):
        at = jnp.where(bottom == 0, s + 1, n_lev - 1 - s)
        for i in range(len(rows)):
            b = i * 2 * halves
            total = acc_in(at, i)
            for g in range(halves):
                f, a = b + g, b + halves + g
                total = total + (nxt[f] - now[f]) * (nxt[a] - now[a])
            acc_out(at, i, total)

    def store(lev, xs):
        at = 0
        for i in range(len(rows)):
            for kind in range(2):
                for g in range(halves):
                    put(lev, i, kind, g, xs[at])
                    at += 1

    tally(n_lev - 1, own, beyond)
    store(mid, own)

    def body(q, nxt):
        s = n_lev - 2 - q
        lev = k0 + dk * s
        now = []
        at = 0
        for i, row in enumerate(rows):
            f = pick(c_ref, BACK, lev, row)
            for kind in range(2):
                for g in range(halves):
                    now.append(part(lev, i, kind, g) + f * nxt[at])
                    at += 1
        tally(s, now, nxt)
        store(lev, now)
        return tuple(now)

    lax.fori_loop(0, n_lev - 1, body, tuple(own), unroll=UNROLL)


def fold_rows(flags, fold_ref, nf_ref, get, mf_ref, n_lev, n_pair):
    @pl.when(flags[1] == 1)
    def _():
        where_to = spread(fold_ref[0:1, :])

        def body(lev, _):
            n3 = spread(nf_ref[lev, 3:4, :])
            for g in range(n_pair // 8):
                f = jnp.take_along_axis(get(lev, 0, g), where_to, axis=1)
                a = jnp.take_along_axis(get(lev, 1, g), where_to, axis=1)
                mf_ref[lev, pl.ds(g * 8, 8), :] = jnp.where(n3 < 0.0, f, a)
            return 0

        lax.fori_loop(0, n_lev, body, 0, unroll=4)


def rows_at(ref, row, lev, kind, g, halves):
    return ref[lev, row, pl.ds((kind * halves + g) * 8, 8), :]


def load(n_lev, n_pair, n_rows, f_hbm, a_hbm, nf_hbm, depth_hbm, f_ref, a_ref, nf_ref, depth_ref, edge_ref, sems):
    part = f_ref.shape[0] // 4
    copies = [
        pltpu.make_async_copy(nf_hbm, nf_ref, sems.at[0]),
        pltpu.make_async_copy(depth_hbm, depth_ref, sems.at[1]),
    ]
    for j in range(4):
        for i, (hbm, to) in enumerate(((f_hbm, f_ref), (a_hbm, a_ref))):
            at = pl.ds(j * part, part)
            copies.append(pltpu.make_async_copy(hbm.at[at, :], to.at[at, :], sems.at[2 + 2 * j + i]))
    for copy in copies:
        copy.start()
    for copy in copies:
        copy.wait()
    stride = n_lev * n_rows
    first = lax.axis_index("level") * n_lev
    depth = depth_ref[...]
    low, high = spread(depth[0:1]), spread(depth[n_rows - 1 : n_rows])

    def body(lev, _):
        w0 = jnp.where(first + lev < low, 1.0, 0.0)
        w3 = jnp.where(first + lev < high, 1.0, 0.0)
        n3 = spread(nf_ref[lev, n_rows - 1 : n_rows, :])
        for g in range(n_pair // 8):
            at = g * 8 * stride + lev * n_rows
            at0, at3 = pl.ds(at, 8, stride=stride), pl.ds(at + n_rows - 1, 8, stride=stride)
            to = pl.ds(g * 8, 8)
            edge_ref[0, lev, to, :] = jnp.where(n3 > 0.0, f_ref[at3, :], a_ref[at3, :]) * w3
            edge_ref[1, lev, to, :] = f_ref[at0, :] * w0
            edge_ref[2, lev, to, :] = a_ref[at0, :] * w0
        return 0

    lax.fori_loop(0, n_lev, body, 0, unroll=UNROLL)


def send_first(n_lev, n_pair, n_rows, edge_ref, depth_ref, flow_ref, even_ref, odd_ref):
    up_even = lax.rem(lax.axis_index("horiz"), 2) == 0
    depth = depth_ref[...]
    low, high = spread(depth[0:1]), spread(depth[n_rows - 1 : n_rows])
    for g in range(n_pair // 8):
        to = pl.ds(g * 8, 8)
        even_ref[n_lev, to, :] = jnp.where(up_even, high, low).astype(F32)
        odd_ref[n_lev, to, :] = jnp.where(up_even, low, high).astype(F32)

    def body(lev, _):
        s0 = spread(flow_ref[lev, n_rows - 1 : n_rows, :])
        for g in range(n_pair // 8):
            to = pl.ds(g * 8, 8)
            north = edge_ref[0, lev, to, :]
            south = jnp.where(s0 < 0.0, edge_ref[1, lev, to, :], edge_ref[2, lev, to, :])
            even_ref[lev, to, :] = jnp.where(up_even, north, south)
            odd_ref[lev, to, :] = jnp.where(up_even, south, north)
        return 0

    lax.fori_loop(0, n_lev, body, 0, unroll=UNROLL)


def prepare(
    n_lev, n_pair, n_rows, f_ref, a_ref, ef_ref, nf_ref, mix_ref, depth_ref, color_ref, fold_ref,
    mid_ref, xe_ref, pi_ref, be_ref, c_ref, wx_ref, hot_ref, mf_ref, inv_ref, xi_ref,
):
    flags = where_am_i(n_pair)
    halves = n_pair // 8
    stride = n_lev * n_rows
    bottom = flags[0]
    first = bottom * n_lev
    k0, dk = order(flags, n_lev)
    depth = depth_ref[...]

    def lay(lev, _):
        wet = jnp.where(first + lev < depth, 1.0, 0.0)
        for row in range(n_rows):
            w = spread(wet[row : row + 1])
            to_ref, line = (xe_ref, row // 3) if row in (0, 3) else (xi_ref, row - 1)
            for kind, from_ref in enumerate((f_ref, a_ref)):
                for g in range(halves):
                    v = from_ref[pl.ds(g * 8 * stride + lev * n_rows + row, 8, stride=stride), :]
                    to_ref[lev, line, pl.ds((kind * halves + g) * 8, 8), :] = v * w
        return 0

    lax.fori_loop(0, n_lev, lay, 0, unroll=UNROLL)

    def coupling(k):
        inner = jnp.where((k >= 0) & (k < 2 * n_lev - 1), 1.0, 0.0)
        m = mix_ref[jnp.clip(k, 0, 2 * n_lev - 2)]
        return m * jnp.where(k + 1 < depth, inner, 0.0)

    def eliminate(s, carry):
        own_f, far_f = carry
        k = bottom * (2 * n_lev - 1) + dk * s
        prev, nxt = coupling(k - 1 + bottom), coupling(k - bottom)
        inverse = 1.0 / (1.0 + nxt + prev * (1.0 - own_f))
        lev = k0 + dk * s
        inv_ref[lev] = inverse
        c_ref[UP, lev] = prev * inverse
        own_f = nxt * inverse
        c_ref[BACK, lev] = own_f
        k = (1 - bottom) * (2 * n_lev - 1) - dk * s
        prev, nxt = coupling(k - bottom), coupling(k - 1 + bottom)
        far_f = nxt / (1.0 + nxt + prev * (1.0 - far_f))
        return own_f, far_f

    one = jnp.zeros((n_rows, LANES), F32)
    own_f, far_f = lax.fori_loop(0, n_lev, eliminate, (one, one), unroll=UNROLL)
    meet = 1.0 / (1.0 - own_f * far_f)
    wx_ref[0] = meet
    wx_ref[1] = own_f * meet
    wx_ref[2] = far_f

    depth_east = east(depth)
    depth_north = jnp.concatenate([depth[1:], jnp.zeros((1, LANES), jnp.int32)], 0)

    def coefs(lev, _):
        k = first + lev
        wet = jnp.where(k < depth, 1.0, 0.0)
        inverse = inv_ref[lev]
        e = ef_ref[lev] * wet * jnp.where(k < depth_east, 1.0, 0.0)
        n = nf_ref[lev] * wet * jnp.where(k < depth_north, 1.0, 0.0)
        w = west(e)
        s = jnp.concatenate([jnp.zeros((1, LANES), F32), n[:-1]], 0)
        plus = [jnp.maximum(v, 0.0) for v in (w, e, s, n)]
        minus = [jnp.maximum(-v, 0.0) for v in (w, e, s, n)]
        c_ref[C0F, lev] = (1.0 - minus[0] - plus[1] - minus[2] - plus[3]) * inverse
        c_ref[C0A, lev] = (1.0 - plus[0] - minus[1] - plus[2] - minus[3]) * inverse
        c_ref[CWF, lev], c_ref[CWA, lev] = plus[0] * inverse, minus[0] * inverse
        c_ref[CEF, lev], c_ref[CEA, lev] = minus[1] * inverse, plus[1] * inverse
        c_ref[CSF, lev], c_ref[CSA, lev] = plus[2] * inverse, minus[2] * inverse
        c_ref[CNF, lev], c_ref[CNA, lev] = minus[3] * inverse, plus[3] * inverse
        c_ref[WI, lev] = wet * inverse
        return 0

    lax.fori_loop(0, n_lev, coefs, 0, unroll=UNROLL)

    ids = lax.broadcasted_iota(jnp.int32, (n_pair, LANES), 0) + flags[3]
    for row in range(n_rows):
        hot_ref[row] = jnp.where(color_ref[row : row + 1, :] == ids, 1.0, 0.0)

    inner_sweep(n_lev, n_pair, flags, xe_ref, xi_ref, c_ref, None, hot_ref, pi_ref, be_ref, mid_ref)
    fold_rows(
        flags, fold_ref, nf_ref, lambda lev, kind, g: rows_at(xe_ref, 1, lev, kind, g, halves), mf_ref, n_lev, n_pair
    )


def inner_sweep(n_lev, n_pair, flags, xe_ref, xi_ref, c_ref, ec_ref, hot_ref, pi_ref, be_ref, mid_ref):
    halves = n_pair // 8

    def at(ref, line):
        return lambda lev, kind, g: rows_at(ref, line, lev, kind, g, halves)

    x = [at(xe_ref, 0), at(xi_ref, 0), at(xi_ref, 1), at(xe_ref, 1)]

    def row(number):
        edge = {0: {C0F: E0F, C0A: E0A}, 3: {C0F: T0F, C0A: T0A}}.get(number, {}) if ec_ref is not None else {}

        def coef(which, lev):
            return ec_ref[edge[which], lev] if which in edge else pick(c_ref, which, lev, number)

        sides = []
        if number > 0:
            sides.append((CSF, x[number - 1]))
        if number < 3:
            sides.append((CNF, x[number + 1]))
        explicit = own_part(n_pair, coef, lambda g: hot_ref[number, pl.ds(g * 8, 8), :], x[number], sides)
        return lambda lev: coef(UP, lev), explicit, number in (1, 2)

    def put(lev, i, kind, g, v):
        to, line = (pi_ref, i) if i < 2 else (be_ref, i - 2)
        to[lev, line, pl.ds((kind * halves + g) * 8, 8), :] = v

    def last(i, kind, g, v):
        mid_ref[i, pl.ds((kind * halves + g) * 8, 8), :] = v

    sweep(flags, n_lev, n_pair, [row(1), row(2), row(0), row(3)], put, last)


def edge_sweep(is_first, n_lev, n_pair, inner_ref, be_ref, c_ref, mf_ref, even_ref, odd_ref, *rest):
    flags = where_am_i(n_pair)
    halves = n_pair // 8
    is_top = flags[1] == 1
    up_even = flags[4] == 0

    def from_south(*at):
        return jnp.where(up_even, odd_ref[at], even_ref[at])

    def from_north(*at):
        return jnp.where(up_even, even_ref[at], odd_ref[at])

    if is_first:
        xe_ref, nf_ref, depth_ref, fold_ref, flow_ref, pe_ref, edge_ref, ec_ref, fs_ref = rest
        first = flags[0] * n_lev
        depth = depth_ref[...]
        own3 = depth[3:4]
        south_depth = from_south(n_lev, slice(0, 1), slice(None))
        folded = jnp.take_along_axis(spread(own3.astype(F32)), spread(fold_ref[0:1, :]), axis=1)[0:1]
        north_depth = jnp.where(is_top, folded, from_north(n_lev, slice(0, 1), slice(None)))
        open_south = jnp.where(flags[2] == 1, 0.0, 1.0)
        for lev in range(n_lev):
            k = first + lev
            kf = k.astype(F32)
            raw = flow_ref[lev, 3:4, :]
            fs_ref[lev] = spread(raw)
            wi0, wi3 = c_ref[WI, lev, 0:1, :], c_ref[WI, lev, 3:4, :]
            s = raw * jnp.where(kf < south_depth, 1.0, 0.0) * open_south * wi0
            n = nf_ref[lev, 3:4, :] * jnp.where(kf < north_depth, 1.0, 0.0) * wi3
            sp, sm, np_, nm = (jnp.maximum(v, 0.0) for v in (s, -s, n, -n))
            ec_ref[E0F, lev] = spread(c_ref[C0F, lev, 0:1, :] - sm)
            ec_ref[E0A, lev] = spread(c_ref[C0A, lev, 0:1, :] - sp)
            ec_ref[ESF, lev] = spread(sp)
            ec_ref[ESA, lev] = spread(sm)
            ec_ref[T0F, lev] = spread(c_ref[C0F, lev, 3:4, :] - np_)
            ec_ref[T0A, lev] = spread(c_ref[C0A, lev, 3:4, :] - nm)
            ec_ref[TNF, lev] = spread(nm)
            ec_ref[TNA, lev] = spread(np_)
    else:
        ec_ref, pe_ref, edge_ref = rest

    def come_north(lev, g):
        to = pl.ds(g * 8, 8)
        come = from_north(lev, to, slice(None))
        return jnp.where(is_top, mf_ref[lev, to, :], come)

    def row(i, number, inflow, come):
        def explicit(lev):
            ks = [ec_ref[inflow + kind, lev] for kind in range(2)]
            ms = [come(lev, g) for g in range(halves)]
            out = []
            for kind in range(2):
                vs = []
                for g in range(halves):
                    v = rows_at(be_ref, i, lev, kind, g, halves) + ks[kind] * ms[g]
                    if is_first:
                        v = v - ks[1 - kind] * rows_at(xe_ref, i, lev, kind, g, halves)
                    vs.append(v)
                out.append(vs)
            return out

        return lambda lev: pick(c_ref, UP, lev, number), explicit, True

    def put(lev, i, kind, g, v):
        pe_ref[lev, i, pl.ds((kind * halves + g) * 8, 8), :] = v

    def last(i, kind, g, v):
        edge_ref[i, pl.ds((kind * halves + g) * 8, 8), :] = v

    rows = [row(0, 0, ESF, lambda lev, g: from_south(lev, pl.ds(g * 8, 8), slice(None))), row(1, 3, TNF, come_north)]
    sweep(flags, n_lev, n_pair, rows, put, last)
    if is_first:
        edge_ref[2:4] = inner_ref[...]


def tallies(is_first, in_ref, out_ref, n_lev):
    if is_first:
        out_ref[0] = jnp.zeros(out_ref.shape[1:], F32)
        out_ref[n_lev] = jnp.zeros(out_ref.shape[1:], F32)
    else:
        out_ref[0] = in_ref[0]
        out_ref[n_lev] = in_ref[n_lev]
    zero = jnp.zeros((8, LANES), F32)

    def put(at, i, v):
        out_ref[at, i] = v

    return (lambda at, i: zero) if is_first else (lambda at, i: in_ref[at, i]), put


def edge_back(is_first, n_lev, n_pair, pe_ref, far_ref, c_ref, wx_ref, nf_ref, fs_ref, *rest):
    flags = where_am_i(n_pair)
    halves = n_pair // 8
    acc_ref, (xe_ref, even_ref, odd_ref, out_ref) = (None, rest) if is_first else (rest[0], rest[1:])
    acc_in, acc_out = tallies(is_first, acc_ref, out_ref, n_lev)
    held, south = {}, {}
    up_even = flags[4] == 0

    def put(lev, i, kind, g, v):
        xe_ref[lev, i, pl.ds((kind * halves + g) * 8, 8), :] = v
        if kind == 0:
            held[i, g] = v
        elif i == 0:
            south[g] = jnp.where(fs_ref[lev] < 0.0, held[i, g], v)
        else:
            n3 = spread(nf_ref[lev, 3:4, :])
            north = jnp.where(n3 > 0.0, held[i, g], v)
            even_ref[lev, pl.ds(g * 8, 8), :] = jnp.where(up_even, north, south[g])
            odd_ref[lev, pl.ds(g * 8, 8), :] = jnp.where(up_even, south[g], north)

    back(
        flags, n_lev, n_pair, (0, 3), wx_ref, lambda i, row, at: far_ref[i, at, :], c_ref,
        lambda lev, i, kind, g: rows_at(pe_ref, i, lev, kind, g, halves), put, acc_in, acc_out,
    )


def inner(
    is_first, n_lev, n_pair, pi_ref, far_ref, c_ref, ec_ref, wx_ref, nf_ref, fold_ref, hot_ref, xe_ref, *rest
):
    flags = where_am_i(n_pair)
    halves = n_pair // 8
    acc_ref, (mid_ref, pn_ref, be_ref, mf_ref, out_ref, xi_ref) = (None, rest) if is_first else (rest[0], rest[1:])
    acc_in, acc_out = tallies(is_first, acc_ref, out_ref, n_lev)

    def put(lev, i, kind, g, v):
        xi_ref[lev, i, pl.ds((kind * halves + g) * 8, 8), :] = v

    back(
        flags, n_lev, n_pair, (1, 2), wx_ref, lambda i, row, at: far_ref[2 * is_first + i, at, :], c_ref,
        lambda lev, i, kind, g: rows_at(pi_ref, i, lev, kind, g, halves), put, acc_in, acc_out,
    )
    inner_sweep(n_lev, n_pair, flags, xe_ref, xi_ref, c_ref, ec_ref, hot_ref, pn_ref, be_ref, mid_ref)
    fold_rows(
        flags, fold_ref, nf_ref, lambda lev, kind, g: rows_at(xe_ref, 1, lev, kind, g, halves), mf_ref, n_lev, n_pair
    )


def finish(
    n_lev, n_pair, n_rows, pe_ref, pi_ref, fare_ref, fari_ref, c_ref, wx_ref, depth_ref, acce_ref, acci_ref,
    x_ref, sens_ref, te_ref, ti_ref,
):
    flags = where_am_i(n_pair)
    halves = n_pair // 8
    def far_of(i, row, at):
        return (fare_ref[i // 3] if i in (0, 3) else fari_ref[i - 1])[at.start : at.start + at.size]

    ps = [(pe_ref, 0), (pi_ref, 0), (pi_ref, 1), (pe_ref, 1)]
    e_in, e_out = tallies(False, acce_ref, te_ref, n_lev)
    i_in, i_out = tallies(False, acci_ref, ti_ref, n_lev)

    def put(lev, i, kind, g, v):
        x_ref[lev * n_rows + i, pl.ds((kind * halves + g) * 8, 8), :] = v

    back(
        flags, n_lev, n_pair, range(4), wx_ref, far_of, c_ref,
        lambda lev, i, kind, g: rows_at(ps[i][0], ps[i][1], lev, kind, g, halves), put,
        lambda at, i: e_in(at, i // 3) if i in (0, 3) else i_in(at, i - 1),
        lambda at, i, v: e_out(at, i // 3, v) if i in (0, 3) else i_out(at, i - 1, v),
    )
    first = flags[0] * n_lev
    depth = depth_ref[...]

    def reduce(lev, _):
        k = first + lev
        live = jnp.where((k + 1 < depth) & (k + 1 < 2 * n_lev), 1.0 / STEPS, 0.0)
        e0, e3 = (jnp.sum(te_ref[lev + 1, i], axis=0, keepdims=True) for i in range(2))
        i1, i2 = (jnp.sum(ti_ref[lev + 1, i], axis=0, keepdims=True) for i in range(2))
        sens_ref[lev] = jnp.concatenate([e0, i1, i2, e3], 0) * live
        return 0

    lax.fori_loop(0, n_lev, reduce, 0, unroll=UNROLL)


def hand_out(n_pair, x_ref, f_hbm, a_hbm, sems):
    copies = [
        pltpu.make_async_copy(x_ref.at[:, kind * n_pair + j, :], hbm.at[j], sems.at[kind * n_pair + j])
        for j in range(n_pair)
        for kind, hbm in enumerate((f_hbm, a_hbm))
    ]
    for copy in copies:
        copy.start()
    for copy in copies:
        copy.wait()


def vmem(*shape):
    return pltpu.VMEM(shape, F32)


def where_am_i(n_pair):
    place, count = lax.axis_index("horiz"), lax.axis_size("horiz")
    return (
        lax.axis_index("level"),
        jnp.where(place == count - 1, 1, 0),
        jnp.where(place == 0, 1, 0),
        lax.axis_index("tracer") * n_pair,
        lax.rem(place, 2),
    )


def call(kernel, outs, args, flops, scratch=(), hbm_in=False, hbm_out=0):
    near, far = pl.BlockSpec(memory_space=pltpu.VMEM), pl.BlockSpec(memory_space=pltpu.HBM)
    return pl.pallas_call(
        kernel,
        out_shape=tuple(outs),
        in_specs=[far if hbm_in else near] * len(args),
        out_specs=tuple([far] * hbm_out + [near] * (len(outs) - hbm_out)),
        scratch_shapes=list(scratch),
        compiler_params=pltpu.CompilerParams(vmem_limit_bytes=24 * 2**20),
        cost_estimate=pl.CostEstimate(flops=flops, bytes_accessed=flops // 8, transcendentals=0),
    )(*[pltpu.with_memory_space_constraint(a, pltpu.HBM if hbm_in else pltpu.VMEM) for a in args])


def per_device(forward_init, adjoint_init, east_flow, north_flow, mixing, depth, color, fold):
    n_pair, n_lev, n_rows, n_x = forward_init.shape
    n_all = 2 * n_pair
    count = lax.axis_size("horiz")
    even = [(2 * i + t, 2 * (i ^ 1) + t) for i in range(count) for t in range(2)]
    odd = []
    for i in range(count):
        partner = ((i - 1) ^ 1) + 1 if i > 0 else count
        odd += [(2 * i + t, 2 * partner + t if partner < count else 2 * i + 1 - t) for t in range(2)]
    pairs = ("horiz", "tracer")
    swap = [(0, 1), (1, 0)]
    f2 = forward_init.reshape(n_pair * n_lev * n_rows, n_x)
    a2 = adjoint_init.reshape(n_pair * n_lev * n_rows, n_x)
    fold2 = fold.reshape(1, n_x)
    work = n_lev * n_rows * n_all * n_x

    flat = vmem(n_pair * n_lev * n_rows, n_x)
    flow = lax.ppermute(north_flow, "horiz", [(i, (i + 1) % count) for i in range(count)])
    f2, a2, north_flow, depth, edge_rows = call(
        functools.partial(load, n_lev, n_pair, n_rows),
        [
            flat,
            flat,
            vmem(n_lev, n_rows, n_x),
            pltpu.VMEM((n_rows, n_x), jnp.int32),
            vmem(3, n_lev, n_pair, n_x),
        ],
        [f2, a2, north_flow, depth],
        work,
        [pltpu.SemaphoreType.DMA((10,))],
        hbm_in=True,
    )
    message = vmem(n_lev + 1, n_pair, n_x)
    to_even, to_odd = call(
        functools.partial(send_first, n_lev, n_pair, n_rows), [message, message], [edge_rows, depth, flow], work
    )
    from_odd = lax.ppermute(to_odd, pairs, odd)
    from_even = lax.ppermute(to_even, pairs, even)
    state = vmem(n_lev, 2, n_all, n_x)
    halo = vmem(n_lev, n_pair, n_x)
    acc = vmem(n_lev + 1, 2, 8, n_x)
    edges = vmem(2, n_all, n_x)
    mid, xe, pi, be, c, wx, hot, mf = call(
        functools.partial(prepare, n_lev, n_pair, n_rows),
        [edges] + [state] * 3 + [vmem(13, n_lev, n_rows, n_x), vmem(3, n_rows, n_x), vmem(n_rows, n_pair, n_x), halo],
        [f2, a2, east_flow, north_flow, mixing, depth, color, fold2],
        work * 10,
        [vmem(n_lev, n_rows, n_x), state],
    )
    acce = acci = None
    for step in range(STEPS):
        if step == 0:
            pe, edge, ec, fs = call(
                functools.partial(edge_sweep, True, n_lev, n_pair),
                [state, vmem(n_rows, n_all, n_x), vmem(8, n_lev, 8, n_x), vmem(n_lev, 8, n_x)],
                [mid, be, c, mf, from_even, from_odd, xe, north_flow, depth, fold2, flow],
                work * 3,
            )
        else:
            pe, edge = call(
                functools.partial(edge_sweep, False, n_lev, n_pair),
                [state, edges],
                [fari, be, c, mf, from_even, from_odd, ec],
                work * 2,
            )
        fare = lax.ppermute(edge, "level", swap)
        if step == 0:
            fari = fare
        if step == STEPS - 1:
            break
        more = [] if step == 0 else [acce]
        xe, to_even, to_odd, acce = call(
            functools.partial(edge_back, step == 0, n_lev, n_pair),
            [state, halo, halo, acc],
            [pe, fare, c, wx, north_flow, fs] + more,
            work * 2,
        )
        from_odd = lax.ppermute(to_odd, pairs, odd)
        from_even = lax.ppermute(to_even, pairs, even)
        more = [] if step == 0 else [acci]
        mid, pi, be, mf, acci = call(
            functools.partial(inner, step == 0, n_lev, n_pair),
            [edges, state, state, halo, acc],
            [pi, fari, c, ec, wx, north_flow, fold2, hot, xe] + more,
            work * 9,
            [state],
        )
        fari = lax.ppermute(mid, "level", swap)
    x, sens = call(
        functools.partial(finish, n_lev, n_pair, n_rows),
        [vmem(n_lev * n_rows, n_all, n_x), vmem(n_lev, n_rows, n_x)],
        [pe, pi, fare, fari, c, wx, depth, acce, acci],
        work * 4,
        [acc, acc],
    )
    out = jax.ShapeDtypeStruct((n_pair, n_lev * n_rows, n_x), F32)
    f_out, a_out = call(
        functools.partial(hand_out, n_pair),
        [out, out],
        [x],
        work * 4,
        [pltpu.SemaphoreType.DMA((n_all,))],
        hbm_out=2,
    )
    sens = sens + lax.ppermute(sens, "tracer", swap)
    return f_out.reshape(forward_init.shape), a_out.reshape(adjoint_init.shape), sens


def solution(mesh):
    tracers, flows = P("tracer", "level", "horiz", None), P("level", "horiz", None)
    return jax.shard_map(
        per_device,
        mesh=mesh,
        in_specs=(tracers, tracers, flows, flows, P(None, "horiz", None), P("horiz", None), P("horiz", None), P()),
        out_specs=(tracers, tracers, flows),
        check_vma=False,
    )
```
